256 devices in a mesh: trial: 8 (over y_hi, x), dp: 8 (over z), tensor: 4 (over y_lo, core).
Axes of the slice: x: 4, y: 4 (y_hi: 2, y_lo: 2; y = y_hi * 2 + y_lo), z: 8, core: 2. Of those that a mesh axis runs over, the one named last changes fastest.
Arguments:
- residual_rows: bfloat16 [32768, 8192], P(('trial', 'dp', 'tensor'))
- input_norm_weight: float32 [8192], replicated, may hold values from 0.25 to 1.75
- trial_row_index: int32 [8, 4096], P(None, 'dp'), may hold values from 0 to 127, as said below
- keyvalue_weight: bfloat16 [8192, 2048], P('tensor'), may hold values from -0.0625 to 0.0625
- adapter_down_weight: bfloat16 [8, 8192, 128], P('trial', 'tensor'), may hold values from -0.0625 to 0.0625
- adapter_up_weight: bfloat16 [8, 64, 2048], P('trial'), may hold values from -0.75 to 0.75
- keyvalue_gradient: bfloat16 [8, 4096, 2048], P('trial', ('dp', 'tensor')), may hold values from -6 to 6
Outputs:
- keyvalue_output: float32 [8, 4096, 2048], P('trial', ('dp', 'tensor'))
- grad_a: float32 [8, 128, 8192], P('trial', 'dp', 'tensor')
- grad_b: float32 [8, 64, 2048], P('trial', None, ('dp', 'tensor'))
The draws below stay inside these ranges and needn't reach their ends.
Inputs may be any that keep to these rules, and one draw needn't show every extreme that they name: `trial_row_index`: within each trial, each index of dp and each block of 16 consecutive tokens taken from one source device, the rows named are distinct.
All inputs are finite; a program needn't handle non-finite values.
Results may differ from the reference program's by a relative error of at most 0.0041.
Values may be sent and summed in bfloat16 or wider, within the bound.
A program may use at most 64 MiB of HBM per device.

```python
import math
import jax
import jax.numpy as jnp
from jax import lax

MODEL_WIDTH = 8192
KEYVALUE_WIDTH = 1024
ADAPTER_RANK = 64
SEL = 16
TRIAL_COUNT = 8
POOL_DEV = 128
POOL = 32768
TOK_DEV = 512
TOKENS = 4096
N_TRIAL = 8
N_DP = 8
N_TENSOR = 4


def draw_residual_rows(key, part):
    key_vals, key_rows, key_cols = jax.random.split(key, 3)
    row_scale = jnp.exp(jax.random.uniform(key_rows, (POOL, 1), jnp.float32, 0.0, math.log(10.0)))
    col_scale = jnp.exp(jax.random.uniform(key_cols, (1, MODEL_WIDTH), jnp.float32, 0.0, math.log(10.0)))
    values = jax.random.normal(key_vals, (POOL, MODEL_WIDTH), jnp.float32)
    return (values * row_scale * col_scale).astype(jnp.bfloat16)


def draw_trial_row_index(key, part):
    groups = N_DP * N_TRIAL * N_TENSOR
    scores = jax.random.randint(key, (TRIAL_COUNT, groups, POOL_DEV), 0, 1048576, jnp.int32)
    scores = scores * POOL_DEV + jnp.arange(POOL_DEV, dtype=jnp.int32)[None, None, :]
    order = jnp.argsort(scores, axis=2).astype(jnp.int32)
    return order[:, :, :SEL].reshape(TRIAL_COUNT, TOKENS)


def raised(result, key, source, target, shards_of, factor):
    owner, partner = [(jnp.arange(result.shape[axis_at]) // (result.shape[axis_at] // shards_of)).reshape([-1 if axis == axis_at else 1 for axis in range(result.ndim)]) for axis_at in (source, target)]
    chosen = jax.random.permutation(key, shards_of)[partner]
    strong = (owner == chosen) | (owner == (partner + shards_of // 2) % shards_of)
    return jnp.where(strong, factor * result, result)


def levels(own_key, extent, cuts, least, top_value):
    loudness, own = 1.0, jax.random.fold_in(own_key, 6)
    for position, blocks in cuts:
        heights = jnp.exp(jax.random.uniform(jax.random.fold_in(own, position), (blocks,), jnp.float32, least / len(cuts), top_value / len(cuts)))
        loudness = loudness * jnp.repeat(heights, extent[position] // blocks).reshape([-1 if axis == position else 1 for axis in range(len(extent))])
    return loudness


def centred(key, dims, width, most, pieces=(), kind=jnp.bfloat16):
    entries = jax.random.normal(key, dims, jnp.float32) * width
    if len(pieces) > 0:
        entries = levels(key, dims, pieces, -0.22, 0.18) * entries
    return jnp.clip(entries, min=-most, max=most).astype(kind)


def heavy_noise(own_key, extent, deviation, bound, shards, heavy, kind=jnp.bfloat16):
    result = deviation * jax.random.normal(own_key, extent, jnp.float32)
    if shards:
        result = result * levels(own_key, extent, shards, -0.22, 0.18)
    return jnp.clip(raised(result, jax.random.fold_in(own_key, 3), *heavy), -bound, bound).astype(kind)


def setup_inputs(seed: int = 0) -> dict:
    splits = jax.random.split(jax.random.key(seed), 8)
    residual_rows = draw_residual_rows(jax.random.fold_in(splits[7], 71), 0)
    input_norm_weight = jnp.clip(1.0 + 0.15 * jax.random.normal(splits[1], (MODEL_WIDTH,), jnp.float32), 0.25, 1.75)
    trial_row_index = draw_trial_row_index(jax.random.fold_in(splits[7], 71), 0)
    keyvalue_weight = centred(splits[3], (MODEL_WIDTH, 2 * KEYVALUE_WIDTH), MODEL_WIDTH ** -0.5, 0.0625, ((0, 4),))
    adapter_down_weight = centred(splits[4], (TRIAL_COUNT, MODEL_WIDTH, 2 * ADAPTER_RANK), MODEL_WIDTH ** -0.5, 0.0625, ((0, 8), (1, 4)))
    adapter_up_weight = centred(splits[5], (TRIAL_COUNT, ADAPTER_RANK, 2 * KEYVALUE_WIDTH), ADAPTER_RANK ** -0.5, 0.75, ((0, 8),))
    keyvalue_gradient = heavy_noise(splits[6], (TRIAL_COUNT, TOKENS, 2 * KEYVALUE_WIDTH), 1.0, 6.0, ((0, 8), (1, 32)), (1, 2, 32, 2.75))
    return dict(residual_rows=residual_rows, input_norm_weight=input_norm_weight, trial_row_index=trial_row_index, keyvalue_weight=keyvalue_weight, adapter_down_weight=adapter_down_weight, adapter_up_weight=adapter_up_weight, keyvalue_gradient=keyvalue_gradient)


adapter_scale = 2.0
norm_eps = 1e-05

def reference(residual_rows, input_norm_weight, trial_row_index, keyvalue_weight, adapter_down_weight, adapter_up_weight, keyvalue_gradient):
    normed_input = MODEL_WIDTH // N_TENSOR
    tok = jnp.arange(TOKENS, dtype=jnp.int32)
    dp_index = tok // TOK_DEV
    source = tok % TOK_DEV // SEL
    source_trial = source // N_TENSOR
    source_tensor = source % N_TENSOR
    keyvalue_list = []
    grad_a_list = []
    up_gradient_list = []
    for trial_index in range(TRIAL_COUNT):
        index = ((source_trial * N_DP + dp_index) * N_TENSOR + source_tensor) * POOL_DEV + trial_row_index[trial_index]
        raw = residual_rows[index.astype(jnp.int32)].astype(jnp.float32)
        msq = lax.optimization_barrier(jnp.mean(raw * raw, axis=1, keepdims=True))
        x = (raw * lax.rsqrt(msq + norm_eps) * input_norm_weight[None, :]).astype(jnp.bfloat16)
        frozen_output = jnp.zeros((TOKENS, 2 * KEYVALUE_WIDTH), jnp.float32)
        down_product = jnp.zeros((TOKENS, 2 * ADAPTER_RANK), jnp.float32)
        for trial_position in range(N_TENSOR):
            row_portion = x[:, trial_position * normed_input:(trial_position + 1) * normed_input]
            part = jnp.dot(row_portion, keyvalue_weight[trial_position * normed_input:(trial_position + 1) * normed_input], preferred_element_type=jnp.float32)
            rank_portion = jnp.dot(row_portion, adapter_down_weight[trial_index][trial_position * normed_input:(trial_position + 1) * normed_input], preferred_element_type=jnp.float32)
            frozen_output = frozen_output + part
            down_product = down_product + rank_portion
        up_weight_full = adapter_up_weight[trial_index].astype(jnp.float32)
        precision_option = lax.Precision.HIGHEST
        adapter_key = jnp.dot(down_product[:, :ADAPTER_RANK], up_weight_full[:, :KEYVALUE_WIDTH], precision=precision_option)
        adapter_value = jnp.dot(down_product[:, ADAPTER_RANK:], up_weight_full[:, KEYVALUE_WIDTH:], precision=precision_option)
        keyvalue_list.append(frozen_output + adapter_scale * jnp.concatenate([adapter_key, adapter_value], axis=1))
        grad_in = keyvalue_gradient[trial_index].astype(jnp.float32)
        key_gradient_part = jnp.dot(grad_in[:, :KEYVALUE_WIDTH], up_weight_full[:, :KEYVALUE_WIDTH].T, precision=precision_option)
        value_gradient_part = jnp.dot(grad_in[:, KEYVALUE_WIDTH:], up_weight_full[:, KEYVALUE_WIDTH:].T, precision=precision_option)
        down_product_gradient = (adapter_scale * jnp.concatenate([key_gradient_part, value_gradient_part], axis=1)).astype(jnp.bfloat16)
        grad_a_list.append(lax.dot_general(down_product_gradient, x, (((0,), (0,)), ((), ())), preferred_element_type=jnp.float32))
        key_up_gradient = jnp.dot(down_product[:, :ADAPTER_RANK].T, grad_in[:, :KEYVALUE_WIDTH], precision=precision_option)
        value_up_gradient = jnp.dot(down_product[:, ADAPTER_RANK:].T, grad_in[:, KEYVALUE_WIDTH:], precision=precision_option)
        up_gradient_list.append(adapter_scale * jnp.concatenate([key_up_gradient, value_up_gradient], axis=1))
    return (jnp.stack(keyvalue_list), jnp.stack(grad_a_list), jnp.stack(up_gradient_list))
```

```python
import jax
import jax.numpy as jnp
from jax import lax
from jax.sharding import PartitionSpec as P

adapter_scale = 2.0
norm_eps = 1e-05


def shards(
    residual_rows,
    input_norm_weight,
    trial_row_index,
    keyvalue_weight,
    adapter_down_weight,
    adapter_up_weight,
    keyvalue_gradient,
):
    trials = lax.axis_size("trial")
    tensors = lax.axis_size("tensor")
    dps = lax.axis_size("dp")
    tok_dev = trial_row_index.shape[1]
    select = tok_dev // (trials * tensors)
    normed_input = keyvalue_weight.shape[0]
    kv_width = keyvalue_weight.shape[1]
    keyvalue_half = kv_width // 2
    rank_index = adapter_up_weight.shape[1]
    pool_dev = residual_rows.shape[0]
    highest_precision = lax.Precision.HIGHEST

    source = lax.axis_index("trial") * tensors + lax.axis_index("tensor")
    picks = lax.dynamic_slice_in_dim(trial_row_index, source * select, select, 1).reshape(-1)
    onehot = (picks[:, None] == jnp.arange(pool_dev, dtype=jnp.int32)[None, :]).astype(jnp.bfloat16)
    wide = jnp.dot(onehot, residual_rows, preferred_element_type=jnp.float32)
    msq = jnp.mean(wide * wide, axis=1, keepdims=True)
    chosen = (wide * lax.rsqrt(msq + norm_eps) * input_norm_weight[None, :]).astype(jnp.bfloat16)
    chosen = chosen.reshape(trials, select, tensors, normed_input).transpose(0, 2, 1, 3)
    arrived = lax.all_to_all(
        chosen.reshape(trials * tensors, select, normed_input),
        ("trial", "tensor"),
        split_axis=0,
        concat_axis=0,
        tiled=True,
    )
    rows = arrived.reshape(tok_dev, normed_input)

    up_weight = adapter_up_weight[0].astype(jnp.float32)
    grad_in = keyvalue_gradient[0].astype(jnp.float32)
    key_gradient_full = jnp.dot(
        grad_in[:, :keyvalue_half], up_weight[:, :keyvalue_half].T, precision=highest_precision
    )
    value_gradient_full = jnp.dot(
        grad_in[:, keyvalue_half:], up_weight[:, keyvalue_half:].T, precision=highest_precision
    )
    rank_gradient = (
        adapter_scale * jnp.concatenate([key_gradient_full, value_gradient_full], axis=1)
    ).astype(jnp.bfloat16)
    every_rank = lax.all_gather(rank_gradient, "tensor", axis=0, tiled=True)
    grad_a_term = lax.dot_general(
        every_rank, rows, (((0,), (0,)), ((), ())), preferred_element_type=jnp.float32
    )

    down_weight = adapter_down_weight[0]
    keyval = jnp.dot(rows, keyvalue_weight, preferred_element_type=jnp.float32)
    ranks = jnp.dot(rows, down_weight, preferred_element_type=jnp.float32)
    summed = lax.psum_scatter(
        jnp.concatenate([keyval, ranks], axis=1), "tensor", scatter_dimension=0, tiled=True
    )
    frozen_output_local = summed[:, :kv_width]
    local_rank_rows = summed[:, kv_width:]
    adapter_key = jnp.dot(
        local_rank_rows[:, :rank_index], up_weight[:, :keyvalue_half], precision=highest_precision
    )
    adapter_value = jnp.dot(
        local_rank_rows[:, rank_index:], up_weight[:, keyvalue_half:], precision=highest_precision
    )
    keyvalue_output = frozen_output_local + adapter_scale * jnp.concatenate(
        [adapter_key, adapter_value], axis=1
    )

    grad_a = lax.psum_scatter(grad_a_term, "dp", scatter_dimension=0, tiled=True)

    key_down_gradient = jnp.dot(
        local_rank_rows[:, :rank_index].T, grad_in[:, :keyvalue_half], precision=highest_precision
    )
    value_down_gradient = jnp.dot(
        local_rank_rows[:, rank_index:].T, grad_in[:, keyvalue_half:], precision=highest_precision
    )
    up_gradient_term = adapter_scale * jnp.concatenate(
        [key_down_gradient, value_down_gradient], axis=1
    )
    width = up_gradient_term.shape[1] // (dps * tensors)
    up_gradient_term = (
        up_gradient_term.reshape(rank_index, dps, tensors, width)
        .transpose(0, 2, 1, 3)
        .reshape(rank_index, dps * tensors * width)
    )
    grad_b = lax.psum_scatter(up_gradient_term, "tensor", scatter_dimension=1, tiled=True)
    grad_b = lax.psum_scatter(grad_b, "dp", scatter_dimension=1, tiled=True)
    return (keyvalue_output[None], grad_a[None], grad_b[None])


def solution(mesh):
    return jax.shard_map(
        shards,
        mesh=mesh,
        in_specs=(
            P(("trial", "dp", "tensor"), None),
            P(),
            P(None, "dp"),
            P("tensor", None),
            P("trial", "tensor", None),
            P("trial", None, None),
            P("trial", ("dp", "tensor"), None),
        ),
        out_specs=(
            P("trial", ("dp", "tensor"), None),
            P("trial", "dp", "tensor"),
            P("trial", None, ("dp", "tensor")),
        ),
        check_vma=False,
    )
```

```python
import functools

import jax
import jax.numpy as jnp
from jax import lax
from jax.experimental import pallas as pl
from jax.experimental.pallas import tpu as pltpu
from jax.sharding import PartitionSpec as P

MESH = pl.DeviceIdType.MESH

adapter_scale = 2.0
norm_eps = 1e-05


def _exchange_sum_kernel(n, group_index, device_of, x_ref, o_ref, recv, send_sems, recv_sems):
    me = group_index()
    barrier = pltpu.get_barrier_semaphore()
    for shift in range(1, n):
        pl.semaphore_signal(
            barrier, inc=1, device_id=device_of(lax.rem(me + shift, n)), device_id_type=MESH
        )
    pl.semaphore_wait(barrier, n - 1)
    copies = []
    for shift in range(1, n):
        target = lax.rem(me + shift, n)
        copy = pltpu.make_async_remote_copy(
            src_ref=x_ref.at[target],
            dst_ref=recv.at[shift],
            send_sem=send_sems.at[shift],
            recv_sem=recv_sems.at[shift],
            device_id=device_of(target),
            device_id_type=MESH,
        )
        copy.start()
        copies.append(copy)
    o_ref[...] = x_ref[me]
    for shift, copy in zip(range(1, n), copies):
        copy.wait_recv()
        o_ref[...] += recv[shift]
    for copy in copies:
        copy.wait_send()


def exchange_sum(x, n, group_index, device_of, collective_id):
    chunk = x.shape[1:]
    return pl.pallas_call(
        functools.partial(_exchange_sum_kernel, n, group_index, device_of),
        out_shape=jax.ShapeDtypeStruct(chunk, x.dtype),
        in_specs=[pl.BlockSpec(memory_space=pltpu.VMEM)],
        out_specs=pl.BlockSpec(memory_space=pltpu.VMEM),
        scratch_shapes=[
            pltpu.VMEM((n,) + chunk, x.dtype),
            pltpu.SemaphoreType.DMA((n,)),
            pltpu.SemaphoreType.DMA((n,)),
        ],
        compiler_params=pltpu.CompilerParams(collective_id=collective_id, has_side_effects=True),
    )(x)


def shards(
    residual_rows,
    input_norm_weight,
    trial_row_index,
    keyvalue_weight,
    adapter_down_weight,
    adapter_up_weight,
    keyvalue_gradient,
):
    trials = lax.axis_size("trial")
    tensors = lax.axis_size("tensor")
    dps = lax.axis_size("dp")
    tok_dev = trial_row_index.shape[1]
    select = tok_dev // (trials * tensors)
    normed_input = keyvalue_weight.shape[0]
    kv_width = keyvalue_weight.shape[1]
    keyvalue_half = kv_width // 2
    rank_index = adapter_up_weight.shape[1]
    pool_dev = residual_rows.shape[0]
    highest_precision = lax.Precision.HIGHEST

    source = lax.axis_index("trial") * tensors + lax.axis_index("tensor")
    picks = lax.dynamic_slice_in_dim(trial_row_index, source * select, select, 1).reshape(-1)
    onehot = (picks[:, None] == jnp.arange(pool_dev, dtype=jnp.int32)[None, :]).astype(jnp.bfloat16)
    wide = jnp.dot(onehot, residual_rows, preferred_element_type=jnp.float32)
    msq = jnp.mean(wide * wide, axis=1, keepdims=True)
    chosen = (wide * lax.rsqrt(msq + norm_eps) * input_norm_weight[None, :]).astype(jnp.bfloat16)
    chosen = chosen.reshape(trials, select, tensors, normed_input).transpose(0, 2, 1, 3)
    arrived = lax.all_to_all(
        chosen.reshape(trials * tensors, select, normed_input),
        ("trial", "tensor"),
        split_axis=0,
        concat_axis=0,
        tiled=True,
    )
    rows = arrived.reshape(tok_dev, normed_input)

    up_weight = adapter_up_weight[0].astype(jnp.float32)
    grad_in = keyvalue_gradient[0].astype(jnp.float32)
    key_gradient_full = jnp.dot(
        grad_in[:, :keyvalue_half], up_weight[:, :keyvalue_half].T, precision=highest_precision
    )
    value_gradient_full = jnp.dot(
        grad_in[:, keyvalue_half:], up_weight[:, keyvalue_half:].T, precision=highest_precision
    )
    rank_gradient = (
        adapter_scale * jnp.concatenate([key_gradient_full, value_gradient_full], axis=1)
    ).astype(jnp.bfloat16)
    every_rank = lax.all_gather(rank_gradient, "tensor", axis=0, tiled=True)
    grad_a_term = lax.dot_general(
        every_rank, rows, (((0,), (0,)), ((), ())), preferred_element_type=jnp.float32
    )

    down_weight = adapter_down_weight[0]
    keyval = jnp.dot(rows, keyvalue_weight, preferred_element_type=jnp.float32)
    ranks = jnp.dot(rows, down_weight, preferred_element_type=jnp.float32)
    summed = lax.psum_scatter(
        jnp.concatenate([keyval, ranks], axis=1), "tensor", scatter_dimension=0, tiled=True
    )
    frozen_output_local = summed[:, :kv_width]
    local_rank_rows = summed[:, kv_width:]
    adapter_key = jnp.dot(
        local_rank_rows[:, :rank_index], up_weight[:, :keyvalue_half], precision=highest_precision
    )
    adapter_value = jnp.dot(
        local_rank_rows[:, rank_index:], up_weight[:, keyvalue_half:], precision=highest_precision
    )
    keyvalue_output = frozen_output_local + adapter_scale * jnp.concatenate(
        [adapter_key, adapter_value], axis=1
    )

    grad_a = exchange_sum(
        grad_a_term.reshape(dps, grad_a_term.shape[0] // dps, grad_a_term.shape[1]),
        dps,
        lambda: lax.axis_index("dp"),
        lambda j: (lax.axis_index("trial"), j, lax.axis_index("tensor")),
        0,
    )

    key_down_gradient = jnp.dot(
        local_rank_rows[:, :rank_index].T, grad_in[:, :keyvalue_half], precision=highest_precision
    )
    value_down_gradient = jnp.dot(
        local_rank_rows[:, rank_index:].T, grad_in[:, keyvalue_half:], precision=highest_precision
    )
    up_gradient_term = adapter_scale * jnp.concatenate(
        [key_down_gradient, value_down_gradient], axis=1
    )
    members = dps * tensors
    width = up_gradient_term.shape[1] // members
    grad_b = exchange_sum(
        up_gradient_term.reshape(rank_index, members, width).transpose(1, 0, 2),
        members,
        lambda: lax.axis_index("dp") * tensors + lax.axis_index("tensor"),
        lambda g: (lax.axis_index("trial"), g // tensors, lax.rem(g, tensors)),
        1,
    )
    return (keyvalue_output[None], grad_a[None], grad_b[None])


def solution(mesh):
    return jax.shard_map(
        shards,
        mesh=mesh,
        in_specs=(
            P(("trial", "dp", "tensor"), None),
            P(),
            P(None, "dp"),
            P("tensor", None),
            P("trial", "tensor", None),
            P("trial", None, None),
            P("trial", ("dp", "tensor"), None),
        ),
        out_specs=(
            P("trial", ("dp", "tensor"), None),
            P("trial", "dp", "tensor"),
            P("trial", None, ("dp", "tensor")),
        ),
        check_vma=False,
    )
```

```python
import functools

import jax
import jax.numpy as jnp
from jax import lax
from jax.experimental import pallas as pl
from jax.experimental.pallas import tpu as pltpu
from jax.sharding import PartitionSpec as P

MESH = pl.DeviceIdType.MESH

adapter_scale = 2.0
norm_eps = 1e-05


def _exchange_sum_kernel(n, group_index, device_of, x_ref, o_ref, recv, send_sems, recv_sems):
    me = group_index()
    barrier = pltpu.get_barrier_semaphore()
    for shift in range(1, n):
        pl.semaphore_signal(
            barrier, inc=1, device_id=device_of(lax.rem(me + shift, n)), device_id_type=MESH
        )
    pl.semaphore_wait(barrier, n - 1)
    copies = []
    for shift in range(1, n):
        target = lax.rem(me + shift, n)
        copy = pltpu.make_async_remote_copy(
            src_ref=x_ref.at[target],
            dst_ref=recv.at[shift],
            send_sem=send_sems.at[shift],
            recv_sem=recv_sems.at[shift],
            device_id=device_of(target),
            device_id_type=MESH,
        )
        copy.start()
        copies.append(copy)
    o_ref[...] = x_ref[me]
    for shift, copy in zip(range(1, n), copies):
        copy.wait_recv()
        o_ref[...] += recv[shift]
    for copy in copies:
        copy.wait_send()


def exchange_sum(x, n, group_index, device_of, collective_id):
    chunk = x.shape[1:]
    return pl.pallas_call(
        functools.partial(_exchange_sum_kernel, n, group_index, device_of),
        out_shape=jax.ShapeDtypeStruct(chunk, x.dtype),
        in_specs=[pl.BlockSpec(memory_space=pltpu.VMEM)],
        out_specs=pl.BlockSpec(memory_space=pltpu.VMEM),
        scratch_shapes=[
            pltpu.VMEM((n,) + chunk, x.dtype),
            pltpu.SemaphoreType.DMA((n,)),
            pltpu.SemaphoreType.DMA((n,)),
        ],
        compiler_params=pltpu.CompilerParams(collective_id=collective_id, has_side_effects=True),
    )(x)


def _two_stage_sum_kernel(n1, n2, x_ref, o_ref, stage, recv1, recv2, sems):
    me1 = lax.axis_index("tensor")
    me2 = lax.axis_index("dp")
    trial = lax.axis_index("trial")
    first = lambda j: (trial, me2, j)
    second = lambda j: (trial, j, me1)
    barrier = pltpu.get_barrier_semaphore()
    for shift in range(1, n1):
        pl.semaphore_signal(barrier, inc=1, device_id=first(lax.rem(me1 + shift, n1)), device_id_type=MESH)
    for shift in range(1, n2):
        pl.semaphore_signal(barrier, inc=1, device_id=second(lax.rem(me2 + shift, n2)), device_id_type=MESH)
    pl.semaphore_wait(barrier, n1 + n2 - 2)
    copies = []
    for shift in range(1, n1):
        target = lax.rem(me1 + shift, n1)
        copy = pltpu.make_async_remote_copy(
            src_ref=x_ref.at[target],
            dst_ref=recv1.at[shift],
            send_sem=sems.at[0, shift],
            recv_sem=sems.at[1, shift],
            device_id=first(target),
            device_id_type=MESH,
        )
        copy.start()
        copies.append(copy)
    stage[...] = x_ref[me1]
    for shift, copy in zip(range(1, n1), copies):
        copy.wait_recv()
        stage[...] += recv1[shift]
    copies2 = []
    for shift in range(1, n2):
        target = lax.rem(me2 + shift, n2)
        copy = pltpu.make_async_remote_copy(
            src_ref=stage.at[target],
            dst_ref=recv2.at[shift],
            send_sem=sems.at[2, shift],
            recv_sem=sems.at[3, shift],
            device_id=second(target),
            device_id_type=MESH,
        )
        copy.start()
        copies2.append(copy)
    o_ref[...] = stage[me2]
    for shift, copy in zip(range(1, n2), copies2):
        copy.wait_recv()
        o_ref[...] += recv2[shift]
    for copy in copies + copies2:
        copy.wait_send()


def two_stage_sum(x, collective_id):
    n1, n2 = x.shape[0], x.shape[1]
    chunk = x.shape[2:]
    return pl.pallas_call(
        functools.partial(_two_stage_sum_kernel, n1, n2),
        out_shape=jax.ShapeDtypeStruct(chunk, x.dtype),
        in_specs=[pl.BlockSpec(memory_space=pltpu.VMEM)],
        out_specs=pl.BlockSpec(memory_space=pltpu.VMEM),
        scratch_shapes=[
            pltpu.VMEM((n2,) + chunk, x.dtype),
            pltpu.VMEM((n1, n2) + chunk, x.dtype),
            pltpu.VMEM((n2,) + chunk, x.dtype),
            pltpu.SemaphoreType.DMA((4, max(n1, n2))),
        ],
        compiler_params=pltpu.CompilerParams(collective_id=collective_id, has_side_effects=True),
    )(x)


def shards(
    residual_rows,
    input_norm_weight,
    trial_row_index,
    keyvalue_weight,
    adapter_down_weight,
    adapter_up_weight,
    keyvalue_gradient,
):
    trials = lax.axis_size("trial")
    tensors = lax.axis_size("tensor")
    dps = lax.axis_size("dp")
    tok_dev = trial_row_index.shape[1]
    select = tok_dev // (trials * tensors)
    normed_input = keyvalue_weight.shape[0]
    kv_width = keyvalue_weight.shape[1]
    keyvalue_half = kv_width // 2
    rank_index = adapter_up_weight.shape[1]
    pool_dev = residual_rows.shape[0]
    highest_precision = lax.Precision.HIGHEST

    source = lax.axis_index("trial") * tensors + lax.axis_index("tensor")
    picks = lax.dynamic_slice_in_dim(trial_row_index, source * select, select, 1).reshape(-1)
    onehot = (picks[:, None] == jnp.arange(pool_dev, dtype=jnp.int32)[None, :]).astype(jnp.bfloat16)
    wide = jnp.dot(onehot, residual_rows, preferred_element_type=jnp.float32)
    msq = jnp.mean(wide * wide, axis=1, keepdims=True)
    chosen = (wide * lax.rsqrt(msq + norm_eps) * input_norm_weight[None, :]).astype(jnp.bfloat16)
    chosen = chosen.reshape(trials, select, tensors, normed_input).transpose(0, 2, 1, 3)
    arrived = lax.all_to_all(
        chosen.reshape(trials * tensors, select, normed_input),
        ("trial", "tensor"),
        split_axis=0,
        concat_axis=0,
        tiled=True,
    )
    rows = arrived.reshape(tok_dev, normed_input)

    up_weight = adapter_up_weight[0].astype(jnp.float32)
    grad_in = keyvalue_gradient[0].astype(jnp.float32)
    key_gradient_full = jnp.dot(
        grad_in[:, :keyvalue_half], up_weight[:, :keyvalue_half].T, precision=highest_precision
    )
    value_gradient_full = jnp.dot(
        grad_in[:, keyvalue_half:], up_weight[:, keyvalue_half:].T, precision=highest_precision
    )
    rank_gradient = (
        adapter_scale * jnp.concatenate([key_gradient_full, value_gradient_full], axis=1)
    ).astype(jnp.bfloat16)
    every_rank = lax.all_gather(rank_gradient, "tensor", axis=0, tiled=True)
    grad_a_term = lax.dot_general(
        every_rank, rows, (((0,), (0,)), ((), ())), preferred_element_type=jnp.float32
    )

    down_weight = adapter_down_weight[0]
    keyval = jnp.dot(rows, keyvalue_weight, preferred_element_type=jnp.float32)
    ranks = jnp.dot(rows, down_weight, preferred_element_type=jnp.float32)
    summed = lax.psum_scatter(
        jnp.concatenate([keyval, ranks], axis=1), "tensor", scatter_dimension=0, tiled=True
    )
    frozen_output_local = summed[:, :kv_width]
    local_rank_rows = summed[:, kv_width:]
    adapter_key = jnp.dot(
        local_rank_rows[:, :rank_index], up_weight[:, :keyvalue_half], precision=highest_precision
    )
    adapter_value = jnp.dot(
        local_rank_rows[:, rank_index:], up_weight[:, keyvalue_half:], precision=highest_precision
    )
    keyvalue_output = frozen_output_local + adapter_scale * jnp.concatenate(
        [adapter_key, adapter_value], axis=1
    )

    grad_a = exchange_sum(
        grad_a_term.reshape(dps, grad_a_term.shape[0] // dps, grad_a_term.shape[1]),
        dps,
        lambda: lax.axis_index("dp"),
        lambda j: (lax.axis_index("trial"), j, lax.axis_index("tensor")),
        0,
    )

    key_down_gradient = jnp.dot(
        local_rank_rows[:, :rank_index].T, grad_in[:, :keyvalue_half], precision=highest_precision
    )
    value_down_gradient = jnp.dot(
        local_rank_rows[:, rank_index:].T, grad_in[:, keyvalue_half:], precision=highest_precision
    )
    up_gradient_term = adapter_scale * jnp.concatenate(
        [key_down_gradient, value_down_gradient], axis=1
    )
    width = up_gradient_term.shape[1] // (dps * tensors)
    grad_b = two_stage_sum(
        up_gradient_term.reshape(rank_index, dps, tensors, width).transpose(2, 1, 0, 3), 1
    )
    return (keyvalue_output[None], grad_a[None], grad_b[None])


def solution(mesh):
    return jax.shard_map(
        shards,
        mesh=mesh,
        in_specs=(
            P(("trial", "dp", "tensor"), None),
            P(),
            P(None, "dp"),
            P("tensor", None),
            P("trial", "tensor", None),
            P("trial", None, None),
            P("trial", ("dp", "tensor"), None),
        ),
        out_specs=(
            P("trial", ("dp", "tensor"), None),
            P("trial", "dp", "tensor"),
            P("trial", None, ("dp", "tensor")),
        ),
        check_vma=False,
    )
```

```python
import functools

import jax
import jax.numpy as jnp
from jax import lax
from jax.experimental import pallas as pl
from jax.experimental.pallas import tpu as pltpu
from jax.sharding import PartitionSpec as P

MESH = pl.DeviceIdType.MESH

adapter_scale = 2.0
norm_eps = 1e-05


def _exchange_sum_kernel(n, group_index, device_of, x_ref, o_ref, recv, send_sems, recv_sems):
    me = group_index()
    barrier = pltpu.get_barrier_semaphore()
    for shift in range(1, n):
        pl.semaphore_signal(
            barrier, inc=1, device_id=device_of(lax.rem(me + shift, n)), device_id_type=MESH
        )
    pl.semaphore_wait(barrier, n - 1)
    copies = []
    for shift in range(1, n):
        target = lax.rem(me + shift, n)
        copy = pltpu.make_async_remote_copy(
            src_ref=x_ref.at[target],
            dst_ref=recv.at[shift],
            send_sem=send_sems.at[shift],
            recv_sem=recv_sems.at[shift],
            device_id=device_of(target),
            device_id_type=MESH,
        )
        copy.start()
        copies.append(copy)
    o_ref[...] = x_ref[me]
    for shift, copy in zip(range(1, n), copies):
        copy.wait_recv()
        o_ref[...] += recv[shift]
    for copy in copies:
        copy.wait_send()


def exchange_sum(x, n, group_index, device_of, collective_id):
    chunk = x.shape[1:]
    return pl.pallas_call(
        functools.partial(_exchange_sum_kernel, n, group_index, device_of),
        out_shape=jax.ShapeDtypeStruct(chunk, x.dtype),
        in_specs=[pl.BlockSpec(memory_space=pltpu.VMEM)],
        out_specs=pl.BlockSpec(memory_space=pltpu.VMEM),
        scratch_shapes=[
            pltpu.VMEM((n,) + chunk, x.dtype),
            pltpu.SemaphoreType.DMA((n,)),
            pltpu.SemaphoreType.DMA((n,)),
        ],
        compiler_params=pltpu.CompilerParams(collective_id=collective_id, has_side_effects=True),
    )(x)


def _two_stage_sum_kernel(n1, n2, x_ref, o_ref, stage, recv1, recv2, sems):
    me1 = lax.axis_index("tensor")
    me2 = lax.axis_index("dp")
    trial = lax.axis_index("trial")
    first = lambda j: (trial, me2, j)
    second = lambda j: (trial, j, me1)
    barrier = pltpu.get_barrier_semaphore()
    for shift in range(1, n1):
        pl.semaphore_signal(barrier, inc=1, device_id=first(lax.rem(me1 + shift, n1)), device_id_type=MESH)
    for shift in range(1, n2):
        pl.semaphore_signal(barrier, inc=1, device_id=second(lax.rem(me2 + shift, n2)), device_id_type=MESH)
    pl.semaphore_wait(barrier, n1 + n2 - 2)
    copies = []
    for shift in range(1, n1):
        target = lax.rem(me1 + shift, n1)
        copy = pltpu.make_async_remote_copy(
            src_ref=x_ref.at[target],
            dst_ref=recv1.at[shift],
            send_sem=sems.at[0, shift],
            recv_sem=sems.at[1, shift],
            device_id=first(target),
            device_id_type=MESH,
        )
        copy.start()
        copies.append(copy)
    stage[...] = x_ref[me1]
    for shift, copy in zip(range(1, n1), copies):
        copy.wait_recv()
        stage[...] += recv1[shift]
    copies2 = []
    for shift in range(1, n2):
        target = lax.rem(me2 + shift, n2)
        copy = pltpu.make_async_remote_copy(
            src_ref=stage.at[target],
            dst_ref=recv2.at[shift],
            send_sem=sems.at[2, shift],
            recv_sem=sems.at[3, shift],
            device_id=second(target),
            device_id_type=MESH,
        )
        copy.start()
        copies2.append(copy)
    o_ref[...] = stage[me2]
    for shift, copy in zip(range(1, n2), copies2):
        copy.wait_recv()
        o_ref[...] += recv2[shift]
    for copy in copies + copies2:
        copy.wait_send()


def two_stage_sum(x, collective_id):
    n1, n2 = x.shape[0], x.shape[1]
    chunk = x.shape[2:]
    return pl.pallas_call(
        functools.partial(_two_stage_sum_kernel, n1, n2),
        out_shape=jax.ShapeDtypeStruct(chunk, x.dtype),
        in_specs=[pl.BlockSpec(memory_space=pltpu.VMEM)],
        out_specs=pl.BlockSpec(memory_space=pltpu.VMEM),
        scratch_shapes=[
            pltpu.VMEM((n2,) + chunk, x.dtype),
            pltpu.VMEM((n1, n2) + chunk, x.dtype),
            pltpu.VMEM((n2,) + chunk, x.dtype),
            pltpu.SemaphoreType.DMA((4, max(n1, n2))),
        ],
        compiler_params=pltpu.CompilerParams(collective_id=collective_id, has_side_effects=True),
    )(x)


def _scatter_rows_kernel(trials, tensors, select, x_ref, o_ref, landed, send_sems, recv_sems):
    n = trials * tensors
    width = o_ref.shape[1]
    me = lax.axis_index("trial") * tensors + lax.axis_index("tensor")
    dp = lax.axis_index("dp")
    member = lambda g: (g // tensors, dp, lax.rem(g, tensors))
    barrier = pltpu.get_barrier_semaphore()
    for shift in range(1, n):
        pl.semaphore_signal(barrier, inc=1, device_id=member(lax.rem(me + shift, n)), device_id_type=MESH)
    pl.semaphore_wait(barrier, n - 1)
    copies = []
    for shift in range(1, n):
        target = lax.rem(me + shift, n)
        copy = pltpu.make_async_remote_copy(
            src_ref=x_ref.at[
                pl.ds(pl.multiple_of((target // tensors) * select, select), select),
                pl.ds(pl.multiple_of(lax.rem(target, tensors) * width, width), width),
            ],
            dst_ref=landed.at[pl.ds(pl.multiple_of(me * select, select), select)],
            send_sem=send_sems.at[shift],
            recv_sem=recv_sems.at[shift],
            device_id=member(target),
            device_id_type=MESH,
        )
        copy.start()
        copies.append(copy)
    own = pl.ds(pl.multiple_of(me * select, select), select)
    o_ref[own, :] = x_ref[
        pl.ds(pl.multiple_of(lax.axis_index("trial") * select, select), select),
        pl.ds(pl.multiple_of(lax.axis_index("tensor") * width, width), width),
    ]
    for shift, copy in zip(range(1, n), copies):
        copy.wait_recv()
        source = pl.ds(pl.multiple_of(lax.rem(me + n - shift, n) * select, select), select)
        o_ref[source, :] = landed[source, :]
    for copy in copies:
        copy.wait_send()


def scatter_rows(x, trials, tensors, select, collective_id):
    width = x.shape[1] // tensors
    rows = trials * tensors * select
    return pl.pallas_call(
        functools.partial(_scatter_rows_kernel, trials, tensors, select),
        out_shape=jax.ShapeDtypeStruct((rows, width), x.dtype),
        in_specs=[pl.BlockSpec(memory_space=pltpu.VMEM)],
        out_specs=pl.BlockSpec(memory_space=pltpu.VMEM),
        scratch_shapes=[
            pltpu.VMEM((rows, width), x.dtype),
            pltpu.SemaphoreType.DMA((trials * tensors,)),
            pltpu.SemaphoreType.DMA((trials * tensors,)),
        ],
        compiler_params=pltpu.CompilerParams(collective_id=collective_id, has_side_effects=True),
    )(x)


def shards(
    residual_rows,
    input_norm_weight,
    trial_row_index,
    keyvalue_weight,
    adapter_down_weight,
    adapter_up_weight,
    keyvalue_gradient,
):
    trials = lax.axis_size("trial")
    tensors = lax.axis_size("tensor")
    dps = lax.axis_size("dp")
    tok_dev = trial_row_index.shape[1]
    select = tok_dev // (trials * tensors)
    normed_input = keyvalue_weight.shape[0]
    kv_width = keyvalue_weight.shape[1]
    keyvalue_half = kv_width // 2
    rank_index = adapter_up_weight.shape[1]
    pool_dev = residual_rows.shape[0]
    highest_precision = lax.Precision.HIGHEST

    source = lax.axis_index("trial") * tensors + lax.axis_index("tensor")
    picks = lax.dynamic_slice_in_dim(trial_row_index, source * select, select, 1).reshape(-1)
    onehot = (picks[:, None] == jnp.arange(pool_dev, dtype=jnp.int32)[None, :]).astype(jnp.bfloat16)
    wide = jnp.dot(onehot, residual_rows, preferred_element_type=jnp.float32)
    msq = jnp.mean(wide * wide, axis=1, keepdims=True)
    chosen = (wide * lax.rsqrt(msq + norm_eps) * input_norm_weight[None, :]).astype(jnp.bfloat16)
    rows = scatter_rows(chosen, trials, tensors, select, 2)

    up_weight = adapter_up_weight[0].astype(jnp.float32)
    grad_in = keyvalue_gradient[0].astype(jnp.float32)
    key_gradient_full = jnp.dot(
        grad_in[:, :keyvalue_half], up_weight[:, :keyvalue_half].T, precision=highest_precision
    )
    value_gradient_full = jnp.dot(
        grad_in[:, keyvalue_half:], up_weight[:, keyvalue_half:].T, precision=highest_precision
    )
    rank_gradient = (
        adapter_scale * jnp.concatenate([key_gradient_full, value_gradient_full], axis=1)
    ).astype(jnp.bfloat16)
    every_rank = lax.all_gather(rank_gradient, "tensor", axis=0, tiled=True)
    grad_a_term = lax.dot_general(
        every_rank, rows, (((0,), (0,)), ((), ())), preferred_element_type=jnp.float32
    )

    down_weight = adapter_down_weight[0]
    keyval = jnp.dot(rows, keyvalue_weight, preferred_element_type=jnp.float32)
    ranks = jnp.dot(rows, down_weight, preferred_element_type=jnp.float32)
    summed = lax.psum_scatter(
        jnp.concatenate([keyval, ranks], axis=1), "tensor", scatter_dimension=0, tiled=True
    )
    frozen_output_local = summed[:, :kv_width]
    local_rank_rows = summed[:, kv_width:]
    adapter_key = jnp.dot(
        local_rank_rows[:, :rank_index], up_weight[:, :keyvalue_half], precision=highest_precision
    )
    adapter_value = jnp.dot(
        local_rank_rows[:, rank_index:], up_weight[:, keyvalue_half:], precision=highest_precision
    )
    keyvalue_output = frozen_output_local + adapter_scale * jnp.concatenate(
        [adapter_key, adapter_value], axis=1
    )

    grad_a = exchange_sum(
        grad_a_term.reshape(dps, grad_a_term.shape[0] // dps, grad_a_term.shape[1]),
        dps,
        lambda: lax.axis_index("dp"),
        lambda j: (lax.axis_index("trial"), j, lax.axis_index("tensor")),
        0,
    )

    key_down_gradient = jnp.dot(
        local_rank_rows[:, :rank_index].T, grad_in[:, :keyvalue_half], precision=highest_precision
    )
    value_down_gradient = jnp.dot(
        local_rank_rows[:, rank_index:].T, grad_in[:, keyvalue_half:], precision=highest_precision
    )
    up_gradient_term = adapter_scale * jnp.concatenate(
        [key_down_gradient, value_down_gradient], axis=1
    )
    width = up_gradient_term.shape[1] // (dps * tensors)
    grad_b = two_stage_sum(
        up_gradient_term.reshape(rank_index, dps, tensors, width).transpose(2, 1, 0, 3), 1
    )
    return (keyvalue_output[None], grad_a[None], grad_b[None])


def solution(mesh):
    return jax.shard_map(
        shards,
        mesh=mesh,
        in_specs=(
            P(("trial", "dp", "tensor"), None),
            P(),
            P(None, "dp"),
            P("tensor", None),
            P("trial", "tensor", None),
            P("trial", None, None),
            P("trial", ("dp", "tensor"), None),
        ),
        out_specs=(
            P("trial", ("dp", "tensor"), None),
            P("trial", "dp", "tensor"),
            P("trial", None, ("dp", "tensor")),
        ),
        check_vma=False,
    )
```

```python
import functools

import jax
import jax.numpy as jnp
from jax import lax
from jax.experimental import pallas as pl
from jax.experimental.pallas import tpu as pltpu
from jax.sharding import PartitionSpec as P

MESH = pl.DeviceIdType.MESH

adapter_scale = 2.0
norm_eps = 1e-05


def _two_stage_sum_kernel(n1, n2, x_ref, o_ref, stage, recv1, recv2, sems):
    me1 = lax.axis_index("tensor")
    me2 = lax.axis_index("dp")
    trial = lax.axis_index("trial")
    first = lambda j: (trial, me2, j)
    second = lambda j: (trial, j, me1)
    barrier = pltpu.get_barrier_semaphore()
    for shift in range(1, n1):
        pl.semaphore_signal(barrier, inc=1, device_id=first(lax.rem(me1 + shift, n1)), device_id_type=MESH)
    for shift in range(1, n2):
        pl.semaphore_signal(barrier, inc=1, device_id=second(lax.rem(me2 + shift, n2)), device_id_type=MESH)
    pl.semaphore_wait(barrier, n1 + n2 - 2)
    copies = []
    for shift in range(1, n1):
        target = lax.rem(me1 + shift, n1)
        copy = pltpu.make_async_remote_copy(
            src_ref=x_ref.at[target],
            dst_ref=recv1.at[shift],
            send_sem=sems.at[0, shift],
            recv_sem=sems.at[1, shift],
            device_id=first(target),
            device_id_type=MESH,
        )
        copy.start()
        copies.append(copy)
    stage[...] = x_ref[me1]
    for shift, copy in zip(range(1, n1), copies):
        copy.wait_recv()
        stage[...] += recv1[shift]
    copies2 = []
    for shift in range(1, n2):
        target = lax.rem(me2 + shift, n2)
        copy = pltpu.make_async_remote_copy(
            src_ref=stage.at[target],
            dst_ref=recv2.at[shift],
            send_sem=sems.at[2, shift],
            recv_sem=sems.at[3, shift],
            device_id=second(target),
            device_id_type=MESH,
        )
        copy.start()
        copies2.append(copy)
    o_ref[...] = stage[me2]
    for shift, copy in zip(range(1, n2), copies2):
        copy.wait_recv()
        o_ref[...] += recv2[shift]
    for copy in copies + copies2:
        copy.wait_send()


def two_stage_sum(x, collective_id):
    n1, n2 = x.shape[0], x.shape[1]
    chunk = x.shape[2:]
    return pl.pallas_call(
        functools.partial(_two_stage_sum_kernel, n1, n2),
        out_shape=jax.ShapeDtypeStruct(chunk, x.dtype),
        in_specs=[pl.BlockSpec(memory_space=pltpu.VMEM)],
        out_specs=pl.BlockSpec(memory_space=pltpu.VMEM),
        scratch_shapes=[
            pltpu.VMEM((n2,) + chunk, x.dtype),
            pltpu.VMEM((n1, n2) + chunk, x.dtype),
            pltpu.VMEM((n2,) + chunk, x.dtype),
            pltpu.SemaphoreType.DMA((4, max(n1, n2))),
        ],
        compiler_params=pltpu.CompilerParams(collective_id=collective_id, has_side_effects=True),
    )(x)


def _tensor_sum_kernel(n, kv_ref, rk_ref, own_kv_ref, own_rk_ref, kv_out, rk_out, recv_kv, recv_rk, sems):
    me = lax.axis_index("tensor")
    member = lambda j: (lax.axis_index("trial"), lax.axis_index("dp"), j)
    barrier = pltpu.get_barrier_semaphore()
    for shift in range(1, n):
        pl.semaphore_signal(barrier, inc=1, device_id=member(lax.rem(me + shift, n)), device_id_type=MESH)
    pl.semaphore_wait(barrier, n - 1)
    copies = []
    for shift in range(1, n):
        target = lax.rem(me + shift, n)
        for which, (src_ref, dst_ref) in enumerate(((kv_ref, recv_kv), (rk_ref, recv_rk))):
            copy = pltpu.make_async_remote_copy(
                src_ref=src_ref.at[target],
                dst_ref=dst_ref.at[shift],
                send_sem=sems.at[2 * which, shift],
                recv_sem=sems.at[2 * which + 1, shift],
                device_id=member(target),
                device_id_type=MESH,
            )
            copy.start()
            copies.append(copy)
    kv_out[...] = own_kv_ref[...]
    rk_out[...] = own_rk_ref[...]
    for shift in range(1, n):
        kv_copy, rk_copy = copies[2 * shift - 2], copies[2 * shift - 1]
        rk_copy.wait_recv()
        rk_out[...] += recv_rk[shift]
        kv_copy.wait_recv()
        kv_out[...] += recv_kv[shift].astype(jnp.float32)
    for copy in copies:
        copy.wait_send()


def tensor_sum(kv, rk, own_kv, own_rk, collective_id):
    n = kv.shape[0]
    vmem = pl.BlockSpec(memory_space=pltpu.VMEM)
    return pl.pallas_call(
        functools.partial(_tensor_sum_kernel, n),
        out_shape=(
            jax.ShapeDtypeStruct(own_kv.shape, jnp.float32),
            jax.ShapeDtypeStruct(own_rk.shape, jnp.float32),
        ),
        in_specs=[vmem] * 4,
        out_specs=(vmem, vmem),
        scratch_shapes=[
            pltpu.VMEM(kv.shape, kv.dtype),
            pltpu.VMEM(rk.shape, rk.dtype),
            pltpu.SemaphoreType.DMA((4, n)),
        ],
        compiler_params=pltpu.CompilerParams(collective_id=collective_id, has_side_effects=True),
    )(kv, rk, own_kv, own_rk)


def shards(
    residual_rows,
    input_norm_weight,
    trial_row_index,
    keyvalue_weight,
    adapter_down_weight,
    adapter_up_weight,
    keyvalue_gradient,
):
    trials = lax.axis_size("trial")
    tensors = lax.axis_size("tensor")
    dps = lax.axis_size("dp")
    tok_dev = trial_row_index.shape[1]
    select = tok_dev // (trials * tensors)
    normed_input = keyvalue_weight.shape[0]
    kv_width = keyvalue_weight.shape[1]
    keyvalue_half = kv_width // 2
    rank_index = adapter_up_weight.shape[1]
    pool_dev = residual_rows.shape[0]
    highest_precision = lax.Precision.HIGHEST

    source = lax.axis_index("trial") * tensors + lax.axis_index("tensor")
    picks = lax.dynamic_slice_in_dim(trial_row_index, source * select, select, 1).reshape(-1)
    onehot = (picks[:, None] == jnp.arange(pool_dev, dtype=jnp.int32)[None, :]).astype(jnp.bfloat16)
    wide = jnp.dot(onehot, residual_rows, preferred_element_type=jnp.float32)
    msq = jnp.mean(wide * wide, axis=1, keepdims=True)
    chosen = (wide * lax.rsqrt(msq + norm_eps) * input_norm_weight[None, :]).astype(jnp.bfloat16)
    chosen = chosen.reshape(trials, select, tensors, normed_input).transpose(0, 2, 1, 3)
    arrived = lax.all_to_all(
        chosen.reshape(trials * tensors, select, normed_input),
        ("trial", "tensor"),
        split_axis=0,
        concat_axis=0,
        tiled=True,
    )
    rows = arrived.reshape(tok_dev, normed_input)

    up_weight = adapter_up_weight[0].astype(jnp.float32)
    grad_in = keyvalue_gradient[0].astype(jnp.float32)
    key_gradient_full = jnp.dot(
        grad_in[:, :keyvalue_half], up_weight[:, :keyvalue_half].T, precision=highest_precision
    )
    value_gradient_full = jnp.dot(
        grad_in[:, keyvalue_half:], up_weight[:, keyvalue_half:].T, precision=highest_precision
    )
    rank_gradient = (
        adapter_scale * jnp.concatenate([key_gradient_full, value_gradient_full], axis=1)
    ).astype(jnp.bfloat16)
    every_rank = lax.all_gather(rank_gradient, "tensor", axis=0, tiled=True)
    grad_a_term = lax.dot_general(
        every_rank, rows, (((0,), (0,)), ((), ())), preferred_element_type=jnp.float32
    )

    down_weight = adapter_down_weight[0]
    keyval = jnp.dot(rows, keyvalue_weight, preferred_element_type=jnp.float32)
    ranks = jnp.dot(rows, down_weight, preferred_element_type=jnp.float32)
    block = tok_dev // tensors
    mine = lax.axis_index("tensor") * block
    frozen_output_local, local_rank_rows = tensor_sum(
        keyval.astype(jnp.bfloat16).reshape(tensors, block, kv_width),
        ranks.reshape(tensors, block, ranks.shape[1]),
        lax.dynamic_slice_in_dim(keyval, mine, block, 0),
        lax.dynamic_slice_in_dim(ranks, mine, block, 0),
        0,
    )
    adapter_key = jnp.dot(
        local_rank_rows[:, :rank_index], up_weight[:, :keyvalue_half], precision=highest_precision
    )
    adapter_value = jnp.dot(
        local_rank_rows[:, rank_index:], up_weight[:, keyvalue_half:], precision=highest_precision
    )
    keyvalue_output = frozen_output_local + adapter_scale * jnp.concatenate(
        [adapter_key, adapter_value], axis=1
    )

    grad_a = lax.psum_scatter(grad_a_term, "dp", scatter_dimension=0, tiled=True)

    key_down_gradient = jnp.dot(
        local_rank_rows[:, :rank_index].T, grad_in[:, :keyvalue_half], precision=highest_precision
    )
    value_down_gradient = jnp.dot(
        local_rank_rows[:, rank_index:].T, grad_in[:, keyvalue_half:], precision=highest_precision
    )
    up_gradient_term = adapter_scale * jnp.concatenate(
        [key_down_gradient, value_down_gradient], axis=1
    )
    width = up_gradient_term.shape[1] // (dps * tensors)
    grad_b = two_stage_sum(
        up_gradient_term.reshape(rank_index, dps, tensors, width).transpose(2, 1, 0, 3), 1
    )
    return (keyvalue_output[None], grad_a[None], grad_b[None])


def solution(mesh):
    return jax.shard_map(
        shards,
        mesh=mesh,
        in_specs=(
            P(("trial", "dp", "tensor"), None),
            P(),
            P(None, "dp"),
            P("tensor", None),
            P("trial", "tensor", None),
            P("trial", None, None),
            P("trial", ("dp", "tensor"), None),
        ),
        out_specs=(
            P("trial", ("dp", "tensor"), None),
            P("trial", "dp", "tensor"),
            P("trial", None, ("dp", "tensor")),
        ),
        check_vma=False,
    )
```

```python
import functools

import jax
import jax.numpy as jnp
from jax import lax
from jax.experimental import pallas as pl
from jax.experimental.pallas import tpu as pltpu
from jax.sharding import PartitionSpec as P

MESH = pl.DeviceIdType.MESH

adapter_scale = 2.0
norm_eps = 1e-05


def _two_stage_sum_kernel(n1, n2, x_ref, o_ref, stage, recv1, recv2, sems):
    me1 = lax.axis_index("tensor")
    me2 = lax.axis_index("dp")
    trial = lax.axis_index("trial")
    first = lambda j: (trial, me2, j)
    second = lambda j: (trial, j, me1)
    barrier = pltpu.get_barrier_semaphore()
    for shift in range(1, n1):
        pl.semaphore_signal(barrier, inc=1, device_id=first(lax.rem(me1 + shift, n1)), device_id_type=MESH)
    for shift in range(1, n2):
        pl.semaphore_signal(barrier, inc=1, device_id=second(lax.rem(me2 + shift, n2)), device_id_type=MESH)
    pl.semaphore_wait(barrier, n1 + n2 - 2)
    copies = []
    for shift in range(1, n1):
        target = lax.rem(me1 + shift, n1)
        copy = pltpu.make_async_remote_copy(
            src_ref=x_ref.at[target],
            dst_ref=recv1.at[shift],
            send_sem=sems.at[0, shift],
            recv_sem=sems.at[1, shift],
            device_id=first(target),
            device_id_type=MESH,
        )
        copy.start()
        copies.append(copy)
    stage[...] = x_ref[me1]
    for shift, copy in zip(range(1, n1), copies):
        copy.wait_recv()
        stage[...] += recv1[shift]
    copies2 = []
    for shift in range(1, n2):
        target = lax.rem(me2 + shift, n2)
        copy = pltpu.make_async_remote_copy(
            src_ref=stage.at[target],
            dst_ref=recv2.at[shift],
            send_sem=sems.at[2, shift],
            recv_sem=sems.at[3, shift],
            device_id=second(target),
            device_id_type=MESH,
        )
        copy.start()
        copies2.append(copy)
    o_ref[...] = stage[me2]
    for shift, copy in zip(range(1, n2), copies2):
        copy.wait_recv()
        o_ref[...] += recv2[shift]
    for copy in copies + copies2:
        copy.wait_send()


def two_stage_sum(x, collective_id):
    n1, n2 = x.shape[0], x.shape[1]
    chunk = x.shape[2:]
    return pl.pallas_call(
        functools.partial(_two_stage_sum_kernel, n1, n2),
        out_shape=jax.ShapeDtypeStruct(chunk, x.dtype),
        in_specs=[pl.BlockSpec(memory_space=pltpu.VMEM)],
        out_specs=pl.BlockSpec(memory_space=pltpu.VMEM),
        scratch_shapes=[
            pltpu.VMEM((n2,) + chunk, x.dtype),
            pltpu.VMEM((n1, n2) + chunk, x.dtype),
            pltpu.VMEM((n2,) + chunk, x.dtype),
            pltpu.SemaphoreType.DMA((4, max(n1, n2))),
        ],
        compiler_params=pltpu.CompilerParams(collective_id=collective_id, has_side_effects=True),
    )(x)


def _tensor_sum_kernel(n, kv_ref, rk_ref, own_kv_ref, own_rk_ref, kv_out, rk_out, recv_kv, recv_rk, sems):
    me = lax.axis_index("tensor")
    member = lambda j: (lax.axis_index("trial"), lax.axis_index("dp"), j)
    barrier = pltpu.get_barrier_semaphore()
    for shift in range(1, n):
        pl.semaphore_signal(barrier, inc=1, device_id=member(lax.rem(me + shift, n)), device_id_type=MESH)
    pl.semaphore_wait(barrier, n - 1)
    copies = []
    for shift in range(1, n):
        target = lax.rem(me + shift, n)
        for which, (src_ref, dst_ref) in enumerate(((kv_ref, recv_kv), (rk_ref, recv_rk))):
            copy = pltpu.make_async_remote_copy(
                src_ref=src_ref.at[target],
                dst_ref=dst_ref.at[shift],
                send_sem=sems.at[2 * which, shift],
                recv_sem=sems.at[2 * which + 1, shift],
                device_id=member(target),
                device_id_type=MESH,
            )
            copy.start()
            copies.append(copy)
    kv_out[...] = own_kv_ref[...]
    rk_out[...] = own_rk_ref[...]
    for shift in range(1, n):
        kv_copy, rk_copy = copies[2 * shift - 2], copies[2 * shift - 1]
        rk_copy.wait_recv()
        rk_out[...] += recv_rk[shift]
        kv_copy.wait_recv()
        kv_out[...] += recv_kv[shift].astype(jnp.float32)
    for copy in copies:
        copy.wait_send()


def tensor_sum(kv, rk, own_kv, own_rk, collective_id):
    n = kv.shape[0]
    vmem = pl.BlockSpec(memory_space=pltpu.VMEM)
    return pl.pallas_call(
        functools.partial(_tensor_sum_kernel, n),
        out_shape=(
            jax.ShapeDtypeStruct(own_kv.shape, jnp.float32),
            jax.ShapeDtypeStruct(own_rk.shape, jnp.float32),
        ),
        in_specs=[vmem] * 4,
        out_specs=(vmem, vmem),
        scratch_shapes=[
            pltpu.VMEM(kv.shape, kv.dtype),
            pltpu.VMEM(rk.shape, rk.dtype),
            pltpu.SemaphoreType.DMA((4, n)),
        ],
        compiler_params=pltpu.CompilerParams(collective_id=collective_id, has_side_effects=True),
    )(kv, rk, own_kv, own_rk)


def shards(
    residual_rows,
    input_norm_weight,
    trial_row_index,
    keyvalue_weight,
    adapter_down_weight,
    adapter_up_weight,
    keyvalue_gradient,
):
    trials = lax.axis_size("trial")
    tensors = lax.axis_size("tensor")
    dps = lax.axis_size("dp")
    tok_dev = trial_row_index.shape[1]
    select = tok_dev // (trials * tensors)
    normed_input = keyvalue_weight.shape[0]
    kv_width = keyvalue_weight.shape[1]
    keyvalue_half = kv_width // 2
    rank_index = adapter_up_weight.shape[1]
    pool_dev = residual_rows.shape[0]
    highest_precision = lax.Precision.HIGHEST

    source = lax.axis_index("trial") * tensors + lax.axis_index("tensor")
    picks = lax.dynamic_slice_in_dim(trial_row_index, source * select, select, 1).reshape(-1)
    onehot = (picks[:, None] == jnp.arange(pool_dev, dtype=jnp.int32)[None, :]).astype(jnp.bfloat16)
    wide = jnp.einsum(
        "tsr,rkf->tksf",
        onehot.reshape(trials, select, pool_dev),
        residual_rows.reshape(pool_dev, tensors, normed_input),
        preferred_element_type=jnp.float32,
    )
    msq = jnp.mean(wide * wide, axis=(1, 3), keepdims=True)
    gain = input_norm_weight.reshape(1, tensors, 1, normed_input)
    chosen = (wide * lax.rsqrt(msq + norm_eps) * gain).astype(jnp.bfloat16)
    arrived = lax.all_to_all(
        chosen.reshape(trials * tensors, select, normed_input),
        ("trial", "tensor"),
        split_axis=0,
        concat_axis=0,
        tiled=True,
    )
    rows = arrived.reshape(tok_dev, normed_input)

    up_weight = adapter_up_weight[0].astype(jnp.float32)
    grad_in = keyvalue_gradient[0].astype(jnp.float32)
    key_gradient_full = jnp.dot(
        grad_in[:, :keyvalue_half], up_weight[:, :keyvalue_half].T, precision=highest_precision
    )
    value_gradient_full = jnp.dot(
        grad_in[:, keyvalue_half:], up_weight[:, keyvalue_half:].T, precision=highest_precision
    )
    rank_gradient = (
        adapter_scale * jnp.concatenate([key_gradient_full, value_gradient_full], axis=1)
    ).astype(jnp.bfloat16)
    every_rank = lax.all_gather(rank_gradient, "tensor", axis=0, tiled=True)
    grad_a_term = lax.dot_general(
        every_rank, rows, (((0,), (0,)), ((), ())), preferred_element_type=jnp.float32
    )

    down_weight = adapter_down_weight[0]
    keyval = jnp.dot(rows, keyvalue_weight, preferred_element_type=jnp.float32)
    ranks = jnp.dot(rows, down_weight, preferred_element_type=jnp.float32)
    block = tok_dev // tensors
    mine = lax.axis_index("tensor") * block
    frozen_output_local, local_rank_rows = tensor_sum(
        keyval.astype(jnp.bfloat16).reshape(tensors, block, kv_width),
        ranks.reshape(tensors, block, ranks.shape[1]),
        lax.dynamic_slice_in_dim(keyval, mine, block, 0),
        lax.dynamic_slice_in_dim(ranks, mine, block, 0),
        0,
    )
    adapter_key = jnp.dot(
        local_rank_rows[:, :rank_index], up_weight[:, :keyvalue_half], precision=highest_precision
    )
    adapter_value = jnp.dot(
        local_rank_rows[:, rank_index:], up_weight[:, keyvalue_half:], precision=highest_precision
    )
    keyvalue_output = frozen_output_local + adapter_scale * jnp.concatenate(
        [adapter_key, adapter_value], axis=1
    )

    grad_a = lax.psum_scatter(grad_a_term, "dp", scatter_dimension=0, tiled=True)

    key_down_gradient = jnp.dot(
        local_rank_rows[:, :rank_index].T, grad_in[:, :keyvalue_half], precision=highest_precision
    )
    value_down_gradient = jnp.dot(
        local_rank_rows[:, rank_index:].T, grad_in[:, keyvalue_half:], precision=highest_precision
    )
    up_gradient_term = adapter_scale * jnp.concatenate(
        [key_down_gradient, value_down_gradient], axis=1
    )
    width = up_gradient_term.shape[1] // (dps * tensors)
    grad_b = two_stage_sum(
        up_gradient_term.reshape(rank_index, dps, tensors, width).transpose(2, 1, 0, 3), 1
    )
    return (keyvalue_output[None], grad_a[None], grad_b[None])


def solution(mesh):
    return jax.shard_map(
        shards,
        mesh=mesh,
        in_specs=(
            P(("trial", "dp", "tensor"), None),
            P(),
            P(None, "dp"),
            P("tensor", None),
            P("trial", "tensor", None),
            P("trial", None, None),
            P("trial", ("dp", "tensor"), None),
        ),
        out_specs=(
            P("trial", ("dp", "tensor"), None),
            P("trial", "dp", "tensor"),
            P("trial", None, ("dp", "tensor")),
        ),
        check_vma=False,
    )
```

```python
import functools

import jax
import jax.numpy as jnp
from jax import lax
from jax.experimental import pallas as pl
from jax.experimental.pallas import tpu as pltpu
from jax.sharding import PartitionSpec as P

MESH = pl.DeviceIdType.MESH

adapter_scale = 2.0
norm_eps = 1e-05


def _tensor_sum_kernel(
    n1, n2, kv_ref, rk_ref, own_kv_ref, own_rk_ref, gk_ref, gv_ref,
    kv_out, rk_out, b_out,
    recv_kv, recv_rk, terms, recv_b1, partial, recv_b2, sems,
):
    me1 = lax.axis_index("tensor")
    me2 = lax.axis_index("dp")
    trial = lax.axis_index("trial")
    first = lambda j: (trial, me2, j)
    second = lambda j: (trial, j, me1)
    quarter = n2 // 2
    barrier = pltpu.get_barrier_semaphore()
    for shift in range(1, n1):
        pl.semaphore_signal(barrier, inc=1, device_id=first(lax.rem(me1 + shift, n1)), device_id_type=MESH)
    for shift in range(1, n2):
        pl.semaphore_signal(barrier, inc=1, device_id=second(lax.rem(me2 + shift, n2)), device_id_type=MESH)
    pl.semaphore_wait(barrier, n1 + n2 - 2)

    def send(src_ref, dst_ref, row, shift, device):
        copy = pltpu.make_async_remote_copy(
            src_ref=src_ref,
            dst_ref=dst_ref.at[shift],
            send_sem=sems.at[row, shift],
            recv_sem=sems.at[row + 1, shift],
            device_id=device,
            device_id_type=MESH,
        )
        copy.start()
        return copy

    rk_copies, kv_copies = [], []
    for shift in range(1, n1):
        target = lax.rem(me1 + shift, n1)
        rk_copies.append(send(rk_ref.at[target], recv_rk, 2, shift, first(target)))
    for shift in range(1, n1):
        target = lax.rem(me1 + shift, n1)
        kv_copies.append(send(kv_ref.at[target], recv_kv, 0, shift, first(target)))

    rk_out[...] = own_rk_ref[...]
    for shift, copy in zip(range(1, n1), rk_copies):
        copy.wait_recv()
        rk_out[...] += recv_rk[shift]

    xa = rk_out[...]
    lane = lax.broadcasted_iota(jnp.int32, xa.shape, 1)
    half = xa.shape[1] // 2
    total = None
    for g_ref, keep in ((gk_ref, lane < half), (gv_ref, lane >= half)):
        part = jnp.where(keep, xa, 0.0)
        high = part.astype(jnp.bfloat16)
        low = (part - high.astype(jnp.float32)).astype(jnp.bfloat16)
        g = g_ref[...]
        for piece in (high, low):
            term = jnp.dot(g, piece, preferred_element_type=jnp.float32)
            total = term if total is None else total + term
    terms[...] = total.reshape(terms.shape)

    b1_copies = []
    for shift in range(1, n1):
        target = lax.rem(me1 + shift, n1)
        b1_copies.append(send(terms.at[target], recv_b1, 4, shift, first(target)))

    kv_out[...] = own_kv_ref[...]
    for shift, copy in zip(range(1, n1), kv_copies):
        copy.wait_recv()
        kv_out[...] += recv_kv[shift].astype(jnp.float32)

    summed = terms[me1]
    for shift, copy in zip(range(1, n1), b1_copies):
        copy.wait_recv()
        summed = summed + recv_b1[shift]
    partial[...] = summed.reshape(partial.shape)

    b2_copies = []
    for shift in range(1, n2):
        target = lax.rem(me2 + shift, n2)
        b2_copies.append(send(partial.at[lax.rem(target, quarter)], recv_b2, 6, shift, second(target)))
    b_out[...] = partial[lax.rem(me2, quarter)]
    for shift, copy in zip(range(1, n2), b2_copies):
        copy.wait_recv()
        b_out[...] += recv_b2[shift]

    for copy in rk_copies + kv_copies + b1_copies + b2_copies:
        copy.wait_send()


def tensor_sum(kv, rk, own_kv, own_rk, gk, gv, n2, collective_id):
    n1 = kv.shape[0]
    quarter = n2 // 2
    columns = gk.shape[0]
    lanes = rk.shape[2]
    block = columns // (n1 * quarter)
    vmem = pl.BlockSpec(memory_space=pltpu.VMEM)
    return pl.pallas_call(
        functools.partial(_tensor_sum_kernel, n1, n2),
        out_shape=(
            jax.ShapeDtypeStruct(own_kv.shape, jnp.float32),
            jax.ShapeDtypeStruct(own_rk.shape, jnp.float32),
            jax.ShapeDtypeStruct((block, lanes), jnp.float32),
        ),
        in_specs=[vmem] * 6,
        out_specs=(vmem, vmem, vmem),
        scratch_shapes=[
            pltpu.VMEM(kv.shape, kv.dtype),
            pltpu.VMEM(rk.shape, rk.dtype),
            pltpu.VMEM((n1, quarter * block, lanes), jnp.float32),
            pltpu.VMEM((n1, quarter * block, lanes), jnp.float32),
            pltpu.VMEM((quarter, block, lanes), jnp.float32),
            pltpu.VMEM((n2, block, lanes), jnp.float32),
            pltpu.SemaphoreType.DMA((8, max(n1, n2))),
        ],
        compiler_params=pltpu.CompilerParams(collective_id=collective_id, has_side_effects=True),
    )(kv, rk, own_kv, own_rk, gk, gv)


def shards(
    residual_rows,
    input_norm_weight,
    trial_row_index,
    keyvalue_weight,
    adapter_down_weight,
    adapter_up_weight,
    keyvalue_gradient,
):
    trials = lax.axis_size("trial")
    tensors = lax.axis_size("tensor")
    dps = lax.axis_size("dp")
    tok_dev = trial_row_index.shape[1]
    select = tok_dev // (trials * tensors)
    normed_input = keyvalue_weight.shape[0]
    kv_width = keyvalue_weight.shape[1]
    keyvalue_half = kv_width // 2
    rank_index = adapter_up_weight.shape[1]
    pool_dev = residual_rows.shape[0]
    highest_precision = lax.Precision.HIGHEST

    source = lax.axis_index("trial") * tensors + lax.axis_index("tensor")
    picks = lax.dynamic_slice_in_dim(trial_row_index, source * select, select, 1).reshape(-1)
    onehot = (picks[:, None] == jnp.arange(pool_dev, dtype=jnp.int32)[None, :]).astype(jnp.bfloat16)
    wide = jnp.einsum(
        "tsr,rkf->tksf",
        onehot.reshape(trials, select, pool_dev),
        residual_rows.reshape(pool_dev, tensors, normed_input),
        preferred_element_type=jnp.float32,
    )
    msq = jnp.mean(wide * wide, axis=(1, 3), keepdims=True)
    gain = input_norm_weight.reshape(1, tensors, 1, normed_input)
    chosen = (wide * lax.rsqrt(msq + norm_eps) * gain).astype(jnp.bfloat16)
    arrived = lax.all_to_all(
        chosen.reshape(trials * tensors, select, normed_input),
        ("trial", "tensor"),
        split_axis=0,
        concat_axis=0,
        tiled=True,
    )
    rows = arrived.reshape(tok_dev, normed_input)

    up_weight = adapter_up_weight[0].astype(jnp.float32)
    grad_in = keyvalue_gradient[0].astype(jnp.float32)
    key_gradient_full = jnp.dot(
        grad_in[:, :keyvalue_half], up_weight[:, :keyvalue_half].T, precision=highest_precision
    )
    value_gradient_full = jnp.dot(
        grad_in[:, keyvalue_half:], up_weight[:, keyvalue_half:].T, precision=highest_precision
    )
    rank_gradient = (
        adapter_scale * jnp.concatenate([key_gradient_full, value_gradient_full], axis=1)
    ).astype(jnp.bfloat16)
    every_rank = lax.all_gather(rank_gradient, "tensor", axis=0, tiled=True)
    grad_a_term = lax.dot_general(
        every_rank, rows, (((0,), (0,)), ((), ())), preferred_element_type=jnp.float32
    )

    down_weight = adapter_down_weight[0]
    keyval = jnp.dot(rows, keyvalue_weight, preferred_element_type=jnp.float32)
    ranks = jnp.dot(rows, down_weight, preferred_element_type=jnp.float32)
    block = tok_dev // tensors
    mine = lax.axis_index("tensor") * block
    quarter = dps // 2
    width = kv_width // (dps * tensors)
    grad_t = keyvalue_gradient[0].T.reshape(2, quarter, tensors, width, tok_dev // tensors)
    grad_t = grad_t.transpose(0, 2, 1, 3, 4).reshape(2, keyvalue_half, tok_dev // tensors)
    frozen_output_local, local_rank_rows, up_block = tensor_sum(
        keyval.astype(jnp.bfloat16).reshape(tensors, block, kv_width),
        ranks.reshape(tensors, block, ranks.shape[1]),
        lax.dynamic_slice_in_dim(keyval, mine, block, 0),
        lax.dynamic_slice_in_dim(ranks, mine, block, 0),
        grad_t[0],
        grad_t[1],
        dps,
        0,
    )
    adapter_key = jnp.dot(
        local_rank_rows[:, :rank_index], up_weight[:, :keyvalue_half], precision=highest_precision
    )
    adapter_value = jnp.dot(
        local_rank_rows[:, rank_index:], up_weight[:, keyvalue_half:], precision=highest_precision
    )
    keyvalue_output = frozen_output_local + adapter_scale * jnp.concatenate(
        [adapter_key, adapter_value], axis=1
    )

    grad_a = lax.psum_scatter(grad_a_term, "dp", scatter_dimension=0, tiled=True)

    grad_b = adapter_scale * jnp.where(
        lax.axis_index("dp") < quarter, up_block[:, :rank_index], up_block[:, rank_index:]
    ).T
    return (keyvalue_output[None], grad_a[None], grad_b[None])


def solution(mesh):
    return jax.shard_map(
        shards,
        mesh=mesh,
        in_specs=(
            P(("trial", "dp", "tensor"), None),
            P(),
            P(None, "dp"),
            P("tensor", None),
            P("trial", "tensor", None),
            P("trial", None, None),
            P("trial", ("dp", "tensor"), None),
        ),
        out_specs=(
            P("trial", ("dp", "tensor"), None),
            P("trial", "dp", "tensor"),
            P("trial", None, ("dp", "tensor")),
        ),
        check_vma=False,
    )
```

```python
import functools

import jax
import jax.numpy as jnp
from jax import lax
from jax.experimental import pallas as pl
from jax.experimental.pallas import tpu as pltpu
from jax.sharding import PartitionSpec as P

MESH = pl.DeviceIdType.MESH

adapter_scale = 2.0
norm_eps = 1e-05


def _tensor_sum_kernel(
    n1, n2, kv_ref, rk_ref, own_kv_ref, own_rk_ref, gk_ref, gv_ref, up_ref,
    kv_out, rk_out, b_out,
    recv_kv, recv_rk, terms, recv_b1, partial, recv_b2, sems,
):
    me1 = lax.axis_index("tensor")
    me2 = lax.axis_index("dp")
    trial = lax.axis_index("trial")
    first = lambda j: (trial, me2, j)
    second = lambda j: (trial, j, me1)
    quarter = n2 // 2
    barrier = pltpu.get_barrier_semaphore()
    for shift in range(1, n1):
        pl.semaphore_signal(barrier, inc=1, device_id=first(lax.rem(me1 + shift, n1)), device_id_type=MESH)
    for shift in range(1, n2):
        pl.semaphore_signal(barrier, inc=1, device_id=second(lax.rem(me2 + shift, n2)), device_id_type=MESH)
    pl.semaphore_wait(barrier, n1 + n2 - 2)

    def send(src_ref, dst_ref, row, shift, device):
        copy = pltpu.make_async_remote_copy(
            src_ref=src_ref,
            dst_ref=dst_ref.at[shift],
            send_sem=sems.at[row, shift],
            recv_sem=sems.at[row + 1, shift],
            device_id=device,
            device_id_type=MESH,
        )
        copy.start()
        return copy

    rk_copies, kv_copies = [], []
    for shift in range(1, n1):
        target = lax.rem(me1 + shift, n1)
        rk_copies.append(send(rk_ref.at[target], recv_rk, 2, shift, first(target)))
    for shift in range(1, n1):
        target = lax.rem(me1 + shift, n1)
        kv_copies.append(send(kv_ref.at[target], recv_kv, 0, shift, first(target)))

    rk_out[...] = own_rk_ref[...]
    for shift, copy in zip(range(1, n1), rk_copies):
        copy.wait_recv()
        rk_out[...] += recv_rk[shift]

    xa = rk_out[...]
    lane = lax.broadcasted_iota(jnp.int32, xa.shape, 1)
    half = xa.shape[1] // 2
    total = None
    for g_ref, keep in ((gk_ref, lane < half), (gv_ref, lane >= half)):
        part = jnp.where(keep, xa, 0.0)
        high = part.astype(jnp.bfloat16)
        low = (part - high.astype(jnp.float32)).astype(jnp.bfloat16)
        g = g_ref[...]
        for piece in (high, low):
            term = jnp.dot(g, piece, preferred_element_type=jnp.float32)
            total = term if total is None else total + term
    terms[...] = total.reshape(terms.shape)

    b1_copies = []
    for shift in range(1, n1):
        target = lax.rem(me1 + shift, n1)
        b1_copies.append(send(terms.at[target], recv_b1, 4, shift, first(target)))

    high = xa.astype(jnp.bfloat16)
    low = (xa - high.astype(jnp.float32)).astype(jnp.bfloat16)
    up = up_ref[...]
    adapter = jnp.dot(high, up, preferred_element_type=jnp.float32) + jnp.dot(
        low, up, preferred_element_type=jnp.float32
    )
    kv_out[...] = own_kv_ref[...] + adapter_scale * adapter
    for shift, copy in zip(range(1, n1), kv_copies):
        copy.wait_recv()
        kv_out[...] += recv_kv[shift].astype(jnp.float32)

    summed = terms[me1]
    for shift, copy in zip(range(1, n1), b1_copies):
        copy.wait_recv()
        summed = summed + recv_b1[shift]
    partial[...] = summed.reshape(partial.shape)

    b2_copies = []
    for shift in range(1, n2):
        target = lax.rem(me2 + shift, n2)
        b2_copies.append(send(partial.at[lax.rem(target, quarter)], recv_b2, 6, shift, second(target)))
    b_out[...] = partial[lax.rem(me2, quarter)]
    for shift, copy in zip(range(1, n2), b2_copies):
        copy.wait_recv()
        b_out[...] += recv_b2[shift]

    for copy in rk_copies + kv_copies + b1_copies + b2_copies:
        copy.wait_send()


def tensor_sum(kv, rk, own_kv, own_rk, gk, gv, up, n2, collective_id):
    n1 = kv.shape[0]
    quarter = n2 // 2
    columns = gk.shape[0]
    lanes = rk.shape[2]
    block = columns // (n1 * quarter)
    vmem = pl.BlockSpec(memory_space=pltpu.VMEM)
    return pl.pallas_call(
        functools.partial(_tensor_sum_kernel, n1, n2),
        out_shape=(
            jax.ShapeDtypeStruct(own_kv.shape, jnp.float32),
            jax.ShapeDtypeStruct(own_rk.shape, jnp.float32),
            jax.ShapeDtypeStruct((block, lanes), jnp.float32),
        ),
        in_specs=[vmem] * 7,
        out_specs=(vmem, vmem, vmem),
        scratch_shapes=[
            pltpu.VMEM(kv.shape, kv.dtype),
            pltpu.VMEM(rk.shape, rk.dtype),
            pltpu.VMEM((n1, quarter * block, lanes), jnp.float32),
            pltpu.VMEM((n1, quarter * block, lanes), jnp.float32),
            pltpu.VMEM((quarter, block, lanes), jnp.float32),
            pltpu.VMEM((n2, block, lanes), jnp.float32),
            pltpu.SemaphoreType.DMA((8, max(n1, n2))),
        ],
        compiler_params=pltpu.CompilerParams(collective_id=collective_id, has_side_effects=True),
    )(kv, rk, own_kv, own_rk, gk, gv, up)


def shards(
    residual_rows,
    input_norm_weight,
    trial_row_index,
    keyvalue_weight,
    adapter_down_weight,
    adapter_up_weight,
    keyvalue_gradient,
):
    trials = lax.axis_size("trial")
    tensors = lax.axis_size("tensor")
    dps = lax.axis_size("dp")
    tok_dev = trial_row_index.shape[1]
    select = tok_dev // (trials * tensors)
    normed_input = keyvalue_weight.shape[0]
    kv_width = keyvalue_weight.shape[1]
    keyvalue_half = kv_width // 2
    rank_index = adapter_up_weight.shape[1]
    pool_dev = residual_rows.shape[0]
    highest_precision = lax.Precision.HIGHEST

    source = lax.axis_index("trial") * tensors + lax.axis_index("tensor")
    picks = lax.dynamic_slice_in_dim(trial_row_index, source * select, select, 1).reshape(-1)
    onehot = (picks[:, None] == jnp.arange(pool_dev, dtype=jnp.int32)[None, :]).astype(jnp.bfloat16)
    wide = jnp.einsum(
        "tsr,rkf->tksf",
        onehot.reshape(trials, select, pool_dev),
        residual_rows.reshape(pool_dev, tensors, normed_input),
        preferred_element_type=jnp.float32,
    )
    msq = jnp.mean(wide * wide, axis=(1, 3), keepdims=True)
    gain = input_norm_weight.reshape(1, tensors, 1, normed_input)
    chosen = (wide * lax.rsqrt(msq + norm_eps) * gain).astype(jnp.bfloat16)
    half_in = normed_input // 2
    chosen = chosen.reshape(trials * tensors, select, normed_input)
    halves = [
        lax.all_to_all(
            chosen[:, :, h * half_in:(h + 1) * half_in],
            ("trial", "tensor"),
            split_axis=0,
            concat_axis=0,
            tiled=True,
        ).reshape(tok_dev, half_in)
        for h in range(2)
    ]

    up_weight = adapter_up_weight[0].astype(jnp.float32)
    grad_in = keyvalue_gradient[0].astype(jnp.float32)
    key_gradient_full = jnp.dot(
        grad_in[:, :keyvalue_half], up_weight[:, :keyvalue_half].T, precision=highest_precision
    )
    value_gradient_full = jnp.dot(
        grad_in[:, keyvalue_half:], up_weight[:, keyvalue_half:].T, precision=highest_precision
    )
    rank_gradient = (
        adapter_scale * jnp.concatenate([key_gradient_full, value_gradient_full], axis=1)
    ).astype(jnp.bfloat16)
    every_rank = lax.all_gather(rank_gradient, "tensor", axis=0, tiled=True)
    grad_a_term = jnp.concatenate(
        [
            lax.dot_general(
                every_rank, rows_h, (((0,), (0,)), ((), ())), preferred_element_type=jnp.float32
            )
            for rows_h in halves
        ],
        axis=1,
    )

    down_weight = adapter_down_weight[0]
    keyval = None
    ranks = None
    for h, rows_h in enumerate(halves):
        features = slice(h * half_in, (h + 1) * half_in)
        kv_h = jnp.dot(rows_h, keyvalue_weight[features], preferred_element_type=jnp.float32)
        rk_h = jnp.dot(rows_h, down_weight[features], preferred_element_type=jnp.float32)
        keyval = kv_h if keyval is None else keyval + kv_h
        ranks = rk_h if ranks is None else ranks + rk_h
    up_bf = adapter_up_weight[0]
    block_up = jnp.zeros((2 * rank_index, kv_width), up_bf.dtype)
    block_up = block_up.at[:rank_index, :keyvalue_half].set(up_bf[:, :keyvalue_half])
    block_up = block_up.at[rank_index:, keyvalue_half:].set(up_bf[:, keyvalue_half:])
    block = tok_dev // tensors
    mine = lax.axis_index("tensor") * block
    quarter = dps // 2
    width = kv_width // (dps * tensors)
    grad_t = keyvalue_gradient[0].T.reshape(2, quarter, tensors, width, tok_dev // tensors)
    grad_t = grad_t.transpose(0, 2, 1, 3, 4).reshape(2, keyvalue_half, tok_dev // tensors)
    frozen_output_local, local_rank_rows, up_block = tensor_sum(
        keyval.astype(jnp.bfloat16).reshape(tensors, block, kv_width),
        ranks.reshape(tensors, block, ranks.shape[1]),
        lax.dynamic_slice_in_dim(keyval, mine, block, 0),
        lax.dynamic_slice_in_dim(ranks, mine, block, 0),
        grad_t[0],
        grad_t[1],
        block_up,
        dps,
        0,
    )
    keyvalue_output = frozen_output_local

    grad_a = lax.psum_scatter(grad_a_term, "dp", scatter_dimension=0, tiled=True)

    grad_b = adapter_scale * jnp.where(
        lax.axis_index("dp") < quarter, up_block[:, :rank_index], up_block[:, rank_index:]
    ).T
    return (keyvalue_output[None], grad_a[None], grad_b[None])


def solution(mesh):
    return jax.shard_map(
        shards,
        mesh=mesh,
        in_specs=(
            P(("trial", "dp", "tensor"), None),
            P(),
            P(None, "dp"),
            P("tensor", None),
            P("trial", "tensor", None),
            P("trial", None, None),
            P("trial", ("dp", "tensor"), None),
        ),
        out_specs=(
            P("trial", ("dp", "tensor"), None),
            P("trial", "dp", "tensor"),
            P("trial", None, ("dp", "tensor")),
        ),
        check_vma=False,
    )
```

```python
import functools

import jax
import jax.numpy as jnp
from jax import lax
from jax.experimental import pallas as pl
from jax.experimental.pallas import tpu as pltpu
from jax.sharding import PartitionSpec as P

MESH = pl.DeviceIdType.MESH

adapter_scale = 2.0
norm_eps = 1e-05


def _tensor_sum_kernel(
    n1, n2, kv_ref, rk_ref, own_kv_ref, own_rk_ref, gk_ref, gv_ref,
    kv_out, rk_out, b_out,
    recv_kv, recv_rk, terms, recv_b1, partial, recv_b2, forward, sems,
):
    me1 = lax.axis_index("tensor")
    me2 = lax.axis_index("dp")
    trial = lax.axis_index("trial")
    first = lambda j: (trial, me2, j)
    second = lambda j: (trial, j, me1)
    quarter = n2 // 2
    barrier = pltpu.get_barrier_semaphore()
    for shift in range(1, n1):
        pl.semaphore_signal(barrier, inc=1, device_id=first(lax.rem(me1 + shift, n1)), device_id_type=MESH)
    for shift in range(1, n2):
        pl.semaphore_signal(barrier, inc=1, device_id=second(lax.rem(me2 + shift, n2)), device_id_type=MESH)
    pl.semaphore_wait(barrier, n1 + n2 - 2)

    def send(src_ref, dst_ref, row, shift, device):
        copy = pltpu.make_async_remote_copy(
            src_ref=src_ref,
            dst_ref=dst_ref.at[shift],
            send_sem=sems.at[row, shift],
            recv_sem=sems.at[row + 1, shift],
            device_id=device,
            device_id_type=MESH,
        )
        copy.start()
        return copy

    partner = me1 + 1 - 2 * lax.rem(me1, 2)
    across = lax.rem(me1 + 2, n1)
    diagonal = across + 1 - 2 * lax.rem(across, 2)
    rk_copies, kv_copies = [], []
    for shift in range(1, n1):
        target = lax.rem(me1 + shift, n1)
        rk_copies.append(send(rk_ref.at[target], recv_rk, 2, shift, first(target)))
    for slot, block in enumerate((partner, diagonal)):
        kv_copies.append(send(kv_ref.at[block], recv_kv, 0, slot, first(partner)))

    rk_out[...] = own_rk_ref[...]
    for shift, copy in zip(range(1, n1), rk_copies):
        copy.wait_recv()
        rk_out[...] += recv_rk[shift]

    xa = rk_out[...]
    lane = lax.broadcasted_iota(jnp.int32, xa.shape, 1)
    half = xa.shape[1] // 2
    total = None
    for g_ref, keep in ((gk_ref, lane < half), (gv_ref, lane >= half)):
        part = jnp.where(keep, xa, 0.0)
        high = part.astype(jnp.bfloat16)
        low = (part - high.astype(jnp.float32)).astype(jnp.bfloat16)
        g = g_ref[...]
        for piece in (high, low):
            term = jnp.dot(g, piece, preferred_element_type=jnp.float32)
            total = term if total is None else total + term
    terms[...] = total.reshape(terms.shape)

    b1_copies = []
    for shift in range(1, n1):
        target = lax.rem(me1 + shift, n1)
        b1_copies.append(send(terms.at[target], recv_b1, 4, shift, first(target)))

    kv_copies[1].wait_recv()
    forward[...] = (
        kv_ref[across].astype(jnp.float32) + recv_kv[1].astype(jnp.float32)
    ).astype(forward.dtype)
    kv_copies.append(send(forward, recv_kv, 0, 2, first(across)))
    kv_copies[0].wait_recv()
    kv_out[...] = own_kv_ref[...] + recv_kv[0].astype(jnp.float32)

    summed = terms[me1]
    for shift, copy in zip(range(1, n1), b1_copies):
        copy.wait_recv()
        summed = summed + recv_b1[shift]
    partial[...] = summed.reshape(partial.shape)

    b2_copies = []
    for shift in range(1, n2):
        target = lax.rem(me2 + shift, n2)
        b2_copies.append(send(partial.at[lax.rem(target, quarter)], recv_b2, 6, shift, second(target)))
    kv_copies[2].wait_recv()
    kv_out[...] += recv_kv[2].astype(jnp.float32)
    b_out[...] = partial[lax.rem(me2, quarter)]
    for shift, copy in zip(range(1, n2), b2_copies):
        copy.wait_recv()
        b_out[...] += recv_b2[shift]

    for copy in rk_copies + kv_copies + b1_copies + b2_copies:
        copy.wait_send()


def tensor_sum(kv, rk, own_kv, own_rk, gk, gv, n2, collective_id):
    n1 = kv.shape[0]
    quarter = n2 // 2
    columns = gk.shape[0]
    lanes = rk.shape[2]
    block = columns // (n1 * quarter)
    vmem = pl.BlockSpec(memory_space=pltpu.VMEM)
    return pl.pallas_call(
        functools.partial(_tensor_sum_kernel, n1, n2),
        out_shape=(
            jax.ShapeDtypeStruct(own_kv.shape, jnp.float32),
            jax.ShapeDtypeStruct(own_rk.shape, jnp.float32),
            jax.ShapeDtypeStruct((block, lanes), jnp.float32),
        ),
        in_specs=[vmem] * 6,
        out_specs=(vmem, vmem, vmem),
        scratch_shapes=[
            pltpu.VMEM(kv.shape, kv.dtype),
            pltpu.VMEM(rk.shape, rk.dtype),
            pltpu.VMEM((n1, quarter * block, lanes), jnp.float32),
            pltpu.VMEM((n1, quarter * block, lanes), jnp.float32),
            pltpu.VMEM((quarter, block, lanes), jnp.float32),
            pltpu.VMEM((n2, block, lanes), jnp.float32),
            pltpu.VMEM(kv.shape[1:], kv.dtype),
            pltpu.SemaphoreType.DMA((8, max(n1, n2))),
        ],
        compiler_params=pltpu.CompilerParams(collective_id=collective_id, has_side_effects=True),
    )(kv, rk, own_kv, own_rk, gk, gv)


def shards(
    residual_rows,
    input_norm_weight,
    trial_row_index,
    keyvalue_weight,
    adapter_down_weight,
    adapter_up_weight,
    keyvalue_gradient,
):
    trials = lax.axis_size("trial")
    tensors = lax.axis_size("tensor")
    dps = lax.axis_size("dp")
    tok_dev = trial_row_index.shape[1]
    select = tok_dev // (trials * tensors)
    normed_input = keyvalue_weight.shape[0]
    kv_width = keyvalue_weight.shape[1]
    keyvalue_half = kv_width // 2
    rank_index = adapter_up_weight.shape[1]
    pool_dev = residual_rows.shape[0]
    highest_precision = lax.Precision.HIGHEST

    source = lax.axis_index("trial") * tensors + lax.axis_index("tensor")
    picks = lax.dynamic_slice_in_dim(trial_row_index, source * select, select, 1).reshape(-1)
    onehot = (picks[:, None] == jnp.arange(pool_dev, dtype=jnp.int32)[None, :]).astype(jnp.bfloat16)
    wide = jnp.einsum(
        "tsr,rkf->tksf",
        onehot.reshape(trials, select, pool_dev),
        residual_rows.reshape(pool_dev, tensors, normed_input),
        preferred_element_type=jnp.float32,
    )
    msq = jnp.mean(wide * wide, axis=(1, 3), keepdims=True)
    gain = input_norm_weight.reshape(1, tensors, 1, normed_input)
    chosen = (wide * lax.rsqrt(msq + norm_eps) * gain).astype(jnp.bfloat16)
    arrived = lax.all_to_all(
        chosen.reshape(trials * tensors, select, normed_input),
        ("trial", "tensor"),
        split_axis=0,
        concat_axis=0,
        tiled=True,
    )
    rows = arrived.reshape(tok_dev, normed_input)

    up_weight = adapter_up_weight[0].astype(jnp.float32)
    grad_in = keyvalue_gradient[0].astype(jnp.float32)
    key_gradient_full = jnp.dot(
        grad_in[:, :keyvalue_half], up_weight[:, :keyvalue_half].T, precision=highest_precision
    )
    value_gradient_full = jnp.dot(
        grad_in[:, keyvalue_half:], up_weight[:, keyvalue_half:].T, precision=highest_precision
    )
    rank_gradient = (
        adapter_scale * jnp.concatenate([key_gradient_full, value_gradient_full], axis=1)
    ).astype(jnp.bfloat16)
    every_rank = lax.all_gather(rank_gradient, "tensor", axis=0, tiled=True)
    grad_a_term = lax.dot_general(
        every_rank, rows, (((0,), (0,)), ((), ())), preferred_element_type=jnp.float32
    )

    down_weight = adapter_down_weight[0]
    keyval = jnp.dot(rows, keyvalue_weight, preferred_element_type=jnp.float32)
    ranks = jnp.dot(rows, down_weight, preferred_element_type=jnp.float32)
    block = tok_dev // tensors
    mine = lax.axis_index("tensor") * block
    quarter = dps // 2
    width = kv_width // (dps * tensors)
    grad_t = keyvalue_gradient[0].T.reshape(2, quarter, tensors, width, tok_dev // tensors)
    grad_t = grad_t.transpose(0, 2, 1, 3, 4).reshape(2, keyvalue_half, tok_dev // tensors)
    frozen_output_local, local_rank_rows, up_block = tensor_sum(
        keyval.astype(jnp.bfloat16).reshape(tensors, block, kv_width),
        ranks.reshape(tensors, block, ranks.shape[1]),
        lax.dynamic_slice_in_dim(keyval, mine, block, 0),
        lax.dynamic_slice_in_dim(ranks, mine, block, 0),
        grad_t[0],
        grad_t[1],
        dps,
        0,
    )
    adapter_key = jnp.dot(
        local_rank_rows[:, :rank_index], up_weight[:, :keyvalue_half], precision=highest_precision
    )
    adapter_value = jnp.dot(
        local_rank_rows[:, rank_index:], up_weight[:, keyvalue_half:], precision=highest_precision
    )
    keyvalue_output = frozen_output_local + adapter_scale * jnp.concatenate(
        [adapter_key, adapter_value], axis=1
    )

    grad_a = lax.psum_scatter(grad_a_term, "dp", scatter_dimension=0, tiled=True)

    grad_b = adapter_scale * jnp.where(
        lax.axis_index("dp") < quarter, up_block[:, :rank_index], up_block[:, rank_index:]
    ).T
    return (keyvalue_output[None], grad_a[None], grad_b[None])


def solution(mesh):
    return jax.shard_map(
        shards,
        mesh=mesh,
        in_specs=(
            P(("trial", "dp", "tensor"), None),
            P(),
            P(None, "dp"),
            P("tensor", None),
            P("trial", "tensor", None),
            P("trial", None, None),
            P("trial", ("dp", "tensor"), None),
        ),
        out_specs=(
            P("trial", ("dp", "tensor"), None),
            P("trial", "dp", "tensor"),
            P("trial", None, ("dp", "tensor")),
        ),
        check_vma=False,
    )
```

```python
import functools

import jax
import jax.numpy as jnp
from jax import lax
from jax.experimental import pallas as pl
from jax.experimental.pallas import tpu as pltpu
from jax.sharding import PartitionSpec as P

MESH = pl.DeviceIdType.MESH

adapter_scale = 2.0
norm_eps = 1e-05


def _tensor_sum_kernel(
    n1, n2, kv_ref, rk_ref, own_kv_ref, own_rk_ref, gk_ref, gv_ref,
    kv_out, rk_out, b_out,
    recv_kv, recv_rk, terms, recv_b1, partial, recv_b2, forward, sems, kv_sems,
):
    me1 = lax.axis_index("tensor")
    me2 = lax.axis_index("dp")
    trial = lax.axis_index("trial")
    first = lambda j: (trial, me2, j)
    second = lambda j: (trial, j, me1)
    quarter = n2 // 2
    barrier = pltpu.get_barrier_semaphore()
    for shift in range(1, n1):
        pl.semaphore_signal(barrier, inc=1, device_id=first(lax.rem(me1 + shift, n1)), device_id_type=MESH)
    for shift in range(1, n2):
        pl.semaphore_signal(barrier, inc=1, device_id=second(lax.rem(me2 + shift, n2)), device_id_type=MESH)
    pl.semaphore_wait(barrier, n1 + n2 - 2)

    def send(src_ref, dst_ref, row, shift, device):
        copy = pltpu.make_async_remote_copy(
            src_ref=src_ref,
            dst_ref=dst_ref.at[shift],
            send_sem=sems.at[row, shift],
            recv_sem=sems.at[row + 1, shift],
            device_id=device,
            device_id_type=MESH,
        )
        copy.start()
        return copy

    partner = me1 + 1 - 2 * lax.rem(me1, 2)
    across = lax.rem(me1 + 2, n1)
    diagonal = across + 1 - 2 * lax.rem(across, 2)
    rk_copies = []
    for shift in range(1, n1):
        target = lax.rem(me1 + shift, n1)
        rk_copies.append(send(rk_ref.at[target], recv_rk, 2, shift, first(target)))
    pieces = kv_sems.shape[2]
    step = kv_ref.shape[1] // pieces

    def send_piece(src_ref, slot, piece, device):
        rows = pl.ds(piece * step, step)
        copy = pltpu.make_async_remote_copy(
            src_ref=src_ref.at[rows],
            dst_ref=recv_kv.at[slot, rows],
            send_sem=kv_sems.at[0, slot, piece],
            recv_sem=kv_sems.at[1, slot, piece],
            device_id=device,
            device_id_type=MESH,
        )
        copy.start()
        return copy

    diagonal_copies = [send_piece(kv_ref.at[diagonal], 1, p, first(partner)) for p in range(pieces)]
    own_copies = [send_piece(kv_ref.at[partner], 0, p, first(partner)) for p in range(pieces)]

    rk_out[...] = own_rk_ref[...]
    for shift, copy in zip(range(1, n1), rk_copies):
        copy.wait_recv()
        rk_out[...] += recv_rk[shift]

    xa = rk_out[...]
    lane = lax.broadcasted_iota(jnp.int32, xa.shape, 1)
    half = xa.shape[1] // 2
    total = None
    for g_ref, keep in ((gk_ref, lane < half), (gv_ref, lane >= half)):
        part = jnp.where(keep, xa, 0.0)
        high = part.astype(jnp.bfloat16)
        low = (part - high.astype(jnp.float32)).astype(jnp.bfloat16)
        g = g_ref[...]
        for piece in (high, low):
            term = jnp.dot(g, piece, preferred_element_type=jnp.float32)
            total = term if total is None else total + term
    terms[...] = total.reshape(terms.shape)

    b1_copies = []
    for shift in range(1, n1):
        target = lax.rem(me1 + shift, n1)
        b1_copies.append(send(terms.at[target], recv_b1, 4, shift, first(target)))

    forward_copies = []
    for p, copy in enumerate(diagonal_copies):
        rows = pl.ds(p * step, step)
        copy.wait_recv()
        forward[rows, :] = (
            kv_ref[across, rows, :].astype(jnp.float32) + recv_kv[1, rows, :].astype(jnp.float32)
        ).astype(forward.dtype)
        forward_copies.append(send_piece(forward, 2, p, first(across)))
    for p, copy in enumerate(own_copies):
        rows = pl.ds(p * step, step)
        copy.wait_recv()
        kv_out[rows, :] = own_kv_ref[rows, :] + recv_kv[0, rows, :].astype(jnp.float32)

    summed = terms[me1]
    for shift, copy in zip(range(1, n1), b1_copies):
        copy.wait_recv()
        summed = summed + recv_b1[shift]
    partial[...] = summed.reshape(partial.shape)

    b2_copies = []
    for shift in range(1, n2):
        target = lax.rem(me2 + shift, n2)
        b2_copies.append(send(partial.at[lax.rem(target, quarter)], recv_b2, 6, shift, second(target)))
    for p, copy in enumerate(forward_copies):
        rows = pl.ds(p * step, step)
        copy.wait_recv()
        kv_out[rows, :] += recv_kv[2, rows, :].astype(jnp.float32)
    b_out[...] = partial[lax.rem(me2, quarter)]
    for shift, copy in zip(range(1, n2), b2_copies):
        copy.wait_recv()
        b_out[...] += recv_b2[shift]

    for copy in rk_copies + diagonal_copies + own_copies + forward_copies + b1_copies + b2_copies:
        copy.wait_send()


def tensor_sum(kv, rk, own_kv, own_rk, gk, gv, n2, collective_id):
    n1 = kv.shape[0]
    quarter = n2 // 2
    columns = gk.shape[0]
    lanes = rk.shape[2]
    block = columns // (n1 * quarter)
    vmem = pl.BlockSpec(memory_space=pltpu.VMEM)
    return pl.pallas_call(
        functools.partial(_tensor_sum_kernel, n1, n2),
        out_shape=(
            jax.ShapeDtypeStruct(own_kv.shape, jnp.float32),
            jax.ShapeDtypeStruct(own_rk.shape, jnp.float32),
            jax.ShapeDtypeStruct((block, lanes), jnp.float32),
        ),
        in_specs=[vmem] * 6,
        out_specs=(vmem, vmem, vmem),
        scratch_shapes=[
            pltpu.VMEM(kv.shape, kv.dtype),
            pltpu.VMEM(rk.shape, rk.dtype),
            pltpu.VMEM((n1, quarter * block, lanes), jnp.float32),
            pltpu.VMEM((n1, quarter * block, lanes), jnp.float32),
            pltpu.VMEM((quarter, block, lanes), jnp.float32),
            pltpu.VMEM((n2, block, lanes), jnp.float32),
            pltpu.VMEM(kv.shape[1:], kv.dtype),
            pltpu.SemaphoreType.DMA((8, max(n1, n2))),
            pltpu.SemaphoreType.DMA((2, 3, 4)),
        ],
        compiler_params=pltpu.CompilerParams(collective_id=collective_id, has_side_effects=True),
    )(kv, rk, own_kv, own_rk, gk, gv)


def shards(
    residual_rows,
    input_norm_weight,
    trial_row_index,
    keyvalue_weight,
    adapter_down_weight,
    adapter_up_weight,
    keyvalue_gradient,
):
    trials = lax.axis_size("trial")
    tensors = lax.axis_size("tensor")
    dps = lax.axis_size("dp")
    tok_dev = trial_row_index.shape[1]
    select = tok_dev // (trials * tensors)
    normed_input = keyvalue_weight.shape[0]
    kv_width = keyvalue_weight.shape[1]
    keyvalue_half = kv_width // 2
    rank_index = adapter_up_weight.shape[1]
    pool_dev = residual_rows.shape[0]
    highest_precision = lax.Precision.HIGHEST

    source = lax.axis_index("trial") * tensors + lax.axis_index("tensor")
    picks = lax.dynamic_slice_in_dim(trial_row_index, source * select, select, 1).reshape(-1)
    onehot = (picks[:, None] == jnp.arange(pool_dev, dtype=jnp.int32)[None, :]).astype(jnp.bfloat16)
    wide = jnp.einsum(
        "tsr,rkf->tksf",
        onehot.reshape(trials, select, pool_dev),
        residual_rows.reshape(pool_dev, tensors, normed_input),
        preferred_element_type=jnp.float32,
    )
    msq = jnp.mean(wide * wide, axis=(1, 3), keepdims=True)
    gain = input_norm_weight.reshape(1, tensors, 1, normed_input)
    chosen = (wide * lax.rsqrt(msq + norm_eps) * gain).astype(jnp.bfloat16)
    arrived = lax.all_to_all(
        chosen.reshape(trials * tensors, select, normed_input),
        ("trial", "tensor"),
        split_axis=0,
        concat_axis=0,
        tiled=True,
    )
    rows = arrived.reshape(tok_dev, normed_input)

    up_weight = adapter_up_weight[0].astype(jnp.float32)
    grad_in = keyvalue_gradient[0].astype(jnp.float32)
    key_gradient_full = jnp.dot(
        grad_in[:, :keyvalue_half], up_weight[:, :keyvalue_half].T, precision=highest_precision
    )
    value_gradient_full = jnp.dot(
        grad_in[:, keyvalue_half:], up_weight[:, keyvalue_half:].T, precision=highest_precision
    )
    rank_gradient = (
        adapter_scale * jnp.concatenate([key_gradient_full, value_gradient_full], axis=1)
    ).astype(jnp.bfloat16)
    every_rank = lax.all_gather(rank_gradient, "tensor", axis=0, tiled=True)
    grad_a_term = lax.dot_general(
        every_rank, rows, (((0,), (0,)), ((), ())), preferred_element_type=jnp.float32
    )

    down_weight = adapter_down_weight[0]
    keyval = jnp.dot(rows, keyvalue_weight, preferred_element_type=jnp.float32)
    ranks = jnp.dot(rows, down_weight, preferred_element_type=jnp.float32)
    block = tok_dev // tensors
    mine = lax.axis_index("tensor") * block
    quarter = dps // 2
    width = kv_width // (dps * tensors)
    grad_t = keyvalue_gradient[0].T.reshape(2, quarter, tensors, width, tok_dev // tensors)
    grad_t = grad_t.transpose(0, 2, 1, 3, 4).reshape(2, keyvalue_half, tok_dev // tensors)
    frozen_output_local, local_rank_rows, up_block = tensor_sum(
        keyval.astype(jnp.bfloat16).reshape(tensors, block, kv_width),
        ranks.reshape(tensors, block, ranks.shape[1]),
        lax.dynamic_slice_in_dim(keyval, mine, block, 0),
        lax.dynamic_slice_in_dim(ranks, mine, block, 0),
        grad_t[0],
        grad_t[1],
        dps,
        0,
    )
    adapter_key = jnp.dot(
        local_rank_rows[:, :rank_index], up_weight[:, :keyvalue_half], precision=highest_precision
    )
    adapter_value = jnp.dot(
        local_rank_rows[:, rank_index:], up_weight[:, keyvalue_half:], precision=highest_precision
    )
    keyvalue_output = frozen_output_local + adapter_scale * jnp.concatenate(
        [adapter_key, adapter_value], axis=1
    )

    grad_a = lax.psum_scatter(grad_a_term, "dp", scatter_dimension=0, tiled=True)

    grad_b = adapter_scale * jnp.where(
        lax.axis_index("dp") < quarter, up_block[:, :rank_index], up_block[:, rank_index:]
    ).T
    return (keyvalue_output[None], grad_a[None], grad_b[None])


def solution(mesh):
    return jax.shard_map(
        shards,
        mesh=mesh,
        in_specs=(
            P(("trial", "dp", "tensor"), None),
            P(),
            P(None, "dp"),
            P("tensor", None),
            P("trial", "tensor", None),
            P("trial", None, None),
            P("trial", ("dp", "tensor"), None),
        ),
        out_specs=(
            P("trial", ("dp", "tensor"), None),
            P("trial", "dp", "tensor"),
            P("trial", None, ("dp", "tensor")),
        ),
        check_vma=False,
    )
```

```python
import functools

import jax
import jax.numpy as jnp
from jax import lax
from jax.experimental import pallas as pl
from jax.experimental.pallas import tpu as pltpu
from jax.sharding import PartitionSpec as P

MESH = pl.DeviceIdType.MESH

adapter_scale = 2.0
norm_eps = 1e-05


def _tensor_sum_kernel(
    n1, n2, kv_ref, rk_ref, own_kv_ref, own_rk_ref, gk_ref, gv_ref,
    kv_out, rk_out, b_out,
    recv_kv, recv_rk, terms, recv_b1, partial, recv_b2, forward, sems, kv_sems,
):
    me1 = lax.axis_index("tensor")
    me2 = lax.axis_index("dp")
    trial = lax.axis_index("trial")
    first = lambda j: (trial, me2, j)
    second = lambda j: (trial, j, me1)
    quarter = n2 // 2
    barrier = pltpu.get_barrier_semaphore()
    for shift in range(1, n1):
        pl.semaphore_signal(barrier, inc=1, device_id=first(lax.rem(me1 + shift, n1)), device_id_type=MESH)
    for shift in range(1, n2):
        pl.semaphore_signal(barrier, inc=1, device_id=second(lax.rem(me2 + shift, n2)), device_id_type=MESH)
    pl.semaphore_wait(barrier, n1 + n2 - 2)

    def send(src_ref, dst_ref, row, shift, device):
        copy = pltpu.make_async_remote_copy(
            src_ref=src_ref,
            dst_ref=dst_ref.at[shift],
            send_sem=sems.at[row, shift],
            recv_sem=sems.at[row + 1, shift],
            device_id=device,
            device_id_type=MESH,
        )
        copy.start()
        return copy

    partner = me1 + 1 - 2 * lax.rem(me1, 2)
    across = lax.rem(me1 + 2, n1)
    diagonal = across + 1 - 2 * lax.rem(across, 2)
    rk_copies = []
    for shift in range(1, n1):
        target = lax.rem(me1 + shift, n1)
        rk_copies.append(send(rk_ref.at[target], recv_rk, 2, shift, first(target)))
    pieces = kv_sems.shape[2]
    step = kv_ref.shape[1] // pieces

    def send_piece(src_ref, slot, piece, device):
        rows = pl.ds(piece * step, step)
        copy = pltpu.make_async_remote_copy(
            src_ref=src_ref.at[rows],
            dst_ref=recv_kv.at[slot, rows],
            send_sem=kv_sems.at[0, slot, piece],
            recv_sem=kv_sems.at[1, slot, piece],
            device_id=device,
            device_id_type=MESH,
        )
        copy.start()
        return copy

    diagonal_copies = [send_piece(kv_ref.at[diagonal], 1, p, first(partner)) for p in range(pieces)]
    own_copies = [send_piece(kv_ref.at[partner], 0, p, first(partner)) for p in range(pieces)]

    rk_out[...] = own_rk_ref[...]
    for shift, copy in zip(range(1, n1), rk_copies):
        copy.wait_recv()
        rk_out[...] += recv_rk[shift]

    xa = rk_out[...]
    lane = lax.broadcasted_iota(jnp.int32, xa.shape, 1)
    half = xa.shape[1] // 2
    total = None
    for g_ref, keep in ((gk_ref, lane < half), (gv_ref, lane >= half)):
        part = jnp.where(keep, xa, 0.0)
        high = part.astype(jnp.bfloat16)
        low = (part - high.astype(jnp.float32)).astype(jnp.bfloat16)
        g = g_ref[...]
        for piece in (high, low):
            term = jnp.dot(g, piece, preferred_element_type=jnp.float32)
            total = term if total is None else total + term
    terms[...] = total.reshape(terms.shape)

    b1_copies = []
    for shift in range(1, n1):
        target = lax.rem(me1 + shift, n1)
        b1_copies.append(send(terms.at[target], recv_b1, 4, shift, first(target)))

    forward_copies = []
    for p, copy in enumerate(diagonal_copies):
        rows = pl.ds(p * step, step)
        copy.wait_recv()
        forward[rows, :] = (
            kv_ref[across, rows, :].astype(jnp.float32) + recv_kv[1, rows, :].astype(jnp.float32)
        ).astype(forward.dtype)
        forward_copies.append(send_piece(forward, 2, p, first(across)))
    for p, copy in enumerate(own_copies):
        rows = pl.ds(p * step, step)
        copy.wait_recv()
        kv_out[rows, :] = own_kv_ref[rows, :] + recv_kv[0, rows, :].astype(jnp.float32)

    summed = terms[me1]
    for shift, copy in zip(range(1, n1), b1_copies):
        copy.wait_recv()
        summed = summed + recv_b1[shift]
    partial[...] = summed.reshape(partial.shape)

    b2_copies = []
    for shift in range(1, n2):
        target = lax.rem(me2 + shift, n2)
        b2_copies.append(send(partial.at[lax.rem(target, quarter)], recv_b2, 6, shift, second(target)))
    for p, copy in enumerate(forward_copies):
        rows = pl.ds(p * step, step)
        copy.wait_recv()
        kv_out[rows, :] += recv_kv[2, rows, :].astype(jnp.float32)
    b_out[...] = partial[lax.rem(me2, quarter)]
    for shift, copy in zip(range(1, n2), b2_copies):
        copy.wait_recv()
        b_out[...] += recv_b2[shift]

    for copy in rk_copies + diagonal_copies + own_copies + forward_copies + b1_copies + b2_copies:
        copy.wait_send()


def tensor_sum(kv, rk, own_kv, own_rk, gk, gv, n2, collective_id):
    n1 = kv.shape[0]
    quarter = n2 // 2
    columns = gk.shape[0]
    lanes = rk.shape[2]
    block = columns // (n1 * quarter)
    vmem = pl.BlockSpec(memory_space=pltpu.VMEM)
    return pl.pallas_call(
        functools.partial(_tensor_sum_kernel, n1, n2),
        out_shape=(
            jax.ShapeDtypeStruct(own_kv.shape, jnp.float32),
            jax.ShapeDtypeStruct(own_rk.shape, jnp.float32),
            jax.ShapeDtypeStruct((block, lanes), jnp.float32),
        ),
        in_specs=[vmem] * 6,
        out_specs=(vmem, vmem, vmem),
        scratch_shapes=[
            pltpu.VMEM(kv.shape, kv.dtype),
            pltpu.VMEM(rk.shape, rk.dtype),
            pltpu.VMEM((n1, quarter * block, lanes), jnp.float32),
            pltpu.VMEM((n1, quarter * block, lanes), jnp.float32),
            pltpu.VMEM((quarter, block, lanes), jnp.float32),
            pltpu.VMEM((n2, block, lanes), jnp.float32),
            pltpu.VMEM(kv.shape[1:], kv.dtype),
            pltpu.SemaphoreType.DMA((8, max(n1, n2))),
            pltpu.SemaphoreType.DMA((2, 3, 4)),
        ],
        compiler_params=pltpu.CompilerParams(collective_id=collective_id, has_side_effects=True),
    )(kv, rk, own_kv, own_rk, gk, gv)


def shards(
    residual_rows,
    input_norm_weight,
    trial_row_index,
    keyvalue_weight,
    adapter_down_weight,
    adapter_up_weight,
    keyvalue_gradient,
):
    trials = lax.axis_size("trial")
    tensors = lax.axis_size("tensor")
    dps = lax.axis_size("dp")
    tok_dev = trial_row_index.shape[1]
    select = tok_dev // (trials * tensors)
    normed_input = keyvalue_weight.shape[0]
    kv_width = keyvalue_weight.shape[1]
    keyvalue_half = kv_width // 2
    rank_index = adapter_up_weight.shape[1]
    pool_dev = residual_rows.shape[0]
    highest_precision = lax.Precision.HIGHEST

    source = lax.axis_index("trial") * tensors + lax.axis_index("tensor")
    picks = lax.dynamic_slice_in_dim(trial_row_index, source * select, select, 1).reshape(-1)
    onehot = (picks[:, None] == jnp.arange(pool_dev, dtype=jnp.int32)[None, :]).astype(jnp.bfloat16)
    wide = jnp.einsum(
        "tsr,rkf->tksf",
        onehot.reshape(trials, select, pool_dev),
        residual_rows.reshape(pool_dev, tensors, normed_input),
        preferred_element_type=jnp.float32,
    )
    raw = residual_rows.astype(jnp.float32)
    row_scale = lax.rsqrt(jnp.mean(raw * raw, axis=1) + norm_eps)
    picked_scale = jnp.dot(onehot.astype(jnp.float32), row_scale, precision=highest_precision)
    gain = input_norm_weight.reshape(1, tensors, 1, normed_input)
    chosen = (wide * picked_scale.reshape(trials, 1, select, 1) * gain).astype(jnp.bfloat16)
    arrived = lax.all_to_all(
        chosen.reshape(trials * tensors, select, normed_input),
        ("trial", "tensor"),
        split_axis=0,
        concat_axis=0,
        tiled=True,
    )
    rows = arrived.reshape(tok_dev, normed_input)

    up_weight = adapter_up_weight[0].astype(jnp.float32)
    grad_in = keyvalue_gradient[0].astype(jnp.float32)
    key_gradient_full = jnp.dot(
        grad_in[:, :keyvalue_half], up_weight[:, :keyvalue_half].T, precision=highest_precision
    )
    value_gradient_full = jnp.dot(
        grad_in[:, keyvalue_half:], up_weight[:, keyvalue_half:].T, precision=highest_precision
    )
    rank_gradient = (
        adapter_scale * jnp.concatenate([key_gradient_full, value_gradient_full], axis=1)
    ).astype(jnp.bfloat16)
    every_rank = lax.all_gather(rank_gradient, "tensor", axis=0, tiled=True)
    grad_a_term = lax.dot_general(
        every_rank, rows, (((0,), (0,)), ((), ())), preferred_element_type=jnp.float32
    )

    down_weight = adapter_down_weight[0]
    keyval = jnp.dot(rows, keyvalue_weight, preferred_element_type=jnp.float32)
    ranks = jnp.dot(rows, down_weight, preferred_element_type=jnp.float32)
    up_bf = adapter_up_weight[0]
    block_up = jnp.zeros((2 * rank_index, kv_width), up_bf.dtype)
    block_up = block_up.at[:rank_index, :keyvalue_half].set(up_bf[:, :keyvalue_half])
    block_up = block_up.at[rank_index:, keyvalue_half:].set(up_bf[:, keyvalue_half:])
    block = tok_dev // tensors
    mine = lax.axis_index("tensor") * block
    quarter = dps // 2
    width = kv_width // (dps * tensors)
    grad_t = keyvalue_gradient[0].T.reshape(2, quarter, tensors, width, tok_dev // tensors)
    grad_t = grad_t.transpose(0, 2, 1, 3, 4).reshape(2, keyvalue_half, tok_dev // tensors)
    frozen_output_local, local_rank_rows, up_block = tensor_sum(
        keyval.astype(jnp.bfloat16).reshape(tensors, block, kv_width),
        ranks.reshape(tensors, block, ranks.shape[1]),
        lax.dynamic_slice_in_dim(keyval, mine, block, 0),
        lax.dynamic_slice_in_dim(ranks, mine, block, 0),
        grad_t[0],
        grad_t[1],
        dps,
        0,
    )
    high = local_rank_rows.astype(jnp.bfloat16)
    low = (local_rank_rows - high.astype(jnp.float32)).astype(jnp.bfloat16)
    adapter = jnp.dot(
        jnp.concatenate([high, low], axis=1),
        jnp.concatenate([block_up, block_up], axis=0),
        preferred_element_type=jnp.float32,
    )
    keyvalue_output = frozen_output_local + adapter_scale * adapter

    grad_a = lax.psum_scatter(grad_a_term, "dp", scatter_dimension=0, tiled=True)

    grad_b = adapter_scale * jnp.where(
        lax.axis_index("dp") < quarter, up_block[:, :rank_index], up_block[:, rank_index:]
    ).T
    return (keyvalue_output[None], grad_a[None], grad_b[None])


def solution(mesh):
    return jax.shard_map(
        shards,
        mesh=mesh,
        in_specs=(
            P(("trial", "dp", "tensor"), None),
            P(),
            P(None, "dp"),
            P("tensor", None),
            P("trial", "tensor", None),
            P("trial", None, None),
            P("trial", ("dp", "tensor"), None),
        ),
        out_specs=(
            P("trial", ("dp", "tensor"), None),
            P("trial", "dp", "tensor"),
            P("trial", None, ("dp", "tensor")),
        ),
        check_vma=False,
    )
```

```python
import functools

import jax
import jax.numpy as jnp
from jax import lax
from jax.experimental import pallas as pl
from jax.experimental.pallas import tpu as pltpu
from jax.sharding import PartitionSpec as P

MESH = pl.DeviceIdType.MESH

adapter_scale = 2.0
norm_eps = 1e-05


def _tensor_sum_kernel(
    n1, n2, rows_ref, w_ref, rk_ref, own_rk_ref, gk_ref, gv_ref,
    kv_out, rk_out, b_out,
    recv_kv, recv_rk, terms, recv_b1, partial, recv_b2, forward, outgoing, across_part, sems, kv_sems,
):
    me1 = lax.axis_index("tensor")
    me2 = lax.axis_index("dp")
    trial = lax.axis_index("trial")
    first = lambda j: (trial, me2, j)
    second = lambda j: (trial, j, me1)
    quarter = n2 // 2
    barrier = pltpu.get_barrier_semaphore()
    for shift in range(1, n1):
        pl.semaphore_signal(barrier, inc=1, device_id=first(lax.rem(me1 + shift, n1)), device_id_type=MESH)
    for shift in range(1, n2):
        pl.semaphore_signal(barrier, inc=1, device_id=second(lax.rem(me2 + shift, n2)), device_id_type=MESH)
    pl.semaphore_wait(barrier, n1 + n2 - 2)

    def send(src_ref, dst_ref, row, shift, device):
        copy = pltpu.make_async_remote_copy(
            src_ref=src_ref,
            dst_ref=dst_ref.at[shift],
            send_sem=sems.at[row, shift],
            recv_sem=sems.at[row + 1, shift],
            device_id=device,
            device_id_type=MESH,
        )
        copy.start()
        return copy

    partner = me1 + 1 - 2 * lax.rem(me1, 2)
    across = lax.rem(me1 + 2, n1)
    diagonal = across + 1 - 2 * lax.rem(across, 2)
    rk_copies = []
    for shift in range(1, n1):
        target = lax.rem(me1 + shift, n1)
        rk_copies.append(send(rk_ref.at[target], recv_rk, 2, shift, first(target)))
    pieces = kv_sems.shape[2]
    step = kv_out.shape[0] // pieces

    def send_piece(src_ref, slot, piece, device):
        rows = pl.ds(piece * step, step)
        copy = pltpu.make_async_remote_copy(
            src_ref=src_ref.at[rows],
            dst_ref=recv_kv.at[slot, rows],
            send_sem=kv_sems.at[0, slot, piece],
            recv_sem=kv_sems.at[1, slot, piece],
            device_id=device,
            device_id_type=MESH,
        )
        copy.start()
        return copy

    tokens = kv_out.shape[0]

    def product(member):
        block = rows_ref[pl.ds(pl.multiple_of(member * tokens, tokens), tokens), :]
        return jnp.dot(block, w_ref[...], preferred_element_type=jnp.float32)

    outgoing[1] = product(diagonal).astype(outgoing.dtype)
    diagonal_copies = [send_piece(outgoing.at[1], 1, p, first(partner)) for p in range(pieces)]
    outgoing[0] = product(partner).astype(outgoing.dtype)
    own_copies = [send_piece(outgoing.at[0], 0, p, first(partner)) for p in range(pieces)]
    across_part[...] = product(across)
    own_part = product(me1)

    rk_out[...] = own_rk_ref[...]
    for shift, copy in zip(range(1, n1), rk_copies):
        copy.wait_recv()
        rk_out[...] += recv_rk[shift]

    xa = rk_out[...]
    lane = lax.broadcasted_iota(jnp.int32, xa.shape, 1)
    half = xa.shape[1] // 2
    total = None
    for g_ref, keep in ((gk_ref, lane < half), (gv_ref, lane >= half)):
        part = jnp.where(keep, xa, 0.0)
        high = part.astype(jnp.bfloat16)
        low = (part - high.astype(jnp.float32)).astype(jnp.bfloat16)
        g = g_ref[...]
        for piece in (high, low):
            term = jnp.dot(g, piece, preferred_element_type=jnp.float32)
            total = term if total is None else total + term
    terms[...] = total.reshape(terms.shape)

    b1_copies = []
    for shift in range(1, n1):
        target = lax.rem(me1 + shift, n1)
        b1_copies.append(send(terms.at[target], recv_b1, 4, shift, first(target)))

    forward_copies = []
    for p, copy in enumerate(diagonal_copies):
        rows = pl.ds(p * step, step)
        copy.wait_recv()
        forward[rows, :] = (
            across_part[rows, :] + recv_kv[1, rows, :].astype(jnp.float32)
        ).astype(forward.dtype)
        forward_copies.append(send_piece(forward, 2, p, first(across)))
    kv_out[...] = own_part
    for p, copy in enumerate(own_copies):
        rows = pl.ds(p * step, step)
        copy.wait_recv()
        kv_out[rows, :] += recv_kv[0, rows, :].astype(jnp.float32)

    summed = terms[me1]
    for shift, copy in zip(range(1, n1), b1_copies):
        copy.wait_recv()
        summed = summed + recv_b1[shift]
    partial[...] = summed.reshape(partial.shape)

    b2_copies = []
    for shift in range(1, n2):
        target = lax.rem(me2 + shift, n2)
        b2_copies.append(send(partial.at[lax.rem(target, quarter)], recv_b2, 6, shift, second(target)))
    for p, copy in enumerate(forward_copies):
        rows = pl.ds(p * step, step)
        copy.wait_recv()
        kv_out[rows, :] += recv_kv[2, rows, :].astype(jnp.float32)
    b_out[...] = partial[lax.rem(me2, quarter)]
    for shift, copy in zip(range(1, n2), b2_copies):
        copy.wait_recv()
        b_out[...] += recv_b2[shift]

    for copy in rk_copies + diagonal_copies + own_copies + forward_copies + b1_copies + b2_copies:
        copy.wait_send()


def tensor_sum(rows, w, rk, own_rk, gk, gv, n2, collective_id):
    n1 = rk.shape[0]
    tokens = rows.shape[0] // n1
    kv_width = w.shape[1]
    quarter = n2 // 2
    columns = gk.shape[0]
    lanes = rk.shape[2]
    block = columns // (n1 * quarter)
    vmem = pl.BlockSpec(memory_space=pltpu.VMEM)
    return pl.pallas_call(
        functools.partial(_tensor_sum_kernel, n1, n2),
        out_shape=(
            jax.ShapeDtypeStruct((tokens, kv_width), jnp.float32),
            jax.ShapeDtypeStruct(own_rk.shape, jnp.float32),
            jax.ShapeDtypeStruct((block, lanes), jnp.float32),
        ),
        in_specs=[vmem] * 6,
        out_specs=(vmem, vmem, vmem),
        scratch_shapes=[
            pltpu.VMEM((n1, tokens, kv_width), jnp.bfloat16),
            pltpu.VMEM(rk.shape, rk.dtype),
            pltpu.VMEM((n1, quarter * block, lanes), jnp.float32),
            pltpu.VMEM((n1, quarter * block, lanes), jnp.float32),
            pltpu.VMEM((quarter, block, lanes), jnp.float32),
            pltpu.VMEM((n2, block, lanes), jnp.float32),
            pltpu.VMEM((tokens, kv_width), jnp.bfloat16),
            pltpu.VMEM((2, tokens, kv_width), jnp.bfloat16),
            pltpu.VMEM((tokens, kv_width), jnp.float32),
            pltpu.SemaphoreType.DMA((8, max(n1, n2))),
            pltpu.SemaphoreType.DMA((2, 3, 4)),
        ],
        compiler_params=pltpu.CompilerParams(collective_id=collective_id, has_side_effects=True),
    )(rows, w, rk, own_rk, gk, gv)


def shards(
    residual_rows,
    input_norm_weight,
    trial_row_index,
    keyvalue_weight,
    adapter_down_weight,
    adapter_up_weight,
    keyvalue_gradient,
):
    trials = lax.axis_size("trial")
    tensors = lax.axis_size("tensor")
    dps = lax.axis_size("dp")
    tok_dev = trial_row_index.shape[1]
    select = tok_dev // (trials * tensors)
    normed_input = keyvalue_weight.shape[0]
    kv_width = keyvalue_weight.shape[1]
    keyvalue_half = kv_width // 2
    rank_index = adapter_up_weight.shape[1]
    pool_dev = residual_rows.shape[0]
    highest_precision = lax.Precision.HIGHEST

    source = lax.axis_index("trial") * tensors + lax.axis_index("tensor")
    picks = lax.dynamic_slice_in_dim(trial_row_index, source * select, select, 1).reshape(-1)
    onehot = (picks[:, None] == jnp.arange(pool_dev, dtype=jnp.int32)[None, :]).astype(jnp.bfloat16)
    wide = jnp.einsum(
        "tsr,rkf->tksf",
        onehot.reshape(trials, select, pool_dev),
        residual_rows.reshape(pool_dev, tensors, normed_input),
        preferred_element_type=jnp.float32,
    )
    msq = jnp.mean(wide * wide, axis=(1, 3), keepdims=True)
    gain = input_norm_weight.reshape(1, tensors, 1, normed_input)
    chosen = (wide * lax.rsqrt(msq + norm_eps) * gain).astype(jnp.bfloat16)
    arrived = lax.all_to_all(
        chosen.reshape(trials * tensors, select, normed_input),
        ("trial", "tensor"),
        split_axis=0,
        concat_axis=0,
        tiled=True,
    )
    rows = arrived.reshape(tok_dev, normed_input)

    up_weight = adapter_up_weight[0].astype(jnp.float32)
    grad_in = keyvalue_gradient[0].astype(jnp.float32)
    key_gradient_full = jnp.dot(
        grad_in[:, :keyvalue_half], up_weight[:, :keyvalue_half].T, precision=highest_precision
    )
    value_gradient_full = jnp.dot(
        grad_in[:, keyvalue_half:], up_weight[:, keyvalue_half:].T, precision=highest_precision
    )
    rank_gradient = (
        adapter_scale * jnp.concatenate([key_gradient_full, value_gradient_full], axis=1)
    ).astype(jnp.bfloat16)
    every_rank = lax.all_gather(rank_gradient, "tensor", axis=0, tiled=True)
    grad_a_term = lax.dot_general(
        every_rank, rows, (((0,), (0,)), ((), ())), preferred_element_type=jnp.float32
    )

    down_weight = adapter_down_weight[0]
    ranks = jnp.dot(rows, down_weight, preferred_element_type=jnp.float32)
    block = tok_dev // tensors
    mine = lax.axis_index("tensor") * block
    quarter = dps // 2
    width = kv_width // (dps * tensors)
    grad_t = keyvalue_gradient[0].T.reshape(2, quarter, tensors, width, tok_dev // tensors)
    grad_t = grad_t.transpose(0, 2, 1, 3, 4).reshape(2, keyvalue_half, tok_dev // tensors)
    frozen_output_local, local_rank_rows, up_block = tensor_sum(
        rows,
        keyvalue_weight,
        ranks.reshape(tensors, block, ranks.shape[1]),
        lax.dynamic_slice_in_dim(ranks, mine, block, 0),
        grad_t[0],
        grad_t[1],
        dps,
        0,
    )
    adapter_key = jnp.dot(
        local_rank_rows[:, :rank_index], up_weight[:, :keyvalue_half], precision=highest_precision
    )
    adapter_value = jnp.dot(
        local_rank_rows[:, rank_index:], up_weight[:, keyvalue_half:], precision=highest_precision
    )
    keyvalue_output = frozen_output_local + adapter_scale * jnp.concatenate(
        [adapter_key, adapter_value], axis=1
    )

    grad_a = lax.psum_scatter(grad_a_term, "dp", scatter_dimension=0, tiled=True)

    grad_b = adapter_scale * jnp.where(
        lax.axis_index("dp") < quarter, up_block[:, :rank_index], up_block[:, rank_index:]
    ).T
    return (keyvalue_output[None], grad_a[None], grad_b[None])


def solution(mesh):
    return jax.shard_map(
        shards,
        mesh=mesh,
        in_specs=(
            P(("trial", "dp", "tensor"), None),
            P(),
            P(None, "dp"),
            P("tensor", None),
            P("trial", "tensor", None),
            P("trial", None, None),
            P("trial", ("dp", "tensor"), None),
        ),
        out_specs=(
            P("trial", ("dp", "tensor"), None),
            P("trial", "dp", "tensor"),
            P("trial", None, ("dp", "tensor")),
        ),
        check_vma=False,
    )
```

```python
import functools

import jax
import jax.numpy as jnp
from jax import lax
from jax.experimental import pallas as pl
from jax.experimental.pallas import tpu as pltpu
from jax.sharding import PartitionSpec as P

MESH = pl.DeviceIdType.MESH

adapter_scale = 2.0
norm_eps = 1e-05


def _tensor_sum_kernel(
    n1, n2, rows_ref, w_ref, rk_ref, own_rk_ref, gk_ref, gv_ref,
    kv_out, rk_out, b_out,
    recv_kv, recv_rk, terms, recv_b1, partial, recv_b2, forward, outgoing, across_part, sems, kv_sems,
):
    me1 = lax.axis_index("tensor")
    me2 = lax.axis_index("dp")
    trial = lax.axis_index("trial")
    first = lambda j: (trial, me2, j)
    second = lambda j: (trial, j, me1)
    quarter = n2 // 2
    barrier = pltpu.get_barrier_semaphore()
    for shift in range(1, n1):
        pl.semaphore_signal(barrier, inc=1, device_id=first(lax.rem(me1 + shift, n1)), device_id_type=MESH)
    for shift in range(1, n2):
        pl.semaphore_signal(barrier, inc=1, device_id=second(lax.rem(me2 + shift, n2)), device_id_type=MESH)
    pl.semaphore_wait(barrier, n1 + n2 - 2)

    def send(src_ref, dst_ref, row, shift, device):
        copy = pltpu.make_async_remote_copy(
            src_ref=src_ref,
            dst_ref=dst_ref.at[shift],
            send_sem=sems.at[row, shift],
            recv_sem=sems.at[row + 1, shift],
            device_id=device,
            device_id_type=MESH,
        )
        copy.start()
        return copy

    partner = me1 + 1 - 2 * lax.rem(me1, 2)
    across = lax.rem(me1 + 2, n1)
    diagonal = across + 1 - 2 * lax.rem(across, 2)
    rk_copies = []
    for shift in range(1, n1):
        target = lax.rem(me1 + shift, n1)
        rk_copies.append(send(rk_ref.at[target], recv_rk, 2, shift, first(target)))
    pieces = kv_sems.shape[2]
    step = kv_out.shape[0] // pieces

    def send_piece(src_ref, slot, piece, device):
        rows = pl.ds(piece * step, step)
        copy = pltpu.make_async_remote_copy(
            src_ref=src_ref.at[rows],
            dst_ref=recv_kv.at[slot, rows],
            send_sem=kv_sems.at[0, slot, piece],
            recv_sem=kv_sems.at[1, slot, piece],
            device_id=device,
            device_id_type=MESH,
        )
        copy.start()
        return copy

    tokens = kv_out.shape[0]

    def product(member):
        block = rows_ref[pl.ds(pl.multiple_of(member * tokens, tokens), tokens), :]
        return jnp.dot(block, w_ref[...], preferred_element_type=jnp.float32)

    outgoing[1] = product(diagonal).astype(outgoing.dtype)
    diagonal_copies = [send_piece(outgoing.at[1], 1, p, first(partner)) for p in range(pieces)]
    outgoing[0] = product(partner).astype(outgoing.dtype)
    own_copies = [send_piece(outgoing.at[0], 0, p, first(partner)) for p in range(pieces)]
    across_part[...] = product(across)
    own_part = product(me1)

    rk_out[...] = own_rk_ref[...]
    for shift, copy in zip(range(1, n1), rk_copies):
        copy.wait_recv()
        rk_out[...] += recv_rk[shift]

    xa = rk_out[...]
    lane = lax.broadcasted_iota(jnp.int32, xa.shape, 1)
    half = xa.shape[1] // 2
    total = None
    for g_ref, keep in ((gk_ref, lane < half), (gv_ref, lane >= half)):
        part = jnp.where(keep, xa, 0.0)
        high = part.astype(jnp.bfloat16)
        low = (part - high.astype(jnp.float32)).astype(jnp.bfloat16)
        g = g_ref[...]
        for piece in (high, low):
            term = jnp.dot(g, piece, preferred_element_type=jnp.float32)
            total = term if total is None else total + term
    terms[...] = total.reshape(terms.shape)

    b1_copies = []
    for shift in range(1, n1):
        target = lax.rem(me1 + shift, n1)
        b1_copies.append(send(terms.at[target], recv_b1, 4, shift, first(target)))

    forward_copies = []
    for p, copy in enumerate(diagonal_copies):
        rows = pl.ds(p * step, step)
        copy.wait_recv()
        forward[rows, :] = (
            across_part[rows, :] + recv_kv[1, rows, :].astype(jnp.float32)
        ).astype(forward.dtype)
        forward_copies.append(send_piece(forward, 2, p, first(across)))
    kv_out[...] = own_part
    for p, copy in enumerate(own_copies):
        rows = pl.ds(p * step, step)
        copy.wait_recv()
        kv_out[rows, :] += recv_kv[0, rows, :].astype(jnp.float32)

    summed = terms[me1]
    for shift, copy in zip(range(1, n1), b1_copies):
        copy.wait_recv()
        summed = summed + recv_b1[shift]
    partial[...] = summed.reshape(partial.shape)

    b2_copies = []
    for shift in range(1, n2):
        target = lax.rem(me2 + shift, n2)
        b2_copies.append(send(partial.at[lax.rem(target, quarter)], recv_b2, 6, shift, second(target)))
    for p, copy in enumerate(forward_copies):
        rows = pl.ds(p * step, step)
        copy.wait_recv()
        kv_out[rows, :] += recv_kv[2, rows, :].astype(jnp.float32)
    b_out[...] = partial[lax.rem(me2, quarter)]
    for shift, copy in zip(range(1, n2), b2_copies):
        copy.wait_recv()
        b_out[...] += recv_b2[shift]

    for copy in rk_copies + diagonal_copies + own_copies + forward_copies + b1_copies + b2_copies:
        copy.wait_send()


def tensor_sum(rows, w, rk, own_rk, gk, gv, n2, collective_id):
    n1 = rk.shape[0]
    tokens = rows.shape[0] // n1
    kv_width = w.shape[1]
    quarter = n2 // 2
    columns = gk.shape[0]
    lanes = rk.shape[2]
    block = columns // (n1 * quarter)
    vmem = pl.BlockSpec(memory_space=pltpu.VMEM)
    return pl.pallas_call(
        functools.partial(_tensor_sum_kernel, n1, n2),
        out_shape=(
            jax.ShapeDtypeStruct((tokens, kv_width), jnp.float32),
            jax.ShapeDtypeStruct(own_rk.shape, jnp.float32),
            jax.ShapeDtypeStruct((block, lanes), jnp.float32),
        ),
        in_specs=[vmem] * 6,
        out_specs=(vmem, vmem, vmem),
        scratch_shapes=[
            pltpu.VMEM((n1, tokens, kv_width), jnp.bfloat16),
            pltpu.VMEM(rk.shape, rk.dtype),
            pltpu.VMEM((n1, quarter * block, lanes), jnp.float32),
            pltpu.VMEM((n1, quarter * block, lanes), jnp.float32),
            pltpu.VMEM((quarter, block, lanes), jnp.float32),
            pltpu.VMEM((n2, block, lanes), jnp.float32),
            pltpu.VMEM((tokens, kv_width), jnp.bfloat16),
            pltpu.VMEM((2, tokens, kv_width), jnp.bfloat16),
            pltpu.VMEM((tokens, kv_width), jnp.float32),
            pltpu.SemaphoreType.DMA((8, max(n1, n2))),
            pltpu.SemaphoreType.DMA((2, 3, 4)),
        ],
        compiler_params=pltpu.CompilerParams(collective_id=collective_id, has_side_effects=True),
    )(rows, w, rk, own_rk, gk, gv)


def shards(
    residual_rows,
    input_norm_weight,
    trial_row_index,
    keyvalue_weight,
    adapter_down_weight,
    adapter_up_weight,
    keyvalue_gradient,
):
    trials = lax.axis_size("trial")
    tensors = lax.axis_size("tensor")
    dps = lax.axis_size("dp")
    tok_dev = trial_row_index.shape[1]
    select = tok_dev // (trials * tensors)
    normed_input = keyvalue_weight.shape[0]
    kv_width = keyvalue_weight.shape[1]
    keyvalue_half = kv_width // 2
    rank_index = adapter_up_weight.shape[1]
    pool_dev = residual_rows.shape[0]
    highest_precision = lax.Precision.HIGHEST

    source = lax.axis_index("trial") * tensors + lax.axis_index("tensor")
    picks = lax.dynamic_slice_in_dim(trial_row_index, source * select, select, 1).reshape(-1)
    onehot = (picks[:, None] == jnp.arange(pool_dev, dtype=jnp.int32)[None, :]).astype(jnp.bfloat16)
    wide = jnp.einsum(
        "tsr,rkf->tksf",
        onehot.reshape(trials, select, pool_dev),
        residual_rows.reshape(pool_dev, tensors, normed_input),
        preferred_element_type=jnp.float32,
    )
    raw = residual_rows.astype(jnp.float32)
    row_scale = lax.rsqrt(jnp.mean(raw * raw, axis=1) + norm_eps)
    picked_scale = jnp.take(row_scale, picks, axis=0)
    gain = input_norm_weight.reshape(1, tensors, 1, normed_input)
    chosen = (wide * picked_scale.reshape(trials, 1, select, 1) * gain).astype(jnp.bfloat16)
    arrived = lax.all_to_all(
        chosen.reshape(trials * tensors, select, normed_input),
        ("trial", "tensor"),
        split_axis=0,
        concat_axis=0,
        tiled=True,
    )
    rows = arrived.reshape(tok_dev, normed_input)

    up_weight = adapter_up_weight[0].astype(jnp.float32)
    grad_in = keyvalue_gradient[0].astype(jnp.float32)
    key_gradient_full = jnp.dot(
        grad_in[:, :keyvalue_half], up_weight[:, :keyvalue_half].T, precision=highest_precision
    )
    value_gradient_full = jnp.dot(
        grad_in[:, keyvalue_half:], up_weight[:, keyvalue_half:].T, precision=highest_precision
    )
    rank_gradient = (
        adapter_scale * jnp.concatenate([key_gradient_full, value_gradient_full], axis=1)
    ).astype(jnp.bfloat16)
    every_rank = lax.all_gather(rank_gradient, "tensor", axis=0, tiled=True)
    grad_a_term = lax.dot_general(
        every_rank, rows, (((0,), (0,)), ((), ())), preferred_element_type=jnp.float32
    )

    down_weight = adapter_down_weight[0]
    ranks = jnp.dot(rows, down_weight, preferred_element_type=jnp.float32)
    block = tok_dev // tensors
    mine = lax.axis_index("tensor") * block
    quarter = dps // 2
    width = kv_width // (dps * tensors)
    grad_t = keyvalue_gradient[0].T.reshape(2, quarter, tensors, width, tok_dev // tensors)
    grad_t = grad_t.transpose(0, 2, 1, 3, 4).reshape(2, keyvalue_half, tok_dev // tensors)
    frozen_output_local, local_rank_rows, up_block = tensor_sum(
        rows,
        keyvalue_weight,
        ranks.reshape(tensors, block, ranks.shape[1]),
        lax.dynamic_slice_in_dim(ranks, mine, block, 0),
        grad_t[0],
        grad_t[1],
        dps,
        0,
    )
    adapter_key = jnp.dot(
        local_rank_rows[:, :rank_index], up_weight[:, :keyvalue_half], precision=highest_precision
    )
    adapter_value = jnp.dot(
        local_rank_rows[:, rank_index:], up_weight[:, keyvalue_half:], precision=highest_precision
    )
    keyvalue_output = frozen_output_local + adapter_scale * jnp.concatenate(
        [adapter_key, adapter_value], axis=1
    )

    grad_a = lax.psum_scatter(grad_a_term, "dp", scatter_dimension=0, tiled=True)

    grad_b = adapter_scale * jnp.where(
        lax.axis_index("dp") < quarter, up_block[:, :rank_index], up_block[:, rank_index:]
    ).T
    return (keyvalue_output[None], grad_a[None], grad_b[None])


def solution(mesh):
    return jax.shard_map(
        shards,
        mesh=mesh,
        in_specs=(
            P(("trial", "dp", "tensor"), None),
            P(),
            P(None, "dp"),
            P("tensor", None),
            P("trial", "tensor", None),
            P("trial", None, None),
            P("trial", ("dp", "tensor"), None),
        ),
        out_specs=(
            P("trial", ("dp", "tensor"), None),
            P("trial", "dp", "tensor"),
            P("trial", None, ("dp", "tensor")),
        ),
        check_vma=False,
    )
```

```python
import functools

import jax
import jax.numpy as jnp
from jax import lax
from jax.experimental import pallas as pl
from jax.experimental.pallas import tpu as pltpu
from jax.sharding import PartitionSpec as P

MESH = pl.DeviceIdType.MESH

adapter_scale = 2.0
norm_eps = 1e-05


def _tensor_sum_kernel(
    n1, n2, rows_ref, w_ref, rk_ref, g_ref,
    kv_out, rk_out, b_out,
    recv_kv, recv_rk, terms, recv_b1, partial, recv_b2, forward, outgoing, across_part, sems, kv_sems,
):
    me1 = lax.axis_index("tensor")
    me2 = lax.axis_index("dp")
    trial = lax.axis_index("trial")
    first = lambda j: (trial, me2, j)
    second = lambda j: (trial, j, me1)
    quarter = n2 // 2
    barrier = pltpu.get_barrier_semaphore()
    for shift in range(1, n1):
        pl.semaphore_signal(barrier, inc=1, device_id=first(lax.rem(me1 + shift, n1)), device_id_type=MESH)
    for shift in range(1, n2):
        pl.semaphore_signal(barrier, inc=1, device_id=second(lax.rem(me2 + shift, n2)), device_id_type=MESH)
    pl.semaphore_wait(barrier, n1 + n2 - 2)

    def send(src_ref, dst_ref, row, shift, device):
        copy = pltpu.make_async_remote_copy(
            src_ref=src_ref,
            dst_ref=dst_ref.at[shift],
            send_sem=sems.at[row, shift],
            recv_sem=sems.at[row + 1, shift],
            device_id=device,
            device_id_type=MESH,
        )
        copy.start()
        return copy

    partner = me1 + 1 - 2 * lax.rem(me1, 2)
    across = lax.rem(me1 + 2, n1)
    diagonal = across + 1 - 2 * lax.rem(across, 2)
    rk_copies = []
    for shift in range(1, n1):
        target = lax.rem(me1 + shift, n1)
        rk_copies.append(send(rk_ref.at[target], recv_rk, 2, shift, first(target)))
    pieces = kv_sems.shape[2]
    step = kv_out.shape[0] // pieces

    def send_piece(src_ref, slot, piece, device):
        rows = pl.ds(piece * step, step)
        copy = pltpu.make_async_remote_copy(
            src_ref=src_ref.at[rows],
            dst_ref=recv_kv.at[slot, rows],
            send_sem=kv_sems.at[0, slot, piece],
            recv_sem=kv_sems.at[1, slot, piece],
            device_id=device,
            device_id_type=MESH,
        )
        copy.start()
        return copy

    tokens = kv_out.shape[0]

    def product(member):
        block = rows_ref[pl.ds(pl.multiple_of(member * tokens, tokens), tokens), :]
        return jnp.dot(block, w_ref[...], preferred_element_type=jnp.float32)

    outgoing[1] = product(diagonal).astype(outgoing.dtype)
    diagonal_copies = [send_piece(outgoing.at[1], 1, p, first(partner)) for p in range(pieces)]
    outgoing[0] = product(partner).astype(outgoing.dtype)
    own_copies = [send_piece(outgoing.at[0], 0, p, first(partner)) for p in range(pieces)]
    across_part[...] = product(across)
    own_part = product(me1)

    rk_out[...] = rk_ref[me1]
    for shift, copy in zip(range(1, n1), rk_copies):
        copy.wait_recv()
        rk_out[...] += recv_rk[shift]

    xa = rk_out[...]
    lane = lax.broadcasted_iota(jnp.int32, xa.shape, 1)
    half = xa.shape[1] // 2
    total = None
    for which, keep in enumerate((lane < half, lane >= half)):
        part = jnp.where(keep, xa, 0.0)
        high = part.astype(jnp.bfloat16)
        low = (part - high.astype(jnp.float32)).astype(jnp.bfloat16)
        g = g_ref[which]
        for piece in (high, low):
            term = jnp.dot(g, piece, preferred_element_type=jnp.float32)
            total = term if total is None else total + term
    terms[...] = total.reshape(terms.shape)

    b1_copies = []
    for shift in range(1, n1):
        target = lax.rem(me1 + shift, n1)
        b1_copies.append(send(terms.at[target], recv_b1, 4, shift, first(target)))

    forward_copies = []
    for p, copy in enumerate(diagonal_copies):
        rows = pl.ds(p * step, step)
        copy.wait_recv()
        forward[rows, :] = (
            across_part[rows, :] + recv_kv[1, rows, :].astype(jnp.float32)
        ).astype(forward.dtype)
        forward_copies.append(send_piece(forward, 2, p, first(across)))
    kv_out[...] = own_part
    for p, copy in enumerate(own_copies):
        rows = pl.ds(p * step, step)
        copy.wait_recv()
        kv_out[rows, :] += recv_kv[0, rows, :].astype(jnp.float32)

    summed = terms[me1]
    for shift, copy in zip(range(1, n1), b1_copies):
        copy.wait_recv()
        summed = summed + recv_b1[shift]
    partial[...] = summed.reshape(partial.shape)

    b2_copies = []
    for shift in range(1, n2):
        target = lax.rem(me2 + shift, n2)
        b2_copies.append(send(partial.at[lax.rem(target, quarter)], recv_b2, 6, shift, second(target)))
    for p, copy in enumerate(forward_copies):
        rows = pl.ds(p * step, step)
        copy.wait_recv()
        kv_out[rows, :] += recv_kv[2, rows, :].astype(jnp.float32)
    b_out[...] = partial[lax.rem(me2, quarter)]
    for shift, copy in zip(range(1, n2), b2_copies):
        copy.wait_recv()
        b_out[...] += recv_b2[shift]

    for copy in rk_copies + diagonal_copies + own_copies + forward_copies + b1_copies + b2_copies:
        copy.wait_send()


def tensor_sum(rows, w, rk, g, n2, collective_id):
    n1 = rk.shape[0]
    tokens = rows.shape[0] // n1
    kv_width = w.shape[1]
    quarter = n2 // 2
    columns = g.shape[1]
    lanes = rk.shape[2]
    block = columns // (n1 * quarter)
    vmem = pl.BlockSpec(memory_space=pltpu.VMEM)
    return pl.pallas_call(
        functools.partial(_tensor_sum_kernel, n1, n2),
        out_shape=(
            jax.ShapeDtypeStruct((tokens, kv_width), jnp.float32),
            jax.ShapeDtypeStruct(rk.shape[1:], jnp.float32),
            jax.ShapeDtypeStruct((block, lanes), jnp.float32),
        ),
        in_specs=[vmem] * 4,
        out_specs=(vmem, vmem, vmem),
        scratch_shapes=[
            pltpu.VMEM((n1, tokens, kv_width), jnp.bfloat16),
            pltpu.VMEM(rk.shape, rk.dtype),
            pltpu.VMEM((n1, quarter * block, lanes), jnp.float32),
            pltpu.VMEM((n1, quarter * block, lanes), jnp.float32),
            pltpu.VMEM((quarter, block, lanes), jnp.float32),
            pltpu.VMEM((n2, block, lanes), jnp.float32),
            pltpu.VMEM((tokens, kv_width), jnp.bfloat16),
            pltpu.VMEM((2, tokens, kv_width), jnp.bfloat16),
            pltpu.VMEM((tokens, kv_width), jnp.float32),
            pltpu.SemaphoreType.DMA((8, max(n1, n2))),
            pltpu.SemaphoreType.DMA((2, 3, 4)),
        ],
        compiler_params=pltpu.CompilerParams(collective_id=collective_id, has_side_effects=True),
    )(rows, w, rk, g)


def shards(
    residual_rows,
    input_norm_weight,
    trial_row_index,
    keyvalue_weight,
    adapter_down_weight,
    adapter_up_weight,
    keyvalue_gradient,
):
    trials = lax.axis_size("trial")
    tensors = lax.axis_size("tensor")
    dps = lax.axis_size("dp")
    tok_dev = trial_row_index.shape[1]
    select = tok_dev // (trials * tensors)
    normed_input = keyvalue_weight.shape[0]
    kv_width = keyvalue_weight.shape[1]
    keyvalue_half = kv_width // 2
    rank_index = adapter_up_weight.shape[1]
    pool_dev = residual_rows.shape[0]
    highest_precision = lax.Precision.HIGHEST

    source = lax.axis_index("trial") * tensors + lax.axis_index("tensor")
    picks = lax.dynamic_slice_in_dim(trial_row_index, source * select, select, 1).reshape(-1)
    onehot = (picks[:, None] == jnp.arange(pool_dev, dtype=jnp.int32)[None, :]).astype(jnp.bfloat16)
    wide = jnp.einsum(
        "tsr,rkf->tksf",
        onehot.reshape(trials, select, pool_dev),
        residual_rows.reshape(pool_dev, tensors, normed_input),
        preferred_element_type=jnp.float32,
    )
    raw = residual_rows.astype(jnp.float32)
    row_scale = lax.rsqrt(jnp.mean(raw * raw, axis=1) + norm_eps)
    picked_scale = jnp.take(row_scale, picks, axis=0)
    gain = input_norm_weight.reshape(1, tensors, 1, normed_input)
    chosen = (wide * picked_scale.reshape(trials, 1, select, 1) * gain).astype(jnp.bfloat16)
    arrived = lax.all_to_all(
        chosen.reshape(trials * tensors, select, normed_input),
        ("trial", "tensor"),
        split_axis=0,
        concat_axis=0,
        tiled=True,
    )
    rows = arrived.reshape(tok_dev, normed_input)

    up_weight = adapter_up_weight[0].astype(jnp.float32)
    grad_in = keyvalue_gradient[0].astype(jnp.float32)
    key_gradient_full = jnp.dot(
        grad_in[:, :keyvalue_half], up_weight[:, :keyvalue_half].T, precision=highest_precision
    )
    value_gradient_full = jnp.dot(
        grad_in[:, keyvalue_half:], up_weight[:, keyvalue_half:].T, precision=highest_precision
    )
    rank_gradient = (
        adapter_scale * jnp.concatenate([key_gradient_full, value_gradient_full], axis=1)
    ).astype(jnp.bfloat16)
    every_rank = lax.all_gather(rank_gradient, "tensor", axis=0, tiled=True)
    grad_a_term = lax.dot_general(
        every_rank, rows, (((0,), (0,)), ((), ())), preferred_element_type=jnp.float32
    )

    down_weight = adapter_down_weight[0]
    ranks = jnp.dot(rows, down_weight, preferred_element_type=jnp.float32)
    block = tok_dev // tensors
    quarter = dps // 2
    width = kv_width // (dps * tensors)
    grad_t = keyvalue_gradient[0].T.reshape(2, quarter, tensors, width, tok_dev // tensors)
    grad_t = grad_t.transpose(0, 2, 1, 3, 4).reshape(2, keyvalue_half, tok_dev // tensors)
    frozen_output_local, local_rank_rows, up_block = tensor_sum(
        rows,
        keyvalue_weight,
        ranks.reshape(tensors, block, ranks.shape[1]),
        grad_t,
        dps,
        0,
    )
    adapter_key = jnp.dot(
        local_rank_rows[:, :rank_index], up_weight[:, :keyvalue_half], precision=highest_precision
    )
    adapter_value = jnp.dot(
        local_rank_rows[:, rank_index:], up_weight[:, keyvalue_half:], precision=highest_precision
    )
    keyvalue_output = frozen_output_local + adapter_scale * jnp.concatenate(
        [adapter_key, adapter_value], axis=1
    )

    grad_a = lax.psum_scatter(grad_a_term, "dp", scatter_dimension=0, tiled=True)

    grad_b = adapter_scale * jnp.where(
        lax.axis_index("dp") < quarter, up_block[:, :rank_index], up_block[:, rank_index:]
    ).T
    return (keyvalue_output[None], grad_a[None], grad_b[None])


def solution(mesh):
    return jax.shard_map(
        shards,
        mesh=mesh,
        in_specs=(
            P(("trial", "dp", "tensor"), None),
            P(),
            P(None, "dp"),
            P("tensor", None),
            P("trial", "tensor", None),
            P("trial", None, None),
            P("trial", ("dp", "tensor"), None),
        ),
        out_specs=(
            P("trial", ("dp", "tensor"), None),
            P("trial", "dp", "tensor"),
            P("trial", None, ("dp", "tensor")),
        ),
        check_vma=False,
    )
```

```python
import functools

import jax
import jax.numpy as jnp
from jax import lax
from jax.experimental import pallas as pl
from jax.experimental.pallas import tpu as pltpu
from jax.sharding import PartitionSpec as P

MESH = pl.DeviceIdType.MESH

adapter_scale = 2.0
norm_eps = 1e-05


def _tensor_sum_kernel(
    n1, n2, rows_ref, w_ref, rk_ref, g_ref,
    kv_out, rk_out, b_out,
    recv_kv, recv_rk, terms, recv_b1, partial, recv_b2, forward, outgoing, across_part, sems, kv_sems,
):
    me1 = lax.axis_index("tensor")
    me2 = lax.axis_index("dp")
    trial = lax.axis_index("trial")
    first = lambda j: (trial, me2, j)
    second = lambda j: (trial, j, me1)
    quarter = n2 // 2
    barrier = pltpu.get_barrier_semaphore()
    for shift in range(1, n1):
        pl.semaphore_signal(barrier, inc=1, device_id=first(lax.rem(me1 + shift, n1)), device_id_type=MESH)
    for shift in range(1, n2):
        pl.semaphore_signal(barrier, inc=1, device_id=second(lax.rem(me2 + shift, n2)), device_id_type=MESH)
    pl.semaphore_wait(barrier, n1 + n2 - 2)

    def send(src_ref, dst_ref, row, shift, device):
        copy = pltpu.make_async_remote_copy(
            src_ref=src_ref,
            dst_ref=dst_ref.at[shift],
            send_sem=sems.at[row, shift],
            recv_sem=sems.at[row + 1, shift],
            device_id=device,
            device_id_type=MESH,
        )
        copy.start()
        return copy

    partner = me1 + 1 - 2 * lax.rem(me1, 2)
    across = lax.rem(me1 + 2, n1)
    diagonal = across + 1 - 2 * lax.rem(across, 2)
    rk_copies = []
    for shift in range(1, n1):
        target = lax.rem(me1 + shift, n1)
        rk_copies.append(send(rk_ref.at[target], recv_rk, 2, shift, first(target)))
    pieces = kv_sems.shape[2]
    step = kv_out.shape[0] // pieces

    def send_piece(src_ref, slot, piece, device):
        rows = pl.ds(piece * step, step)
        copy = pltpu.make_async_remote_copy(
            src_ref=src_ref.at[rows],
            dst_ref=recv_kv.at[slot, rows],
            send_sem=kv_sems.at[0, slot, piece],
            recv_sem=kv_sems.at[1, slot, piece],
            device_id=device,
            device_id_type=MESH,
        )
        copy.start()
        return copy

    tokens = kv_out.shape[0]

    def product(member):
        block = rows_ref[pl.ds(pl.multiple_of(member * tokens, tokens), tokens), :]
        return jnp.dot(block, w_ref[...], preferred_element_type=jnp.float32)

    outgoing[1] = product(diagonal).astype(outgoing.dtype)
    diagonal_copies = [send_piece(outgoing.at[1], 1, p, first(partner)) for p in range(pieces)]
    outgoing[0] = product(partner).astype(outgoing.dtype)
    own_copies = [send_piece(outgoing.at[0], 0, p, first(partner)) for p in range(pieces)]
    across_part[...] = product(across)
    own_part = product(me1)

    rk_out[...] = rk_ref[me1]
    for shift, copy in zip(range(1, n1), rk_copies):
        copy.wait_recv()
        rk_out[...] += recv_rk[shift]

    xa = rk_out[...]
    lane = lax.broadcasted_iota(jnp.int32, xa.shape, 1)
    half = xa.shape[1] // 2
    total = None
    for which, keep in enumerate((lane < half, lane >= half)):
        part = jnp.where(keep, xa, 0.0)
        high = part.astype(jnp.bfloat16)
        low = (part - high.astype(jnp.float32)).astype(jnp.bfloat16)
        g = g_ref[which]
        for piece in (high, low):
            term = jnp.dot(g, piece, preferred_element_type=jnp.float32)
            total = term if total is None else total + term
    terms[...] = total.reshape(terms.shape)

    b1_copies = []
    for shift in range(1, n1):
        target = lax.rem(me1 + shift, n1)
        b1_copies.append(send(terms.at[target], recv_b1, 4, shift, first(target)))

    forward_copies = []
    for p, copy in enumerate(diagonal_copies):
        rows = pl.ds(p * step, step)
        copy.wait_recv()
        forward[rows, :] = (
            across_part[rows, :] + recv_kv[1, rows, :].astype(jnp.float32)
        ).astype(forward.dtype)
        forward_copies.append(send_piece(forward, 2, p, first(across)))
    kv_out[...] = own_part
    for p, copy in enumerate(own_copies):
        rows = pl.ds(p * step, step)
        copy.wait_recv()
        kv_out[rows, :] += recv_kv[0, rows, :].astype(jnp.float32)

    summed = terms[me1]
    for shift, copy in zip(range(1, n1), b1_copies):
        copy.wait_recv()
        summed = summed + recv_b1[shift]
    partial[...] = summed.reshape(partial.shape)

    b2_copies = []
    for shift in range(1, n2):
        target = lax.rem(me2 + shift, n2)
        b2_copies.append(send(partial.at[lax.rem(target, quarter)], recv_b2, 6, shift, second(target)))
    for p, copy in enumerate(forward_copies):
        rows = pl.ds(p * step, step)
        copy.wait_recv()
        kv_out[rows, :] += recv_kv[2, rows, :].astype(jnp.float32)
    reduced = partial[lax.rem(me2, quarter)]
    for shift, copy in zip(range(1, n2), b2_copies):
        copy.wait_recv()
        reduced = reduced + recv_b2[shift]
    by_rank = reduced.T
    ranks_here = b_out.shape[0]
    b_out[...] = adapter_scale * jnp.where(
        me2 < quarter, by_rank[:ranks_here, :], by_rank[ranks_here:, :]
    )

    for copy in rk_copies + diagonal_copies + own_copies + forward_copies + b1_copies + b2_copies:
        copy.wait_send()


def tensor_sum(rows, w, rk, g, n2, collective_id):
    n1 = rk.shape[0]
    tokens = rows.shape[0] // n1
    kv_width = w.shape[1]
    quarter = n2 // 2
    columns = g.shape[1]
    lanes = rk.shape[2]
    block = columns // (n1 * quarter)
    vmem = pl.BlockSpec(memory_space=pltpu.VMEM)
    return pl.pallas_call(
        functools.partial(_tensor_sum_kernel, n1, n2),
        out_shape=(
            jax.ShapeDtypeStruct((tokens, kv_width), jnp.float32),
            jax.ShapeDtypeStruct(rk.shape[1:], jnp.float32),
            jax.ShapeDtypeStruct((lanes // 2, block), jnp.float32),
        ),
        in_specs=[vmem] * 4,
        out_specs=(vmem, vmem, vmem),
        scratch_shapes=[
            pltpu.VMEM((n1, tokens, kv_width), jnp.bfloat16),
            pltpu.VMEM(rk.shape, rk.dtype),
            pltpu.VMEM((n1, quarter * block, lanes), jnp.float32),
            pltpu.VMEM((n1, quarter * block, lanes), jnp.float32),
            pltpu.VMEM((quarter, block, lanes), jnp.float32),
            pltpu.VMEM((n2, block, lanes), jnp.float32),
            pltpu.VMEM((tokens, kv_width), jnp.bfloat16),
            pltpu.VMEM((2, tokens, kv_width), jnp.bfloat16),
            pltpu.VMEM((tokens, kv_width), jnp.float32),
            pltpu.SemaphoreType.DMA((8, max(n1, n2))),
            pltpu.SemaphoreType.DMA((2, 3, 4)),
        ],
        compiler_params=pltpu.CompilerParams(collective_id=collective_id, has_side_effects=True),
    )(rows, w, rk, g)


def shards(
    residual_rows,
    input_norm_weight,
    trial_row_index,
    keyvalue_weight,
    adapter_down_weight,
    adapter_up_weight,
    keyvalue_gradient,
):
    trials = lax.axis_size("trial")
    tensors = lax.axis_size("tensor")
    dps = lax.axis_size("dp")
    tok_dev = trial_row_index.shape[1]
    select = tok_dev // (trials * tensors)
    normed_input = keyvalue_weight.shape[0]
    kv_width = keyvalue_weight.shape[1]
    keyvalue_half = kv_width // 2
    rank_index = adapter_up_weight.shape[1]
    pool_dev = residual_rows.shape[0]
    highest_precision = lax.Precision.HIGHEST

    source = lax.axis_index("trial") * tensors + lax.axis_index("tensor")
    picks = lax.dynamic_slice_in_dim(trial_row_index, source * select, select, 1).reshape(-1)
    onehot = (picks[:, None] == jnp.arange(pool_dev, dtype=jnp.int32)[None, :]).astype(jnp.bfloat16)
    wide = jnp.einsum(
        "tsr,rkf->tksf",
        onehot.reshape(trials, select, pool_dev),
        residual_rows.reshape(pool_dev, tensors, normed_input),
        preferred_element_type=jnp.float32,
    )
    raw = residual_rows.astype(jnp.float32)
    row_scale = lax.rsqrt(jnp.mean(raw * raw, axis=1) + norm_eps)
    picked_scale = jnp.take(row_scale, picks, axis=0)
    gain = input_norm_weight.reshape(1, tensors, 1, normed_input)
    chosen = (wide * picked_scale.reshape(trials, 1, select, 1) * gain).astype(jnp.bfloat16)
    arrived = lax.all_to_all(
        chosen.reshape(trials * tensors, select, normed_input),
        ("trial", "tensor"),
        split_axis=0,
        concat_axis=0,
        tiled=True,
    )
    rows = arrived.reshape(tok_dev, normed_input)

    up_weight = adapter_up_weight[0].astype(jnp.float32)
    grad_in = keyvalue_gradient[0].astype(jnp.float32)
    key_gradient_full = jnp.dot(
        grad_in[:, :keyvalue_half], up_weight[:, :keyvalue_half].T, precision=highest_precision
    )
    value_gradient_full = jnp.dot(
        grad_in[:, keyvalue_half:], up_weight[:, keyvalue_half:].T, precision=highest_precision
    )
    rank_gradient = (
        adapter_scale * jnp.concatenate([key_gradient_full, value_gradient_full], axis=1)
    ).astype(jnp.bfloat16)
    every_rank = lax.all_gather(rank_gradient, "tensor", axis=0, tiled=True)
    grad_a_term = lax.dot_general(
        every_rank, rows, (((0,), (0,)), ((), ())), preferred_element_type=jnp.float32
    )

    down_weight = adapter_down_weight[0]
    ranks = jnp.dot(rows, down_weight, preferred_element_type=jnp.float32)
    block = tok_dev // tensors
    quarter = dps // 2
    width = kv_width // (dps * tensors)
    grad_t = keyvalue_gradient[0].T.reshape(2, quarter, tensors, width, tok_dev // tensors)
    grad_t = grad_t.transpose(0, 2, 1, 3, 4).reshape(2, keyvalue_half, tok_dev // tensors)
    frozen_output_local, local_rank_rows, up_block = tensor_sum(
        rows,
        keyvalue_weight,
        ranks.reshape(tensors, block, ranks.shape[1]),
        grad_t,
        dps,
        0,
    )
    adapter_key = jnp.dot(
        local_rank_rows[:, :rank_index], up_weight[:, :keyvalue_half], precision=highest_precision
    )
    adapter_value = jnp.dot(
        local_rank_rows[:, rank_index:], up_weight[:, keyvalue_half:], precision=highest_precision
    )
    keyvalue_output = frozen_output_local + adapter_scale * jnp.concatenate(
        [adapter_key, adapter_value], axis=1
    )

    grad_a = lax.psum_scatter(grad_a_term, "dp", scatter_dimension=0, tiled=True)

    grad_b = up_block
    return (keyvalue_output[None], grad_a[None], grad_b[None])


def solution(mesh):
    return jax.shard_map(
        shards,
        mesh=mesh,
        in_specs=(
            P(("trial", "dp", "tensor"), None),
            P(),
            P(None, "dp"),
            P("tensor", None),
            P("trial", "tensor", None),
            P("trial", None, None),
            P("trial", ("dp", "tensor"), None),
        ),
        out_specs=(
            P("trial", ("dp", "tensor"), None),
            P("trial", "dp", "tensor"),
            P("trial", None, ("dp", "tensor")),
        ),
        check_vma=False,
    )
```

```python
import functools

import jax
import jax.numpy as jnp
from jax import lax
from jax.experimental import pallas as pl
from jax.experimental.pallas import tpu as pltpu
from jax.sharding import PartitionSpec as P

MESH = pl.DeviceIdType.MESH

adapter_scale = 2.0
norm_eps = 1e-05


def _tensor_sum_kernel(
    n1, n2, rows_ref, w_ref, rk_ref, g_ref,
    kv_out, rk_out, b_out,
    recv_kv, recv_rk, terms, recv_b1, partial, recv_b2, forward, outgoing, across_part, sems, kv_sems,
):
    me1 = lax.axis_index("tensor")
    me2 = lax.axis_index("dp")
    trial = lax.axis_index("trial")
    first = lambda j: (trial, me2, j)
    second = lambda j: (trial, j, me1)
    quarter = n2 // 2
    barrier = pltpu.get_barrier_semaphore()
    for shift in range(1, n1):
        pl.semaphore_signal(barrier, inc=1, device_id=first(lax.rem(me1 + shift, n1)), device_id_type=MESH)
    for shift in range(1, n2):
        pl.semaphore_signal(barrier, inc=1, device_id=second(lax.rem(me2 + shift, n2)), device_id_type=MESH)
    pl.semaphore_wait(barrier, n1 + n2 - 2)

    def send(src_ref, dst_ref, row, shift, device):
        copy = pltpu.make_async_remote_copy(
            src_ref=src_ref,
            dst_ref=dst_ref.at[shift],
            send_sem=sems.at[row, shift],
            recv_sem=sems.at[row + 1, shift],
            device_id=device,
            device_id_type=MESH,
        )
        copy.start()
        return copy

    partner = me1 + 1 - 2 * lax.rem(me1, 2)
    across = lax.rem(me1 + 2, n1)
    diagonal = across + 1 - 2 * lax.rem(across, 2)
    rk_copies = []
    for shift in range(1, n1):
        target = lax.rem(me1 + shift, n1)
        rk_copies.append(send(rk_ref.at[target], recv_rk, 2, shift, first(target)))
    pieces = kv_sems.shape[2]
    step = kv_out.shape[0] // pieces

    def send_piece(src_ref, slot, piece, device):
        rows = pl.ds(piece * step, step)
        copy = pltpu.make_async_remote_copy(
            src_ref=src_ref.at[rows],
            dst_ref=recv_kv.at[slot, rows],
            send_sem=kv_sems.at[0, slot, piece],
            recv_sem=kv_sems.at[1, slot, piece],
            device_id=device,
            device_id_type=MESH,
        )
        copy.start()
        return copy

    tokens = kv_out.shape[0]

    def product(member):
        block = rows_ref[pl.ds(pl.multiple_of(member * tokens, tokens), tokens), :]
        return jnp.dot(block, w_ref[...], preferred_element_type=jnp.float32)

    outgoing[1] = product(diagonal).astype(outgoing.dtype)
    diagonal_copies = [send_piece(outgoing.at[1], 1, p, first(partner)) for p in range(pieces)]
    outgoing[0] = product(partner).astype(outgoing.dtype)
    own_copies = [send_piece(outgoing.at[0], 0, p, first(partner)) for p in range(pieces)]
    across_part[...] = product(across)
    own_part = product(me1)

    rk_out[...] = rk_ref[me1]
    for shift, copy in zip(range(1, n1), rk_copies):
        copy.wait_recv()
        rk_out[...] += recv_rk[shift]

    xa = rk_out[...]
    lane = lax.broadcasted_iota(jnp.int32, xa.shape, 1)
    half = xa.shape[1] // 2
    total = None
    for which, keep in enumerate((lane < half, lane >= half)):
        part = jnp.where(keep, xa, 0.0)
        high = part.astype(jnp.bfloat16)
        low = (part - high.astype(jnp.float32)).astype(jnp.bfloat16)
        g = g_ref[which]
        for piece in (high, low):
            term = jnp.dot(g, piece, preferred_element_type=jnp.float32)
            total = term if total is None else total + term
    terms[...] = total.reshape(terms.shape)

    b1_copies = []
    for shift in range(1, n1):
        target = lax.rem(me1 + shift, n1)
        b1_copies.append(send(terms.at[target], recv_b1, 4, shift, first(target)))

    forward_copies = []
    for p, copy in enumerate(diagonal_copies):
        rows = pl.ds(p * step, step)
        copy.wait_recv()
        forward[rows, :] = (
            across_part[rows, :] + recv_kv[1, rows, :].astype(jnp.float32)
        ).astype(forward.dtype)
        forward_copies.append(send_piece(forward, 2, p, first(across)))
    kv_out[...] = own_part
    for p, copy in enumerate(own_copies):
        rows = pl.ds(p * step, step)
        copy.wait_recv()
        kv_out[rows, :] += recv_kv[0, rows, :].astype(jnp.float32)

    summed = terms[me1]
    for shift, copy in zip(range(1, n1), b1_copies):
        copy.wait_recv()
        summed = summed + recv_b1[shift]
    partial[...] = summed.reshape(partial.shape)

    b2_copies = []
    for shift in range(1, n2):
        target = lax.rem(me2 + shift, n2)
        b2_copies.append(send(partial.at[lax.rem(target, quarter)], recv_b2, 6, shift, second(target)))
    for p, copy in enumerate(forward_copies):
        rows = pl.ds(p * step, step)
        copy.wait_recv()
        kv_out[rows, :] += recv_kv[2, rows, :].astype(jnp.float32)
    reduced = partial[lax.rem(me2, quarter)]
    for shift, copy in zip(range(1, n2), b2_copies):
        copy.wait_recv()
        reduced = reduced + recv_b2[shift]
    by_rank = reduced.T
    ranks_here = b_out.shape[0]
    b_out[...] = adapter_scale * jnp.where(
        me2 < quarter, by_rank[:ranks_here, :], by_rank[ranks_here:, :]
    )

    for copy in rk_copies + diagonal_copies + own_copies + forward_copies + b1_copies + b2_copies:
        copy.wait_send()


def tensor_sum(rows, w, rk, g, n2, collective_id):
    n1 = rk.shape[0]
    tokens = rows.shape[0] // n1
    kv_width = w.shape[1]
    quarter = n2 // 2
    columns = g.shape[1]
    lanes = rk.shape[2]
    block = columns // (n1 * quarter)
    vmem = pl.BlockSpec(memory_space=pltpu.VMEM)
    return pl.pallas_call(
        functools.partial(_tensor_sum_kernel, n1, n2),
        out_shape=(
            jax.ShapeDtypeStruct((tokens, kv_width), jnp.float32),
            jax.ShapeDtypeStruct(rk.shape[1:], jnp.float32),
            jax.ShapeDtypeStruct((lanes // 2, block), jnp.float32),
        ),
        in_specs=[vmem] * 4,
        out_specs=(vmem, vmem, vmem),
        scratch_shapes=[
            pltpu.VMEM((n1, tokens, kv_width), jnp.bfloat16),
            pltpu.VMEM(rk.shape, rk.dtype),
            pltpu.VMEM((n1, quarter * block, lanes), jnp.float32),
            pltpu.VMEM((n1, quarter * block, lanes), jnp.float32),
            pltpu.VMEM((quarter, block, lanes), jnp.float32),
            pltpu.VMEM((n2, block, lanes), jnp.float32),
            pltpu.VMEM((tokens, kv_width), jnp.bfloat16),
            pltpu.VMEM((2, tokens, kv_width), jnp.bfloat16),
            pltpu.VMEM((tokens, kv_width), jnp.float32),
            pltpu.SemaphoreType.DMA((8, max(n1, n2))),
            pltpu.SemaphoreType.DMA((2, 3, 4)),
        ],
        compiler_params=pltpu.CompilerParams(collective_id=collective_id, has_side_effects=True),
    )(rows, w, rk, g)


def shards(
    residual_rows,
    input_norm_weight,
    trial_row_index,
    keyvalue_weight,
    adapter_down_weight,
    adapter_up_weight,
    keyvalue_gradient,
):
    trials = lax.axis_size("trial")
    tensors = lax.axis_size("tensor")
    dps = lax.axis_size("dp")
    tok_dev = trial_row_index.shape[1]
    select = tok_dev // (trials * tensors)
    normed_input = keyvalue_weight.shape[0]
    kv_width = keyvalue_weight.shape[1]
    keyvalue_half = kv_width // 2
    rank_index = adapter_up_weight.shape[1]
    pool_dev = residual_rows.shape[0]
    highest_precision = lax.Precision.HIGHEST

    source = lax.axis_index("trial") * tensors + lax.axis_index("tensor")
    picks = lax.dynamic_slice_in_dim(trial_row_index, source * select, select, 1).reshape(-1)
    onehot = (picks[:, None] == jnp.arange(pool_dev, dtype=jnp.int32)[None, :]).astype(jnp.bfloat16)
    wide = jnp.einsum(
        "tsr,rkf->tksf",
        onehot.reshape(trials, select, pool_dev),
        residual_rows.reshape(pool_dev, tensors, normed_input),
        preferred_element_type=jnp.float32,
    )
    raw = residual_rows.astype(jnp.float32)
    row_scale = lax.rsqrt(jnp.mean(raw * raw, axis=1) + norm_eps)
    picked_scale = jnp.take(row_scale, picks, axis=0)
    gain = input_norm_weight.reshape(1, tensors, 1, normed_input)
    chosen = (wide * picked_scale.reshape(trials, 1, select, 1) * gain).astype(jnp.bfloat16)
    arrived = lax.all_to_all(
        chosen.reshape(trials * tensors, select, normed_input),
        ("trial", "tensor"),
        split_axis=0,
        concat_axis=0,
        tiled=True,
    )
    rows = arrived.reshape(tok_dev, normed_input)

    up_weight = adapter_up_weight[0].astype(jnp.float32)
    grad_in = keyvalue_gradient[0].astype(jnp.float32)
    key_gradient_full = jnp.dot(
        grad_in[:, :keyvalue_half], up_weight[:, :keyvalue_half].T, precision=highest_precision
    )
    value_gradient_full = jnp.dot(
        grad_in[:, keyvalue_half:], up_weight[:, keyvalue_half:].T, precision=highest_precision
    )
    rank_gradient = (
        adapter_scale * jnp.concatenate([key_gradient_full, value_gradient_full], axis=1)
    ).astype(jnp.bfloat16)
    every_rank = lax.all_gather(rank_gradient, "tensor", axis=0, tiled=True)
    grad_a_term = lax.dot_general(
        every_rank, rows, (((0,), (0,)), ((), ())), preferred_element_type=jnp.float32
    )

    down_weight = adapter_down_weight[0]
    ranks = jnp.dot(rows, down_weight, preferred_element_type=jnp.float32)
    block = tok_dev // tensors
    quarter = dps // 2
    width = kv_width // (dps * tensors)
    grad_t = keyvalue_gradient[0].T.reshape(2, quarter, tensors, width, tok_dev // tensors)
    grad_t = grad_t.transpose(0, 2, 1, 3, 4).reshape(2, keyvalue_half, tok_dev // tensors)
    frozen_output_local, local_rank_rows, up_block = tensor_sum(
        rows,
        keyvalue_weight,
        ranks.reshape(tensors, block, ranks.shape[1]),
        grad_t,
        dps,
        0,
    )
    block_up = jnp.zeros((2 * rank_index, kv_width), jnp.float32)
    block_up = block_up.at[:rank_index, :keyvalue_half].set(up_weight[:, :keyvalue_half])
    block_up = block_up.at[rank_index:, keyvalue_half:].set(up_weight[:, keyvalue_half:])
    keyvalue_output = frozen_output_local + adapter_scale * jnp.dot(
        local_rank_rows, block_up, precision=highest_precision
    )

    grad_a = lax.psum_scatter(grad_a_term, "dp", scatter_dimension=0, tiled=True)

    grad_b = up_block
    return (keyvalue_output[None], grad_a[None], grad_b[None])


def solution(mesh):
    return jax.shard_map(
        shards,
        mesh=mesh,
        in_specs=(
            P(("trial", "dp", "tensor"), None),
            P(),
            P(None, "dp"),
            P("tensor", None),
            P("trial", "tensor", None),
            P("trial", None, None),
            P("trial", ("dp", "tensor"), None),
        ),
        out_specs=(
            P("trial", ("dp", "tensor"), None),
            P("trial", "dp", "tensor"),
            P("trial", None, ("dp", "tensor")),
        ),
        check_vma=False,
    )
```

```python
import functools

import jax
import jax.numpy as jnp
from jax import lax
from jax.experimental import pallas as pl
from jax.experimental.pallas import tpu as pltpu
from jax.sharding import PartitionSpec as P

MESH = pl.DeviceIdType.MESH

adapter_scale = 2.0
norm_eps = 1e-05


def _tensor_sum_kernel(
    n1, n2, rows_ref, w_ref, dw_ref, g_ref,
    kv_out, rk_out, b_out,
    recv_kv, recv_rk, terms, recv_b1, partial, recv_b2, forward, outgoing, across_part, rk_ref, sems, kv_sems,
):
    me1 = lax.axis_index("tensor")
    me2 = lax.axis_index("dp")
    trial = lax.axis_index("trial")
    first = lambda j: (trial, me2, j)
    second = lambda j: (trial, j, me1)
    quarter = n2 // 2
    barrier = pltpu.get_barrier_semaphore()
    for shift in range(1, n1):
        pl.semaphore_signal(barrier, inc=1, device_id=first(lax.rem(me1 + shift, n1)), device_id_type=MESH)
    for shift in range(1, n2):
        pl.semaphore_signal(barrier, inc=1, device_id=second(lax.rem(me2 + shift, n2)), device_id_type=MESH)
    rk_ref[...] = jnp.dot(rows_ref[...], dw_ref[...], preferred_element_type=jnp.float32).reshape(rk_ref.shape)
    pl.semaphore_wait(barrier, n1 + n2 - 2)

    def send(src_ref, dst_ref, row, shift, device):
        copy = pltpu.make_async_remote_copy(
            src_ref=src_ref,
            dst_ref=dst_ref.at[shift],
            send_sem=sems.at[row, shift],
            recv_sem=sems.at[row + 1, shift],
            device_id=device,
            device_id_type=MESH,
        )
        copy.start()
        return copy

    partner = me1 + 1 - 2 * lax.rem(me1, 2)
    across = lax.rem(me1 + 2, n1)
    diagonal = across + 1 - 2 * lax.rem(across, 2)
    rk_copies = []
    for shift in range(1, n1):
        target = lax.rem(me1 + shift, n1)
        rk_copies.append(send(rk_ref.at[target], recv_rk, 2, shift, first(target)))
    pieces = kv_sems.shape[2]
    step = kv_out.shape[0] // pieces

    def send_piece(src_ref, slot, piece, device):
        rows = pl.ds(piece * step, step)
        copy = pltpu.make_async_remote_copy(
            src_ref=src_ref.at[rows],
            dst_ref=recv_kv.at[slot, rows],
            send_sem=kv_sems.at[0, slot, piece],
            recv_sem=kv_sems.at[1, slot, piece],
            device_id=device,
            device_id_type=MESH,
        )
        copy.start()
        return copy

    tokens = kv_out.shape[0]

    def product(member):
        block = rows_ref[pl.ds(pl.multiple_of(member * tokens, tokens), tokens), :]
        return jnp.dot(block, w_ref[...], preferred_element_type=jnp.float32)

    outgoing[1] = product(diagonal).astype(outgoing.dtype)
    diagonal_copies = [send_piece(outgoing.at[1], 1, p, first(partner)) for p in range(pieces)]
    outgoing[0] = product(partner).astype(outgoing.dtype)
    own_copies = [send_piece(outgoing.at[0], 0, p, first(partner)) for p in range(pieces)]
    across_part[...] = product(across)
    own_part = product(me1)

    rk_out[...] = rk_ref[me1]
    for shift, copy in zip(range(1, n1), rk_copies):
        copy.wait_recv()
        rk_out[...] += recv_rk[shift]

    xa = rk_out[...]
    lane = lax.broadcasted_iota(jnp.int32, xa.shape, 1)
    half = xa.shape[1] // 2
    total = None
    for which, keep in enumerate((lane < half, lane >= half)):
        part = jnp.where(keep, xa, 0.0)
        high = part.astype(jnp.bfloat16)
        low = (part - high.astype(jnp.float32)).astype(jnp.bfloat16)
        g = g_ref[which]
        for piece in (high, low):
            term = jnp.dot(g, piece, preferred_element_type=jnp.float32)
            total = term if total is None else total + term
    terms[...] = total.reshape(terms.shape)

    b1_copies = []
    for shift in range(1, n1):
        target = lax.rem(me1 + shift, n1)
        b1_copies.append(send(terms.at[target], recv_b1, 4, shift, first(target)))

    forward_copies = []
    for p, copy in enumerate(diagonal_copies):
        rows = pl.ds(p * step, step)
        copy.wait_recv()
        forward[rows, :] = (
            across_part[rows, :] + recv_kv[1, rows, :].astype(jnp.float32)
        ).astype(forward.dtype)
        forward_copies.append(send_piece(forward, 2, p, first(across)))
    kv_out[...] = own_part
    for p, copy in enumerate(own_copies):
        rows = pl.ds(p * step, step)
        copy.wait_recv()
        kv_out[rows, :] += recv_kv[0, rows, :].astype(jnp.float32)

    summed = terms[me1]
    for shift, copy in zip(range(1, n1), b1_copies):
        copy.wait_recv()
        summed = summed + recv_b1[shift]
    partial[...] = summed.reshape(partial.shape)

    b2_copies = []
    for shift in range(1, n2):
        target = lax.rem(me2 + shift, n2)
        b2_copies.append(send(partial.at[lax.rem(target, quarter)], recv_b2, 6, shift, second(target)))
    for p, copy in enumerate(forward_copies):
        rows = pl.ds(p * step, step)
        copy.wait_recv()
        kv_out[rows, :] += recv_kv[2, rows, :].astype(jnp.float32)
    reduced = partial[lax.rem(me2, quarter)]
    for shift, copy in zip(range(1, n2), b2_copies):
        copy.wait_recv()
        reduced = reduced + recv_b2[shift]
    by_rank = reduced.T
    ranks_here = b_out.shape[0]
    b_out[...] = adapter_scale * jnp.where(
        me2 < quarter, by_rank[:ranks_here, :], by_rank[ranks_here:, :]
    )

    for copy in rk_copies + diagonal_copies + own_copies + forward_copies + b1_copies + b2_copies:
        copy.wait_send()


def tensor_sum(rows, w, dw, g, n1, n2, collective_id):
    tokens = rows.shape[0] // n1
    kv_width = w.shape[1]
    quarter = n2 // 2
    columns = g.shape[1]
    lanes = dw.shape[1]
    block = columns // (n1 * quarter)
    vmem = pl.BlockSpec(memory_space=pltpu.VMEM)
    return pl.pallas_call(
        functools.partial(_tensor_sum_kernel, n1, n2),
        out_shape=(
            jax.ShapeDtypeStruct((tokens, kv_width), jnp.float32),
            jax.ShapeDtypeStruct((tokens, lanes), jnp.float32),
            jax.ShapeDtypeStruct((lanes // 2, block), jnp.float32),
        ),
        in_specs=[vmem] * 4,
        out_specs=(vmem, vmem, vmem),
        scratch_shapes=[
            pltpu.VMEM((n1, tokens, kv_width), jnp.bfloat16),
            pltpu.VMEM((n1, tokens, lanes), jnp.float32),
            pltpu.VMEM((n1, quarter * block, lanes), jnp.float32),
            pltpu.VMEM((n1, quarter * block, lanes), jnp.float32),
            pltpu.VMEM((quarter, block, lanes), jnp.float32),
            pltpu.VMEM((n2, block, lanes), jnp.float32),
            pltpu.VMEM((tokens, kv_width), jnp.bfloat16),
            pltpu.VMEM((2, tokens, kv_width), jnp.bfloat16),
            pltpu.VMEM((tokens, kv_width), jnp.float32),
            pltpu.VMEM((n1, tokens, lanes), jnp.float32),
            pltpu.SemaphoreType.DMA((8, max(n1, n2))),
            pltpu.SemaphoreType.DMA((2, 3, 4)),
        ],
        compiler_params=pltpu.CompilerParams(collective_id=collective_id, has_side_effects=True),
    )(rows, w, dw, g)


def shards(
    residual_rows,
    input_norm_weight,
    trial_row_index,
    keyvalue_weight,
    adapter_down_weight,
    adapter_up_weight,
    keyvalue_gradient,
):
    trials = lax.axis_size("trial")
    tensors = lax.axis_size("tensor")
    dps = lax.axis_size("dp")
    tok_dev = trial_row_index.shape[1]
    select = tok_dev // (trials * tensors)
    normed_input = keyvalue_weight.shape[0]
    kv_width = keyvalue_weight.shape[1]
    keyvalue_half = kv_width // 2
    rank_index = adapter_up_weight.shape[1]
    pool_dev = residual_rows.shape[0]
    highest_precision = lax.Precision.HIGHEST

    source = lax.axis_index("trial") * tensors + lax.axis_index("tensor")
    picks = lax.dynamic_slice_in_dim(trial_row_index, source * select, select, 1).reshape(-1)
    onehot = (picks[:, None] == jnp.arange(pool_dev, dtype=jnp.int32)[None, :]).astype(jnp.bfloat16)
    wide = jnp.einsum(
        "tsr,rkf->tksf",
        onehot.reshape(trials, select, pool_dev),
        residual_rows.reshape(pool_dev, tensors, normed_input),
        preferred_element_type=jnp.float32,
    )
    raw = residual_rows.astype(jnp.float32)
    row_scale = lax.rsqrt(jnp.mean(raw * raw, axis=1) + norm_eps)
    picked_scale = jnp.take(row_scale, picks, axis=0)
    gain = input_norm_weight.reshape(1, tensors, 1, normed_input)
    chosen = (wide * picked_scale.reshape(trials, 1, select, 1) * gain).astype(jnp.bfloat16)
    arrived = lax.all_to_all(
        chosen.reshape(trials * tensors, select, normed_input),
        ("trial", "tensor"),
        split_axis=0,
        concat_axis=0,
        tiled=True,
    )
    rows = arrived.reshape(tok_dev, normed_input)

    up_weight = adapter_up_weight[0].astype(jnp.float32)
    grad_in = keyvalue_gradient[0].astype(jnp.float32)
    key_gradient_full = jnp.dot(
        grad_in[:, :keyvalue_half], up_weight[:, :keyvalue_half].T, precision=highest_precision
    )
    value_gradient_full = jnp.dot(
        grad_in[:, keyvalue_half:], up_weight[:, keyvalue_half:].T, precision=highest_precision
    )
    rank_gradient = (
        adapter_scale * jnp.concatenate([key_gradient_full, value_gradient_full], axis=1)
    ).astype(jnp.bfloat16)
    quarter = dps // 2
    width = kv_width // (dps * tensors)
    grad_t = keyvalue_gradient[0].T.reshape(2, quarter, tensors, width, tok_dev // tensors)
    grad_t = grad_t.transpose(0, 2, 1, 3, 4).reshape(2, keyvalue_half, tok_dev // tensors)
    grad_t, rank_gradient = lax.optimization_barrier((grad_t, rank_gradient))
    every_rank = lax.all_gather(rank_gradient, "tensor", axis=0, tiled=True)
    grad_a_term = lax.dot_general(
        every_rank, rows, (((0,), (0,)), ((), ())), preferred_element_type=jnp.float32
    )

    frozen_output_local, local_rank_rows, up_block = tensor_sum(
        rows,
        keyvalue_weight,
        adapter_down_weight[0],
        grad_t,
        tensors,
        dps,
        0,
    )
    adapter_key = jnp.dot(
        local_rank_rows[:, :rank_index], up_weight[:, :keyvalue_half], precision=highest_precision
    )
    adapter_value = jnp.dot(
        local_rank_rows[:, rank_index:], up_weight[:, keyvalue_half:], precision=highest_precision
    )
    keyvalue_output = frozen_output_local + adapter_scale * jnp.concatenate(
        [adapter_key, adapter_value], axis=1
    )

    grad_a = lax.psum_scatter(grad_a_term, "dp", scatter_dimension=0, tiled=True)

    grad_b = up_block
    return (keyvalue_output[None], grad_a[None], grad_b[None])


def solution(mesh):
    return jax.shard_map(
        shards,
        mesh=mesh,
        in_specs=(
            P(("trial", "dp", "tensor"), None),
            P(),
            P(None, "dp"),
            P("tensor", None),
            P("trial", "tensor", None),
            P("trial", None, None),
            P("trial", ("dp", "tensor"), None),
        ),
        out_specs=(
            P("trial", ("dp", "tensor"), None),
            P("trial", "dp", "tensor"),
            P("trial", None, ("dp", "tensor")),
        ),
        check_vma=False,
    )
```

```python
import functools

import jax
import jax.numpy as jnp
from jax import lax
from jax.experimental import pallas as pl
from jax.experimental.pallas import tpu as pltpu
from jax.sharding import PartitionSpec as P

MESH = pl.DeviceIdType.MESH

adapter_scale = 2.0
norm_eps = 1e-05


def _tensor_sum_kernel(
    n1, n2, rows_ref, w_ref, dw_ref, g_ref, up_ref,
    kv_out, rk_out, b_out,
    recv_kv, recv_rk, terms, recv_b1, partial, recv_b2, forward, outgoing, across_part, rk_ref, sems, kv_sems,
):
    me1 = lax.axis_index("tensor")
    me2 = lax.axis_index("dp")
    trial = lax.axis_index("trial")
    first = lambda j: (trial, me2, j)
    second = lambda j: (trial, j, me1)
    quarter = n2 // 2
    barrier = pltpu.get_barrier_semaphore()
    for shift in range(1, n1):
        pl.semaphore_signal(barrier, inc=1, device_id=first(lax.rem(me1 + shift, n1)), device_id_type=MESH)
    for shift in range(1, n2):
        pl.semaphore_signal(barrier, inc=1, device_id=second(lax.rem(me2 + shift, n2)), device_id_type=MESH)
    rk_ref[...] = jnp.dot(rows_ref[...], dw_ref[...], preferred_element_type=jnp.float32).reshape(rk_ref.shape)
    pl.semaphore_wait(barrier, n1 + n2 - 2)

    def send(src_ref, dst_ref, row, shift, device):
        copy = pltpu.make_async_remote_copy(
            src_ref=src_ref,
            dst_ref=dst_ref.at[shift],
            send_sem=sems.at[row, shift],
            recv_sem=sems.at[row + 1, shift],
            device_id=device,
            device_id_type=MESH,
        )
        copy.start()
        return copy

    partner = me1 + 1 - 2 * lax.rem(me1, 2)
    across = lax.rem(me1 + 2, n1)
    diagonal = across + 1 - 2 * lax.rem(across, 2)
    rk_copies = []
    for shift in range(1, n1):
        target = lax.rem(me1 + shift, n1)
        rk_copies.append(send(rk_ref.at[target], recv_rk, 2, shift, first(target)))
    pieces = kv_sems.shape[2]
    step = kv_out.shape[0] // pieces

    def send_piece(src_ref, slot, piece, device):
        rows = pl.ds(piece * step, step)
        copy = pltpu.make_async_remote_copy(
            src_ref=src_ref.at[rows],
            dst_ref=recv_kv.at[slot, rows],
            send_sem=kv_sems.at[0, slot, piece],
            recv_sem=kv_sems.at[1, slot, piece],
            device_id=device,
            device_id_type=MESH,
        )
        copy.start()
        return copy

    tokens = kv_out.shape[0]

    def product(member):
        block = rows_ref[pl.ds(pl.multiple_of(member * tokens, tokens), tokens), :]
        return jnp.dot(block, w_ref[...], preferred_element_type=jnp.float32)

    outgoing[1] = product(diagonal).astype(outgoing.dtype)
    diagonal_copies = [send_piece(outgoing.at[1], 1, p, first(partner)) for p in range(pieces)]
    outgoing[0] = product(partner).astype(outgoing.dtype)
    own_copies = [send_piece(outgoing.at[0], 0, p, first(partner)) for p in range(pieces)]
    across_part[...] = product(across)
    own_part = product(me1)

    rk_out[...] = rk_ref[me1]
    for shift, copy in zip(range(1, n1), rk_copies):
        copy.wait_recv()
        rk_out[...] += recv_rk[shift]

    xa = rk_out[...]
    lane = lax.broadcasted_iota(jnp.int32, xa.shape, 1)
    half = xa.shape[1] // 2
    total = None
    for which, keep in enumerate((lane < half, lane >= half)):
        part = jnp.where(keep, xa, 0.0)
        high = part.astype(jnp.bfloat16)
        low = (part - high.astype(jnp.float32)).astype(jnp.bfloat16)
        g = g_ref[which]
        for piece in (high, low):
            term = jnp.dot(g, piece, preferred_element_type=jnp.float32)
            total = term if total is None else total + term
    terms[...] = total.reshape(terms.shape)

    b1_copies = []
    for shift in range(1, n1):
        target = lax.rem(me1 + shift, n1)
        b1_copies.append(send(terms.at[target], recv_b1, 4, shift, first(target)))

    forward_copies = []
    for p, copy in enumerate(diagonal_copies):
        rows = pl.ds(p * step, step)
        copy.wait_recv()
        forward[rows, :] = (
            across_part[rows, :] + recv_kv[1, rows, :].astype(jnp.float32)
        ).astype(forward.dtype)
        forward_copies.append(send_piece(forward, 2, p, first(across)))
    xa_high = xa.astype(jnp.bfloat16)
    xa_low = (xa - xa_high.astype(jnp.float32)).astype(jnp.bfloat16)
    up = up_ref[...]
    adapter = jnp.dot(xa_high, up, preferred_element_type=jnp.float32) + jnp.dot(
        xa_low, up, preferred_element_type=jnp.float32
    )
    kv_out[...] = own_part + adapter_scale * adapter
    for p, copy in enumerate(own_copies):
        rows = pl.ds(p * step, step)
        copy.wait_recv()
        kv_out[rows, :] += recv_kv[0, rows, :].astype(jnp.float32)

    summed = terms[me1]
    for shift, copy in zip(range(1, n1), b1_copies):
        copy.wait_recv()
        summed = summed + recv_b1[shift]
    partial[...] = summed.reshape(partial.shape)

    b2_copies = []
    for shift in range(1, n2):
        target = lax.rem(me2 + shift, n2)
        b2_copies.append(send(partial.at[lax.rem(target, quarter)], recv_b2, 6, shift, second(target)))
    for p, copy in enumerate(forward_copies):
        rows = pl.ds(p * step, step)
        copy.wait_recv()
        kv_out[rows, :] += recv_kv[2, rows, :].astype(jnp.float32)
    reduced = partial[lax.rem(me2, quarter)]
    for shift, copy in zip(range(1, n2), b2_copies):
        copy.wait_recv()
        reduced = reduced + recv_b2[shift]
    by_rank = reduced.T
    ranks_here = b_out.shape[0]
    b_out[...] = adapter_scale * jnp.where(
        me2 < quarter, by_rank[:ranks_here, :], by_rank[ranks_here:, :]
    )

    for copy in rk_copies + diagonal_copies + own_copies + forward_copies + b1_copies + b2_copies:
        copy.wait_send()


def tensor_sum(rows, w, dw, g, up, n1, n2, collective_id):
    tokens = rows.shape[0] // n1
    kv_width = w.shape[1]
    quarter = n2 // 2
    columns = g.shape[1]
    lanes = dw.shape[1]
    block = columns // (n1 * quarter)
    vmem = pl.BlockSpec(memory_space=pltpu.VMEM)
    return pl.pallas_call(
        functools.partial(_tensor_sum_kernel, n1, n2),
        out_shape=(
            jax.ShapeDtypeStruct((tokens, kv_width), jnp.float32),
            jax.ShapeDtypeStruct((tokens, lanes), jnp.float32),
            jax.ShapeDtypeStruct((lanes // 2, block), jnp.float32),
        ),
        in_specs=[vmem] * 5,
        out_specs=(vmem, vmem, vmem),
        scratch_shapes=[
            pltpu.VMEM((n1, tokens, kv_width), jnp.bfloat16),
            pltpu.VMEM((n1, tokens, lanes), jnp.float32),
            pltpu.VMEM((n1, quarter * block, lanes), jnp.float32),
            pltpu.VMEM((n1, quarter * block, lanes), jnp.float32),
            pltpu.VMEM((quarter, block, lanes), jnp.float32),
            pltpu.VMEM((n2, block, lanes), jnp.float32),
            pltpu.VMEM((tokens, kv_width), jnp.bfloat16),
            pltpu.VMEM((2, tokens, kv_width), jnp.bfloat16),
            pltpu.VMEM((tokens, kv_width), jnp.float32),
            pltpu.VMEM((n1, tokens, lanes), jnp.float32),
            pltpu.SemaphoreType.DMA((8, max(n1, n2))),
            pltpu.SemaphoreType.DMA((2, 3, 4)),
        ],
        compiler_params=pltpu.CompilerParams(collective_id=collective_id, has_side_effects=True),
    )(rows, w, dw, g, up)


def shards(
    residual_rows,
    input_norm_weight,
    trial_row_index,
    keyvalue_weight,
    adapter_down_weight,
    adapter_up_weight,
    keyvalue_gradient,
):
    trials = lax.axis_size("trial")
    tensors = lax.axis_size("tensor")
    dps = lax.axis_size("dp")
    tok_dev = trial_row_index.shape[1]
    select = tok_dev // (trials * tensors)
    normed_input = keyvalue_weight.shape[0]
    kv_width = keyvalue_weight.shape[1]
    keyvalue_half = kv_width // 2
    rank_index = adapter_up_weight.shape[1]
    pool_dev = residual_rows.shape[0]
    highest_precision = lax.Precision.HIGHEST

    source = lax.axis_index("trial") * tensors + lax.axis_index("tensor")
    picks = lax.dynamic_slice_in_dim(trial_row_index, source * select, select, 1).reshape(-1)
    onehot = (picks[:, None] == jnp.arange(pool_dev, dtype=jnp.int32)[None, :]).astype(jnp.bfloat16)
    wide = jnp.einsum(
        "tsr,rkf->tksf",
        onehot.reshape(trials, select, pool_dev),
        residual_rows.reshape(pool_dev, tensors, normed_input),
        preferred_element_type=jnp.float32,
    )
    raw = residual_rows.astype(jnp.float32)
    row_scale = lax.rsqrt(jnp.mean(raw * raw, axis=1) + norm_eps)
    picked_scale = jnp.take(row_scale, picks, axis=0)
    gain = input_norm_weight.reshape(1, tensors, 1, normed_input)
    chosen = (wide * picked_scale.reshape(trials, 1, select, 1) * gain).astype(jnp.bfloat16)
    arrived = lax.all_to_all(
        chosen.reshape(trials * tensors, select, normed_input),
        ("trial", "tensor"),
        split_axis=0,
        concat_axis=0,
        tiled=True,
    )
    rows = arrived.reshape(tok_dev, normed_input)

    up_weight = adapter_up_weight[0].astype(jnp.float32)
    grad_in = keyvalue_gradient[0].astype(jnp.float32)
    key_gradient_full = jnp.dot(
        grad_in[:, :keyvalue_half], up_weight[:, :keyvalue_half].T, precision=highest_precision
    )
    value_gradient_full = jnp.dot(
        grad_in[:, keyvalue_half:], up_weight[:, keyvalue_half:].T, precision=highest_precision
    )
    rank_gradient = (
        adapter_scale * jnp.concatenate([key_gradient_full, value_gradient_full], axis=1)
    ).astype(jnp.bfloat16)
    quarter = dps // 2
    width = kv_width // (dps * tensors)
    grad_t = keyvalue_gradient[0].T.reshape(2, quarter, tensors, width, tok_dev // tensors)
    grad_t = grad_t.transpose(0, 2, 1, 3, 4).reshape(2, keyvalue_half, tok_dev // tensors)
    grad_t, rank_gradient = lax.optimization_barrier((grad_t, rank_gradient))
    every_rank = lax.all_gather(rank_gradient, "tensor", axis=0, tiled=True)
    grad_a_term = lax.dot_general(
        every_rank, rows, (((0,), (0,)), ((), ())), preferred_element_type=jnp.float32
    )

    up_bf = adapter_up_weight[0]
    block_up = jnp.zeros((2 * rank_index, kv_width), up_bf.dtype)
    block_up = block_up.at[:rank_index, :keyvalue_half].set(up_bf[:, :keyvalue_half])
    block_up = block_up.at[rank_index:, keyvalue_half:].set(up_bf[:, keyvalue_half:])
    frozen_output_local, local_rank_rows, up_block = tensor_sum(
        rows,
        keyvalue_weight,
        adapter_down_weight[0],
        grad_t,
        block_up,
        tensors,
        dps,
        0,
    )
    keyvalue_output = frozen_output_local

    grad_a = lax.psum_scatter(grad_a_term, "dp", scatter_dimension=0, tiled=True)

    grad_b = up_block
    return (keyvalue_output[None], grad_a[None], grad_b[None])


def solution(mesh):
    return jax.shard_map(
        shards,
        mesh=mesh,
        in_specs=(
            P(("trial", "dp", "tensor"), None),
            P(),
            P(None, "dp"),
            P("tensor", None),
            P("trial", "tensor", None),
            P("trial", None, None),
            P("trial", ("dp", "tensor"), None),
        ),
        out_specs=(
            P("trial", ("dp", "tensor"), None),
            P("trial", "dp", "tensor"),
            P("trial", None, ("dp", "tensor")),
        ),
        check_vma=False,
    )
```

```python
import functools

import jax
import jax.numpy as jnp
from jax import lax
from jax.experimental import pallas as pl
from jax.experimental.pallas import tpu as pltpu
from jax.sharding import PartitionSpec as P

MESH = pl.DeviceIdType.MESH

adapter_scale = 2.0
norm_eps = 1e-05


def _tensor_sum_kernel(
    n1, n2, rows_ref, w_ref, dw_ref, g_ref,
    kv_out, rk_out, b_out,
    recv_kv, recv_rk, terms, recv_b1, partial, recv_b2, forward, outgoing, across_part, rk_ref, sems, kv_sems,
):
    me1 = lax.axis_index("tensor")
    me2 = lax.axis_index("dp")
    trial = lax.axis_index("trial")
    first = lambda j: (trial, me2, j)
    second = lambda j: (trial, j, me1)
    quarter = n2 // 2
    barrier = pltpu.get_barrier_semaphore()
    for shift in range(1, n1):
        pl.semaphore_signal(barrier, inc=1, device_id=first(lax.rem(me1 + shift, n1)), device_id_type=MESH)
    for shift in range(1, n2):
        pl.semaphore_signal(barrier, inc=1, device_id=second(lax.rem(me2 + shift, n2)), device_id_type=MESH)
    rk_ref[...] = jnp.dot(rows_ref[...], dw_ref[...], preferred_element_type=jnp.float32).reshape(rk_ref.shape)
    pl.semaphore_wait(barrier, n1 + n2 - 2)

    def send(src_ref, dst_ref, row, shift, device):
        copy = pltpu.make_async_remote_copy(
            src_ref=src_ref,
            dst_ref=dst_ref.at[shift],
            send_sem=sems.at[row, shift],
            recv_sem=sems.at[row + 1, shift],
            device_id=device,
            device_id_type=MESH,
        )
        copy.start()
        return copy

    partner = me1 + 1 - 2 * lax.rem(me1, 2)
    across = lax.rem(me1 + 2, n1)
    diagonal = across + 1 - 2 * lax.rem(across, 2)
    rk_copies = []
    for shift in range(1, n1):
        target = lax.rem(me1 + shift, n1)
        rk_copies.append(send(rk_ref.at[target], recv_rk, 2, shift, first(target)))
    pieces = kv_sems.shape[2]
    step = kv_out.shape[0] // pieces

    def send_piece(src_ref, slot, piece, device):
        rows = pl.ds(piece * step, step)
        copy = pltpu.make_async_remote_copy(
            src_ref=src_ref.at[rows],
            dst_ref=recv_kv.at[slot, rows],
            send_sem=kv_sems.at[0, slot, piece],
            recv_sem=kv_sems.at[1, slot, piece],
            device_id=device,
            device_id_type=MESH,
        )
        copy.start()
        return copy

    tokens = kv_out.shape[0]

    def product(member):
        block = rows_ref[pl.ds(pl.multiple_of(member * tokens, tokens), tokens), :]
        return jnp.dot(block, w_ref[...], preferred_element_type=jnp.float32)

    outgoing[1] = product(diagonal).astype(outgoing.dtype)
    diagonal_copies = [send_piece(outgoing.at[1], 1, p, first(partner)) for p in range(pieces)]
    outgoing[0] = product(partner).astype(outgoing.dtype)
    own_copies = [send_piece(outgoing.at[0], 0, p, first(partner)) for p in range(pieces)]
    across_part[...] = product(across)
    own_part = product(me1)

    rk_out[...] = rk_ref[me1]
    for shift, copy in zip(range(1, n1), rk_copies):
        copy.wait_recv()
        rk_out[...] += recv_rk[shift]

    xa = rk_out[...]
    lane = lax.broadcasted_iota(jnp.int32, xa.shape, 1)
    half = xa.shape[1] // 2
    total = None
    for which, keep in enumerate((lane < half, lane >= half)):
        part = jnp.where(keep, xa, 0.0)
        high = part.astype(jnp.bfloat16)
        low = (part - high.astype(jnp.float32)).astype(jnp.bfloat16)
        g = g_ref[which]
        for piece in (high, low):
            term = jnp.dot(g, piece, preferred_element_type=jnp.float32)
            total = term if total is None else total + term
    terms[...] = total.reshape(terms.shape)

    b1_copies = []
    for shift in range(1, n1):
        target = lax.rem(me1 + shift, n1)
        b1_copies.append(send(terms.at[target], recv_b1, 4, shift, first(target)))

    forward_copies = []
    for p, copy in enumerate(diagonal_copies):
        rows = pl.ds(p * step, step)
        copy.wait_recv()
        forward[rows, :] = (
            across_part[rows, :] + recv_kv[1, rows, :].astype(jnp.float32)
        ).astype(forward.dtype)
        forward_copies.append(send_piece(forward, 2, p, first(across)))
    kv_out[...] = own_part
    for p, copy in enumerate(own_copies):
        rows = pl.ds(p * step, step)
        copy.wait_recv()
        kv_out[rows, :] += recv_kv[0, rows, :].astype(jnp.float32)

    summed = terms[me1]
    for shift, copy in zip(range(1, n1), b1_copies):
        copy.wait_recv()
        summed = summed + recv_b1[shift]
    partial[...] = summed.reshape(partial.shape)

    b2_copies = []
    for shift in range(1, n2):
        target = lax.rem(me2 + shift, n2)
        b2_copies.append(send(partial.at[lax.rem(target, quarter)], recv_b2, 6, shift, second(target)))
    for p, copy in enumerate(forward_copies):
        rows = pl.ds(p * step, step)
        copy.wait_recv()
        kv_out[rows, :] += recv_kv[2, rows, :].astype(jnp.float32)
    reduced = partial[lax.rem(me2, quarter)]
    for shift, copy in zip(range(1, n2), b2_copies):
        copy.wait_recv()
        reduced = reduced + recv_b2[shift]
    by_rank = reduced.T
    ranks_here = b_out.shape[0]
    b_out[...] = adapter_scale * jnp.where(
        me2 < quarter, by_rank[:ranks_here, :], by_rank[ranks_here:, :]
    )

    for copy in rk_copies + diagonal_copies + own_copies + forward_copies + b1_copies + b2_copies:
        copy.wait_send()


def tensor_sum(rows, w, dw, g, n1, n2, collective_id):
    tokens = rows.shape[0] // n1
    kv_width = w.shape[1]
    quarter = n2 // 2
    columns = g.shape[1]
    lanes = dw.shape[1]
    block = columns // (n1 * quarter)
    vmem = pl.BlockSpec(memory_space=pltpu.VMEM)
    return pl.pallas_call(
        functools.partial(_tensor_sum_kernel, n1, n2),
        out_shape=(
            jax.ShapeDtypeStruct((tokens, kv_width), jnp.float32),
            jax.ShapeDtypeStruct((tokens, lanes), jnp.float32),
            jax.ShapeDtypeStruct((lanes // 2, block), jnp.float32),
        ),
        in_specs=[vmem] * 4,
        out_specs=(vmem, vmem, vmem),
        scratch_shapes=[
            pltpu.VMEM((n1, tokens, kv_width), jnp.bfloat16),
            pltpu.VMEM((n1, tokens, lanes), jnp.float32),
            pltpu.VMEM((n1, quarter * block, lanes), jnp.float32),
            pltpu.VMEM((n1, quarter * block, lanes), jnp.float32),
            pltpu.VMEM((quarter, block, lanes), jnp.float32),
            pltpu.VMEM((n2, block, lanes), jnp.float32),
            pltpu.VMEM((tokens, kv_width), jnp.bfloat16),
            pltpu.VMEM((2, tokens, kv_width), jnp.bfloat16),
            pltpu.VMEM((tokens, kv_width), jnp.float32),
            pltpu.VMEM((n1, tokens, lanes), jnp.float32),
            pltpu.SemaphoreType.DMA((8, max(n1, n2))),
            pltpu.SemaphoreType.DMA((2, 3, 4)),
        ],
        compiler_params=pltpu.CompilerParams(collective_id=collective_id, has_side_effects=True),
    )(rows, w, dw, g)


def shards(
    residual_rows,
    input_norm_weight,
    trial_row_index,
    keyvalue_weight,
    adapter_down_weight,
    adapter_up_weight,
    keyvalue_gradient,
):
    trials = lax.axis_size("trial")
    tensors = lax.axis_size("tensor")
    dps = lax.axis_size("dp")
    tok_dev = trial_row_index.shape[1]
    select = tok_dev // (trials * tensors)
    normed_input = keyvalue_weight.shape[0]
    kv_width = keyvalue_weight.shape[1]
    keyvalue_half = kv_width // 2
    rank_index = adapter_up_weight.shape[1]
    pool_dev = residual_rows.shape[0]
    highest_precision = lax.Precision.HIGHEST

    source = lax.axis_index("trial") * tensors + lax.axis_index("tensor")
    picks = lax.dynamic_slice_in_dim(trial_row_index, source * select, select, 1).reshape(-1)
    onehot = (picks[:, None] == jnp.arange(pool_dev, dtype=jnp.int32)[None, :]).astype(jnp.bfloat16)
    wide = jnp.einsum(
        "tsr,rkf->tksf",
        onehot.reshape(trials, select, pool_dev),
        residual_rows.reshape(pool_dev, tensors, normed_input),
        preferred_element_type=jnp.float32,
    )
    raw = residual_rows.astype(jnp.float32)
    row_scale = lax.rsqrt(jnp.mean(raw * raw, axis=1) + norm_eps)
    picked_scale = jnp.sum(
        jnp.where(picks[:, None] == jnp.arange(pool_dev, dtype=jnp.int32)[None, :], row_scale[None, :], 0.0),
        axis=1,
    )
    gain = input_norm_weight.reshape(1, tensors, 1, normed_input)
    chosen = (wide * picked_scale.reshape(trials, 1, select, 1) * gain).astype(jnp.bfloat16)
    arrived = lax.all_to_all(
        chosen.reshape(trials * tensors, select, normed_input),
        ("trial", "tensor"),
        split_axis=0,
        concat_axis=0,
        tiled=True,
    )
    rows = arrived.reshape(tok_dev, normed_input)

    up_weight = adapter_up_weight[0].astype(jnp.float32)
    grad_in = keyvalue_gradient[0].astype(jnp.float32)
    key_gradient_full = jnp.dot(
        grad_in[:, :keyvalue_half], up_weight[:, :keyvalue_half].T, precision=highest_precision
    )
    value_gradient_full = jnp.dot(
        grad_in[:, keyvalue_half:], up_weight[:, keyvalue_half:].T, precision=highest_precision
    )
    rank_gradient = (
        adapter_scale * jnp.concatenate([key_gradient_full, value_gradient_full], axis=1)
    ).astype(jnp.bfloat16)
    quarter = dps // 2
    width = kv_width // (dps * tensors)
    grad_t = keyvalue_gradient[0].T.reshape(2, quarter, tensors, width, tok_dev // tensors)
    grad_t = grad_t.transpose(0, 2, 1, 3, 4).reshape(2, keyvalue_half, tok_dev // tensors)
    grad_t, rank_gradient = lax.optimization_barrier((grad_t, rank_gradient))
    every_rank = lax.all_gather(rank_gradient, "tensor", axis=0, tiled=True)
    grad_a_term = lax.dot_general(
        every_rank, rows, (((0,), (0,)), ((), ())), preferred_element_type=jnp.float32
    )

    frozen_output_local, local_rank_rows, up_block = tensor_sum(
        rows,
        keyvalue_weight,
        adapter_down_weight[0],
        grad_t,
        tensors,
        dps,
        0,
    )
    adapter_key = jnp.dot(
        local_rank_rows[:, :rank_index], up_weight[:, :keyvalue_half], precision=highest_precision
    )
    adapter_value = jnp.dot(
        local_rank_rows[:, rank_index:], up_weight[:, keyvalue_half:], precision=highest_precision
    )
    keyvalue_output = frozen_output_local + adapter_scale * jnp.concatenate(
        [adapter_key, adapter_value], axis=1
    )

    grad_a = lax.psum_scatter(grad_a_term, "dp", scatter_dimension=0, tiled=True)

    grad_b = up_block
    return (keyvalue_output[None], grad_a[None], grad_b[None])


def solution(mesh):
    return jax.shard_map(
        shards,
        mesh=mesh,
        in_specs=(
            P(("trial", "dp", "tensor"), None),
            P(),
            P(None, "dp"),
            P("tensor", None),
            P("trial", "tensor", None),
            P("trial", None, None),
            P("trial", ("dp", "tensor"), None),
        ),
        out_specs=(
            P("trial", ("dp", "tensor"), None),
            P("trial", "dp", "tensor"),
            P("trial", None, ("dp", "tensor")),
        ),
        check_vma=False,
    )
```

```python
import functools

import jax
import jax.numpy as jnp
from jax import lax
from jax.experimental import pallas as pl
from jax.experimental.pallas import tpu as pltpu
from jax.sharding import PartitionSpec as P

MESH = pl.DeviceIdType.MESH

adapter_scale = 2.0
norm_eps = 1e-05


def _tensor_sum_kernel(
    n1, n2, rows_ref, w_ref, dw_ref, g_ref,
    kv_out, rk_out, b_out,
    recv_kv, recv_rk, terms, recv_b1, partial, recv_b2, forward, outgoing, across_part, rk_ref, sems, kv_sems,
):
    me1 = lax.axis_index("tensor")
    me2 = lax.axis_index("dp")
    trial = lax.axis_index("trial")
    first = lambda j: (trial, me2, j)
    second = lambda j: (trial, j, me1)
    quarter = n2 // 2
    barrier = pltpu.get_barrier_semaphore()
    for shift in range(1, n1):
        pl.semaphore_signal(barrier, inc=1, device_id=first(lax.rem(me1 + shift, n1)), device_id_type=MESH)
    for shift in range(1, n2):
        pl.semaphore_signal(barrier, inc=1, device_id=second(lax.rem(me2 + shift, n2)), device_id_type=MESH)
    rk_ref[...] = jnp.dot(rows_ref[...], dw_ref[...], preferred_element_type=jnp.float32).reshape(rk_ref.shape)
    pl.semaphore_wait(barrier, n1 + n2 - 2)

    def send(src_ref, dst_ref, row, shift, device):
        copy = pltpu.make_async_remote_copy(
            src_ref=src_ref,
            dst_ref=dst_ref.at[shift],
            send_sem=sems.at[row, shift],
            recv_sem=sems.at[row + 1, shift],
            device_id=device,
            device_id_type=MESH,
        )
        copy.start()
        return copy

    partner = me1 + 1 - 2 * lax.rem(me1, 2)
    across = lax.rem(me1 + 2, n1)
    diagonal = across + 1 - 2 * lax.rem(across, 2)
    rk_copies = []
    for shift in range(1, n1):
        target = lax.rem(me1 + shift, n1)
        rk_copies.append(send(rk_ref.at[target], recv_rk, 2, shift, first(target)))
    pieces = kv_sems.shape[2]
    step = kv_out.shape[0] // pieces

    def send_piece(src_ref, slot, piece, device):
        rows = pl.ds(piece * step, step)
        copy = pltpu.make_async_remote_copy(
            src_ref=src_ref.at[rows],
            dst_ref=recv_kv.at[slot, rows],
            send_sem=kv_sems.at[0, slot, piece],
            recv_sem=kv_sems.at[1, slot, piece],
            device_id=device,
            device_id_type=MESH,
        )
        copy.start()
        return copy

    tokens = kv_out.shape[0]

    def product(member):
        block = rows_ref[pl.ds(pl.multiple_of(member * tokens, tokens), tokens), :]
        return jnp.dot(block, w_ref[...], preferred_element_type=jnp.float32)

    outgoing[1] = product(diagonal).astype(outgoing.dtype)
    diagonal_copies = [send_piece(outgoing.at[1], 1, p, first(partner)) for p in range(pieces)]
    outgoing[0] = product(partner).astype(outgoing.dtype)
    own_copies = [send_piece(outgoing.at[0], 0, p, first(partner)) for p in range(pieces)]
    across_part[...] = product(across)
    own_part = product(me1)

    rk_out[...] = rk_ref[me1]
    for shift, copy in zip(range(1, n1), rk_copies):
        copy.wait_recv()
        rk_out[...] += recv_rk[shift]

    xa = rk_out[...]
    lane = lax.broadcasted_iota(jnp.int32, xa.shape, 1)
    half = xa.shape[1] // 2
    total = None
    for which, keep in enumerate((lane < half, lane >= half)):
        part = jnp.where(keep, xa, 0.0)
        high = part.astype(jnp.bfloat16)
        low = (part - high.astype(jnp.float32)).astype(jnp.bfloat16)
        g = g_ref[which]
        for piece in (high, low):
            term = jnp.dot(g, piece, preferred_element_type=jnp.float32)
            total = term if total is None else total + term
    terms[...] = total.reshape(terms.shape)

    b1_copies = []
    for shift in range(1, n1):
        target = lax.rem(me1 + shift, n1)
        b1_copies.append(send(terms.at[target], recv_b1, 4, shift, first(target)))

    forward_copies = []
    for p, copy in enumerate(diagonal_copies):
        rows = pl.ds(p * step, step)
        copy.wait_recv()
        forward[rows, :] = (
            across_part[rows, :] + recv_kv[1, rows, :].astype(jnp.float32)
        ).astype(forward.dtype)
        forward_copies.append(send_piece(forward, 2, p, first(across)))
    kv_out[...] = own_part
    for p, copy in enumerate(own_copies):
        rows = pl.ds(p * step, step)
        copy.wait_recv()
        kv_out[rows, :] += recv_kv[0, rows, :].astype(jnp.float32)

    summed = terms[me1]
    for shift, copy in zip(range(1, n1), b1_copies):
        copy.wait_recv()
        summed = summed + recv_b1[shift]
    partial[...] = summed.reshape(partial.shape)

    b2_copies = []
    for shift in range(1, n2):
        target = lax.rem(me2 + shift, n2)
        b2_copies.append(send(partial.at[lax.rem(target, quarter)], recv_b2, 6, shift, second(target)))
    for p, copy in enumerate(forward_copies):
        rows = pl.ds(p * step, step)
        copy.wait_recv()
        kv_out[rows, :] += recv_kv[2, rows, :].astype(jnp.float32)
    reduced = partial[lax.rem(me2, quarter)]
    for shift, copy in zip(range(1, n2), b2_copies):
        copy.wait_recv()
        reduced = reduced + recv_b2[shift]
    by_rank = reduced.T
    ranks_here = b_out.shape[0]
    b_out[...] = adapter_scale * jnp.where(
        me2 < quarter, by_rank[:ranks_here, :], by_rank[ranks_here:, :]
    )

    for copy in rk_copies + diagonal_copies + own_copies + forward_copies + b1_copies + b2_copies:
        copy.wait_send()


def tensor_sum(rows, w, dw, g, n1, n2, collective_id):
    tokens = rows.shape[0] // n1
    kv_width = w.shape[1]
    quarter = n2 // 2
    columns = g.shape[1]
    lanes = dw.shape[1]
    block = columns // (n1 * quarter)
    vmem = pl.BlockSpec(memory_space=pltpu.VMEM)
    return pl.pallas_call(
        functools.partial(_tensor_sum_kernel, n1, n2),
        out_shape=(
            jax.ShapeDtypeStruct((tokens, kv_width), jnp.float32),
            jax.ShapeDtypeStruct((tokens, lanes), jnp.float32),
            jax.ShapeDtypeStruct((lanes // 2, block), jnp.float32),
        ),
        in_specs=[vmem] * 4,
        out_specs=(vmem, vmem, vmem),
        scratch_shapes=[
            pltpu.VMEM((n1, tokens, kv_width), jnp.bfloat16),
            pltpu.VMEM((n1, tokens, lanes), jnp.float32),
            pltpu.VMEM((n1, quarter * block, lanes), jnp.float32),
            pltpu.VMEM((n1, quarter * block, lanes), jnp.float32),
            pltpu.VMEM((quarter, block, lanes), jnp.float32),
            pltpu.VMEM((n2, block, lanes), jnp.float32),
            pltpu.VMEM((tokens, kv_width), jnp.bfloat16),
            pltpu.VMEM((2, tokens, kv_width), jnp.bfloat16),
            pltpu.VMEM((tokens, kv_width), jnp.float32),
            pltpu.VMEM((n1, tokens, lanes), jnp.float32),
            pltpu.SemaphoreType.DMA((8, max(n1, n2))),
            pltpu.SemaphoreType.DMA((2, 3, 4)),
        ],
        compiler_params=pltpu.CompilerParams(collective_id=collective_id, has_side_effects=True),
    )(rows, w, dw, g)


def shards(
    residual_rows,
    input_norm_weight,
    trial_row_index,
    keyvalue_weight,
    adapter_down_weight,
    adapter_up_weight,
    keyvalue_gradient,
):
    trials = lax.axis_size("trial")
    tensors = lax.axis_size("tensor")
    dps = lax.axis_size("dp")
    tok_dev = trial_row_index.shape[1]
    select = tok_dev // (trials * tensors)
    normed_input = keyvalue_weight.shape[0]
    kv_width = keyvalue_weight.shape[1]
    keyvalue_half = kv_width // 2
    rank_index = adapter_up_weight.shape[1]
    pool_dev = residual_rows.shape[0]
    highest_precision = lax.Precision.HIGHEST

    source = lax.axis_index("trial") * tensors + lax.axis_index("tensor")
    picks = lax.dynamic_slice_in_dim(trial_row_index, source * select, select, 1).reshape(-1)
    onehot = (picks[:, None] == jnp.arange(pool_dev, dtype=jnp.int32)[None, :]).astype(jnp.bfloat16)
    wide = jnp.einsum(
        "tsr,rkf->tksf",
        onehot.reshape(trials, select, pool_dev),
        residual_rows.reshape(pool_dev, tensors, normed_input),
        preferred_element_type=jnp.float32,
    )
    raw = residual_rows.astype(jnp.float32)
    lane_groups = lax.optimization_barrier((raw * raw).reshape(pool_dev, -1, 128).sum(axis=1))
    row_scale = lax.rsqrt(lane_groups.sum(axis=1) / raw.shape[1] + norm_eps)
    picked_scale = jnp.sum(
        jnp.where(picks[:, None] == jnp.arange(pool_dev, dtype=jnp.int32)[None, :], row_scale[None, :], 0.0),
        axis=1,
    )
    gain = input_norm_weight.reshape(1, tensors, 1, normed_input)
    chosen = (wide * picked_scale.reshape(trials, 1, select, 1) * gain).astype(jnp.bfloat16)
    arrived = lax.all_to_all(
        chosen.reshape(trials * tensors, select, normed_input),
        ("trial", "tensor"),
        split_axis=0,
        concat_axis=0,
        tiled=True,
    )
    rows = arrived.reshape(tok_dev, normed_input)

    up_weight = adapter_up_weight[0].astype(jnp.float32)
    grad_in = keyvalue_gradient[0].astype(jnp.float32)
    key_gradient_full = jnp.dot(
        grad_in[:, :keyvalue_half], up_weight[:, :keyvalue_half].T, precision=highest_precision
    )
    value_gradient_full = jnp.dot(
        grad_in[:, keyvalue_half:], up_weight[:, keyvalue_half:].T, precision=highest_precision
    )
    rank_gradient = (
        adapter_scale * jnp.concatenate([key_gradient_full, value_gradient_full], axis=1)
    ).astype(jnp.bfloat16)
    quarter = dps // 2
    width = kv_width // (dps * tensors)
    grad_t = keyvalue_gradient[0].T.reshape(2, quarter, tensors, width, tok_dev // tensors)
    grad_t = grad_t.transpose(0, 2, 1, 3, 4).reshape(2, keyvalue_half, tok_dev // tensors)
    grad_t, rank_gradient = lax.optimization_barrier((grad_t, rank_gradient))
    every_rank = lax.all_gather(rank_gradient, "tensor", axis=0, tiled=True)
    grad_a_term = lax.dot_general(
        every_rank, rows, (((0,), (0,)), ((), ())), preferred_element_type=jnp.float32
    )

    frozen_output_local, local_rank_rows, up_block = tensor_sum(
        rows,
        keyvalue_weight,
        adapter_down_weight[0],
        grad_t,
        tensors,
        dps,
        0,
    )
    adapter_key = jnp.dot(
        local_rank_rows[:, :rank_index], up_weight[:, :keyvalue_half], precision=highest_precision
    )
    adapter_value = jnp.dot(
        local_rank_rows[:, rank_index:], up_weight[:, keyvalue_half:], precision=highest_precision
    )
    keyvalue_output = frozen_output_local + adapter_scale * jnp.concatenate(
        [adapter_key, adapter_value], axis=1
    )

    grad_a = lax.psum_scatter(grad_a_term, "dp", scatter_dimension=0, tiled=True)

    grad_b = up_block
    return (keyvalue_output[None], grad_a[None], grad_b[None])


def solution(mesh):
    return jax.shard_map(
        shards,
        mesh=mesh,
        in_specs=(
            P(("trial", "dp", "tensor"), None),
            P(),
            P(None, "dp"),
            P("tensor", None),
            P("trial", "tensor", None),
            P("trial", None, None),
            P("trial", ("dp", "tensor"), None),
        ),
        out_specs=(
            P("trial", ("dp", "tensor"), None),
            P("trial", "dp", "tensor"),
            P("trial", None, ("dp", "tensor")),
        ),
        check_vma=False,
    )
```
